32 devices in a mesh: dp: 4 (over y, core), tensor: 8 (over z, x).
Axes of the slice: x: 2, y: 2, z: 4, core: 2. Of those that a mesh axis runs over, the one named last changes fastest.
Arguments:
- inputs: bfloat16 [8192, 1024], P(('dp', 'tensor')), may hold values from -6 to 6
- qkv_weight: bfloat16 [1024, 3072], P(None, 'tensor'), may hold values from -0.1875 to 0.1875
- qkv_bias: bfloat16 [3072], P('tensor'), may hold values from -3 to 3
- dense_weight: bfloat16 [1024, 1024], P('tensor'), may hold values from -1 to 1
- up_weight: bfloat16 [1024, 4096], P(None, 'tensor'), may hold values from -0.1875 to 0.1875
- up_bias: bfloat16 [4096], P('tensor'), may hold values from -3 to 3
- down_weight: bfloat16 [4096, 1024], P('tensor'), may hold values from -0.09375 to 0.09375
- out_bias: bfloat16 [1024], replicated, may hold values from -3 to 3
- gain_one: bfloat16 [1024], replicated, may hold values from 0.099609375 to 1.8984375
- shift_one: bfloat16 [1024], replicated, may hold values from -2 to 2
- gain_two: bfloat16 [1024], replicated, may hold values from 0.099609375 to 1.8984375
- shift_two: bfloat16 [1024], replicated, may hold values from -2 to 2
- feature_omega: float32 [64, 64], replicated, may hold values from -0.75 to 0.75
- doc_ids: int32 [4, 2048], P('dp'), may hold values from 0 to 7, never falling along the last dimension, each value on 1 to 1024 neighbouring positions
- out_grad: bfloat16 [8192, 1024], P(('dp', 'tensor')), may hold values from -6 to 6
Outputs:
- layer_out: bfloat16 [8192, 1024], P(('dp', 'tensor'))
- input_grad: float32 [8192, 1024], P(('dp', 'tensor'))
- qkv_weight_grad: float32 [1024, 3072], P(None, 'tensor')
- qkv_bias_grad: float32 [3072], P('tensor')
- dense_weight_grad: float32 [1024, 1024], P('tensor')
- up_weight_grad: float32 [1024, 4096], P(None, 'tensor')
- up_bias_grad: float32 [4096], P('tensor')
- down_weight_grad: float32 [4096, 1024], P('tensor')
- out_bias_grad: float32 [1024], P('tensor')
- gain_one_grad: float32 [1024], P('tensor')
- shift_one_grad: float32 [1024], P('tensor')
- gain_two_grad: float32 [1024], P('tensor')
- shift_two_grad: float32 [1024], P('tensor')
The draws below stay inside these ranges and needn't reach their ends.
Inputs may be any that keep to these rules, and one draw needn't show every extreme that they name: `doc_ids`: in each packed row the document numbers never fall; a document holds at most 1024 tokens and some document holds exactly that many.
All inputs are finite; a program needn't handle non-finite values.
Results may differ from the reference program's by a relative error of at most 0.0072.
Values may be sent and summed in bfloat16 or wider, within the bound.
No kernel may reach another device: no remote copies, remote signals or barrier semaphores. Data moves between devices by JAX's collectives and lax.ppermute only.
A program may use at most 192 MiB of HBM per device.

```python
import math
import jax
import jax.numpy as jnp
import numpy as np
from jax import lax

HEADS = 16
HEAD_DIM = 64
D = 1024
FF = 4096
ROT = 16
FEAT = 64
LEN = 2048
SEQS = 4
TOKENS = 8192


def level_of(key, shape, cuts, low, high):
    def one(axis_at, blocks):
        heights = jax.random.uniform(jax.random.fold_in(jax.random.fold_in(key, 6), axis_at), (blocks,), jnp.float32, low / len(cuts), high / len(cuts))
        return jnp.repeat(jnp.exp(heights), shape[axis_at] // blocks).reshape((-1,) + (1,) * (len(shape) - axis_at - 1))

    gain = one(*cuts[0])
    for cut in cuts[1:]:
        gain = gain * one(*cut)
    return gain


def split_up(count, total, most, lean):
    portions = [(1 << 20) // math.isqrt(standing ** lean) + 1 for standing in range(2, count + 1)]
    rest, given = total - most - (count - 1), [1] * (count - 1)
    while rest > 0:
        movable = [i for i in range(count - 1) if given[i] < most]
        whole, remaining = sum([portions[i] for i in movable]), rest
        for i in movable:
            more = min(most - given[i], max(1, remaining * portions[i] // whole), rest)
            given[i] = given[i] + more
            rest = rest - more
    return np.array([most] + given)


def ragged_sizes(own_key, amount, total, most, skew):
    if amount == 2:
        one = jax.random.randint(own_key, (), max(1, total - most), min(most, total - 1) + 1)
        return jnp.stack([one, total - one])
    sizes = jnp.asarray(split_up(amount, total, most, skew), jnp.int32)
    pairs = (amount - 1) // 2
    source_of, sink = sizes[1:1 + 2 * pairs:2], sizes[2:2 + 2 * pairs:2]
    slack = jnp.minimum(source_of - 1, most - sink)
    moved = jax.random.randint(jax.random.fold_in(own_key, 1), (pairs,), 0, 1 << 20) % (slack + 1)
    sizes = sizes.at[1:1 + 2 * pairs:2].set(source_of - moved).at[2:2 + 2 * pairs:2].set(sink + moved)
    return sizes[jax.random.permutation(jax.random.fold_in(own_key, 2), amount)]


def gaussian(rng, dims, deviation, limit, split=(), kind=jnp.bfloat16):
    gain = level_of(rng, dims, split, -0.22, 0.18) if split else 1.0
    entries = jax.random.normal(rng, dims, jnp.float32) * deviation * gain
    return jnp.minimum(jnp.maximum(entries, -limit), limit).astype(kind)


def setup_inputs(seed: int = 0) -> dict:
    key_list = jax.random.split(jax.random.key(seed), 16)
    return {
        "inputs": gaussian(key_list[0], (TOKENS, D), 1.0, 6.0, ((0, 32),)),
        "qkv_weight": gaussian(key_list[1], (D, 3 * D), D ** -0.5, 0.1875, ((1, 8),)),
        "qkv_bias": gaussian(key_list[2], (3 * D,), 0.5, 3.0, ((0, 8),)),
        "dense_weight": gaussian(key_list[3], (D, D), (D // 32) ** -0.5, 1.0, ((0, 8),)),
        "up_weight": gaussian(key_list[4], (D, FF), D ** -0.5, 0.1875, ((1, 8),)),
        "up_bias": gaussian(key_list[5], (FF,), 0.5, 3.0, ((0, 8),)),
        "down_weight": gaussian(key_list[6], (FF, D), FF ** -0.5, 0.09375, ((0, 8),)),
        "out_bias": gaussian(key_list[7], (D,), 0.5, 3.0),
        "gain_one": jnp.clip(1.0 + 0.18 * jax.random.normal(key_list[8], (D,), jnp.float32), 0.099609375, 1.8984375).astype(jnp.bfloat16),
        "shift_one": gaussian(key_list[9], (D,), 0.3, 2.0),
        "gain_two": jnp.clip(1.0 + 0.18 * jax.random.normal(key_list[10], (D,), jnp.float32), 0.099609375, 1.8984375).astype(jnp.bfloat16),
        "shift_two": gaussian(key_list[11], (D,), 0.3, 2.0),
        "feature_omega": gaussian(key_list[12], (HEAD_DIM, FEAT), HEAD_DIM ** -0.5, 0.75, (), jnp.float32),
        "doc_ids": jax.vmap(lambda own: jnp.searchsorted(jnp.cumsum(ragged_sizes(own, 8, LEN, LEN // 2, 0)), jnp.arange(LEN), side="right"))(jax.random.split(key_list[13], SEQS)).reshape((SEQS, LEN)).astype(jnp.int32),
        "out_grad": gaussian(key_list[14], (TOKENS, D), 1.0, 6.0, ((0, 32),)),
    }


EPS = 1e-05
EXACT = lax.Precision.HIGHEST

@jax.custom_vjp
def low(v):
    return lax.optimization_barrier(v.astype(jnp.bfloat16)).astype(jnp.float32)

@jax.custom_vjp
def low_back(v):
    return v

def low_keep(v):
    return (low(v), None)

def low_pass(kept, grad):
    return (grad,)

def back_keep(v):
    return (v, None)

def back_low(kept, grad):
    return (low(grad),)
low.defvjp(low_keep, low_pass)
low_back.defvjp(back_keep, back_low)

def layer_norm(values, gain_row, offset):
    row_mean = lax.optimization_barrier(jnp.mean(values, axis=-1, keepdims=True))
    centred = values - row_mean
    spread = lax.optimization_barrier(jnp.mean(centred * centred, axis=-1, keepdims=True))
    return centred * lax.rsqrt(spread + EPS) * gain_row + offset

def dct_matrix(extent):
    indices = jnp.arange(extent, dtype=jnp.float32)
    cosines = jnp.cos(jnp.pi * (indices[:, None] + 0.5) * indices[None, :] / extent)
    scales = jnp.where(indices == 0, jnp.sqrt(1.0 / extent), jnp.sqrt(2.0 / extent))
    return cosines * scales[None, :]

def rotary_tables(positions, turned):
    half_rot = turned // 2
    frequencies = 10000.0 ** (-(jnp.arange(half_rot, dtype=jnp.float32) * 2.0 / turned))
    angles = positions.astype(jnp.float32)[:, None] * frequencies[None, :]
    return (jnp.cos(angles), jnp.sin(angles))

def rotate(values, cosine_table, sine_table):
    half_rot = cosine_table.shape[-1]
    leading = values[..., :half_rot]
    trailing = values[..., half_rot:2 * half_rot]
    return jnp.concatenate([leading * cosine_table - trailing * sine_table, trailing * cosine_table + leading * sine_table, values[..., 2 * half_rot:]], axis=-1)

def sequence_forward(params, seq_rows, doc_row, omega, cosine_table, sine_table):
    qkv_weight, qkv_bias, dense_weight, up_weight, up_bias, down_weight, out_bias, gain_one, shift_one, gain_two, shift_two = params
    mixing = jnp.dot(dct_matrix(HEAD_DIM), omega, precision=EXACT)
    normed_one = low(layer_norm(seq_rows, gain_one, shift_one))
    normed_two = low(layer_norm(seq_rows, gain_two, shift_two))
    projected = low_back(jnp.dot(normed_one, qkv_weight, precision=EXACT) + qkv_bias)
    projected = projected.reshape(LEN, HEADS, 3, HEAD_DIM)
    queries = jnp.transpose(projected[:, :, 0], (1, 0, 2))
    key_heads = jnp.transpose(projected[:, :, 1], (1, 0, 2))
    value_heads = low(jnp.transpose(projected[:, :, 2], (1, 0, 2)))
    query_feat = low(jnp.exp(jnp.einsum('hte,ef->htf', rotate(queries, cosine_table, sine_table), mixing, precision=EXACT)))
    key_feat = low(jnp.exp(jnp.einsum('hte,ef->htf', rotate(key_heads, cosine_table, sine_table), mixing, precision=EXACT)))
    places = jnp.arange(LEN)
    allowed = (doc_row[:, None] == doc_row[None, :]) & (places[:, None] >= places[None, :])

    def attend(pieces):
        query_rows, key_rows, value_rows = pieces
        weights = jnp.where(allowed, jnp.dot(query_rows, key_rows.T, precision=EXACT), 0.0)
        totals = lax.optimization_barrier(jnp.sum(weights, axis=-1, keepdims=True))
        return jnp.dot(weights, value_rows, precision=EXACT) / totals
    mixed_rows = lax.map(jax.checkpoint(attend), (query_feat, key_feat, value_heads))
    merged = low(jnp.transpose(mixed_rows, (1, 0, 2)).reshape(LEN, HEADS * HEAD_DIM))
    hidden = low_back(jnp.dot(normed_two, up_weight, precision=EXACT) + up_bias)
    activated = low(jax.nn.gelu(hidden, approximate=False))
    return seq_rows + jnp.dot(merged, dense_weight, precision=EXACT) + jnp.dot(activated, down_weight, precision=EXACT) + out_bias

def reference(inputs, qkv_weight, qkv_bias, dense_weight, up_weight, up_bias, down_weight, out_bias, gain_one, shift_one, gain_two, shift_two, feature_omega, doc_ids, out_grad):
    params = tuple((member.astype(jnp.float32) for member in (qkv_weight, qkv_bias, dense_weight, up_weight, up_bias, down_weight, out_bias, gain_one, shift_one, gain_two, shift_two)))
    omega = feature_omega.astype(jnp.float32)
    cosine_table, sine_table = rotary_tables(jnp.arange(LEN), ROT)
    rows_all = inputs.astype(jnp.float32).reshape(SEQS, LEN, D)
    grads_all = out_grad.astype(jnp.float32).reshape(SEQS, LEN, D)
    zero_grads = tuple((jnp.zeros_like(member) for member in params))

    def one_sequence(totals, pieces):
        seq_rows, doc_row, cotangent = pieces
        output, pullback = jax.vjp(lambda weights, token_rows: sequence_forward(weights, token_rows, doc_row, omega, cosine_table, sine_table), params, seq_rows)
        weight_grads, row_grads = pullback(cotangent)
        summed = tuple((total + added for total, added in zip(totals, weight_grads)))
        return (summed, (output, row_grads))
    totals, (outputs, row_grads) = lax.scan(one_sequence, zero_grads, (rows_all, doc_ids, grads_all))
    return (outputs.reshape(TOKENS, D).astype(jnp.bfloat16), row_grads.reshape(TOKENS, D), totals[0], totals[1], totals[2], totals[3], totals[4], totals[5], totals[6], totals[7], totals[8], totals[9], totals[10])
```

```python
import functools

import jax
import jax.numpy as jnp
from jax import lax
from jax.experimental import pallas as pl
from jax.experimental.pallas import tpu as pltpu
from jax.sharding import PartitionSpec as P

HEAD_DIM = 64
ROT = 16
EPS = 1e-05
EXACT = lax.Precision.HIGHEST
F32 = jnp.float32
BF16 = jnp.bfloat16
AXES = ("dp", "tensor")
VMEM_LIMIT = 56 * 1024 * 1024


def dot(a, b, dims=((1,), (0,)), precision=None):
    return lax.dot_general(a, b, (dims, ((), ())), precision=precision, preferred_element_type=F32)


NN = ((1,), (0,))
NT = ((1,), (1,))
TN = ((0,), (0,))


def dct_matrix(extent):
    indices = jnp.arange(extent, dtype=F32)
    cosines = jnp.cos(jnp.pi * (indices[:, None] + 0.5) * indices[None, :] / extent)
    scales = jnp.where(indices == 0, jnp.sqrt(1.0 / extent), jnp.sqrt(2.0 / extent))
    return cosines * scales[None, :]


def rope_tables(positions):
    half = ROT // 2
    frequencies = 10000.0 ** (-(jnp.arange(half, dtype=F32) * 2.0 / ROT))
    angles = positions.astype(F32)[:, None] * frequencies[None, :]
    cosine, sine = jnp.cos(angles), jnp.sin(angles)
    rows = positions.shape[0]
    rest = jnp.ones((rows, HEAD_DIM - ROT), F32)
    none = jnp.zeros((rows, half), F32)
    still = jnp.zeros((rows, HEAD_DIM - ROT), F32)
    keep = jnp.concatenate([cosine, cosine, rest] * 2, axis=1)
    ahead = jnp.concatenate([-sine, none, still] * 2, axis=1)
    behind = jnp.concatenate([none, sine, still] * 2, axis=1)
    return keep, ahead, behind


def turn(values, keep, ahead, behind, sign):
    width = 2 * HEAD_DIM
    half = ROT // 2
    moved = (
        pltpu.roll(values, width - half, axis=1) * ahead + pltpu.roll(values, half, axis=1) * behind
    )
    return values * keep + sign * moved


def halves(values):
    high = values.astype(BF16)
    return high, (values - high.astype(F32)).astype(BF16)


def widened(values):
    rows = values.shape[0]
    lanes = lax.broadcasted_iota(jnp.int32, (rows, HEAD_DIM), 1)
    return jnp.concatenate([values.astype(F32), (lanes < 2).astype(F32)], axis=1).astype(BF16)


def features_kernel(
    heads,
    table,
    x_ref,
    gain_one,
    shift_one,
    gain_two,
    shift_two,
    own_w,
    far_w,
    own_b,
    far_b,
    keep,
    ahead,
    behind,
    mixing,
    docs,
    norm_one,
    norm_two,
    mean_out,
    scale_out,
    feat_out,
    value_out,
    state_out,
):
    @pl.when(pl.program_id(0) == 0)
    def _():
        state_out[...] = jnp.zeros_like(state_out)

    x = x_ref[...].astype(F32)
    mean = jnp.mean(x, axis=-1, keepdims=True)
    centred = x - mean
    scale = lax.rsqrt(jnp.mean(centred * centred, axis=-1, keepdims=True) + EPS)
    unit = centred * scale
    one = (unit * gain_one[...] + shift_one[...]).astype(BF16)
    norm_one[...] = one
    norm_two[...] = (unit * gain_two[...] + shift_two[...]).astype(BF16)
    mean_out[...] = mean
    scale_out[...] = scale
    chosen = docs[...] == table[1]
    for side, (weight, bias) in enumerate(((own_w, own_b), (far_w, far_b))):
        projected = dot(one, weight[...]) + bias[...]
        for head in range(heads):
            start = head * 3 * HEAD_DIM
            place = side * heads + head
            pair = projected[:, start : start + 2 * HEAD_DIM]
            value = projected[:, start + 2 * HEAD_DIM : start + 3 * HEAD_DIM].astype(BF16)
            rotated = turn(pair, keep[...], ahead[...], behind[...], 1.0)
            feat = jnp.exp(dot(rotated, mixing[...], precision=EXACT))
            feat_out[:, place * 128 : (place + 1) * 128] = feat
            value_out[:, place * HEAD_DIM : (place + 1) * HEAD_DIM] = value
            key = jnp.where(chosen, feat[:, HEAD_DIM:], 0.0).astype(BF16)
            state_out[place] += dot(key, widened(value), TN)


def split_feat(feat):
    return feat[:, :HEAD_DIM].astype(BF16), feat[:, HEAD_DIM:].astype(BF16)


def allowed_pairs(doc_col, doc_row):
    size = doc_col.shape[0]
    rows = lax.broadcasted_iota(jnp.int32, (size, size), 0)
    cols = lax.broadcasted_iota(jnp.int32, (size, size), 1)
    return (doc_col == doc_row) & (rows >= cols)


def forward_kernel(
    heads,
    blocks,
    table,
    feat_ref,
    value_ref,
    doc_col,
    doc_row,
    first_state,
    mixed_out,
    merged_out,
    inverse_out,
    states_out,
    state,
):
    step = pl.program_id(0)

    @pl.when(step == 0)
    def _():
        state[...] = first_state[...]

    before = table[3 + step]
    last = table[3 + 2 * blocks + step]
    kept = (last == before).astype(F32)
    allowed = allowed_pairs(doc_col[...], doc_row[0])
    carried = doc_col[...] == before
    chosen = doc_col[...] == last
    mixed_parts, inverse_parts = [], []
    for head in range(heads):
        query, key = split_feat(feat_ref[:, head * 128 : (head + 1) * 128])
        value = widened(value_ref[:, head * HEAD_DIM : (head + 1) * HEAD_DIM])
        memory = state[head]
        states_out[0, head] = memory
        high, low = halves(memory)
        weights = jnp.where(allowed, dot(query, key, NT), 0.0).astype(BF16)
        sums = dot(weights, value) + jnp.where(carried, dot(query, high) + dot(query, low), 0.0)
        inverse = 1.0 / sums[:, HEAD_DIM : HEAD_DIM + 1]
        mixed_parts.append(sums[:, :HEAD_DIM] * inverse)
        inverse_parts.append(inverse)
        picked = jnp.where(chosen, key.astype(F32), 0.0).astype(BF16)
        state[head] = kept * memory + dot(picked, value, TN)
    mixed = jnp.concatenate(mixed_parts, axis=1)
    mixed_out[...] = mixed
    merged_out[...] = mixed.astype(BF16)
    inverse_out[...] = jnp.concatenate(inverse_parts, axis=1)


def grad_pair(mixed_grad, inverse, mixed):
    part = (mixed_grad * inverse).astype(BF16)
    total = -jnp.sum(part.astype(F32) * mixed, axis=-1, keepdims=True)
    high, low = halves(total)
    rows = mixed_grad.shape[0]
    lanes = lax.broadcasted_iota(jnp.int32, (rows, HEAD_DIM), 1)
    tail = jnp.where(lanes == 0, high.astype(F32), 0.0) + jnp.where(lanes == 1, low.astype(F32), 0.0)
    return jnp.concatenate([part.astype(F32), tail], axis=1).astype(BF16)


def later_kernel(heads, table, feat_ref, mixed_ref, inverse_ref, grad_ref, docs, later_out):
    @pl.when(pl.program_id(0) == 0)
    def _():
        later_out[...] = jnp.zeros_like(later_out)

    chosen = docs[...] == table[2]
    for head in range(heads):
        span = slice(head * HEAD_DIM, (head + 1) * HEAD_DIM)
        both = grad_pair(grad_ref[:, span], inverse_ref[:, head : head + 1], mixed_ref[:, span])
        query = jnp.where(chosen, feat_ref[:, head * 128 : head * 128 + HEAD_DIM], 0.0)
        later_out[head] += dot(query.astype(BF16), both, TN)


def backward_kernel(
    heads,
    blocks,
    table,
    feat_ref,
    value_ref,
    mixed_ref,
    inverse_ref,
    grad_ref,
    doc_col,
    doc_row,
    states_ref,
    first_later,
    keep,
    ahead,
    behind,
    mixing,
    own_out,
    far_out,
    later,
):
    step = blocks - 1 - pl.program_id(0)

    @pl.when(pl.program_id(0) == 0)
    def _():
        later[...] = first_later[...]

    before = table[3 + step]
    after = table[3 + blocks + step]
    first = table[3 + 3 * blocks + step]
    kept = (first == after).astype(F32)
    allowed = allowed_pairs(doc_col[...], doc_row[0])
    carried = doc_col[...] == before
    linked = doc_col[...] == after
    chosen = doc_col[...] == first
    for head in range(heads):
        span = slice(head * HEAD_DIM, (head + 1) * HEAD_DIM)
        feat = feat_ref[:, head * 128 : (head + 1) * 128]
        query, key = split_feat(feat)
        value = widened(value_ref[:, span])
        both = grad_pair(grad_ref[:, span], inverse_ref[:, head : head + 1], mixed_ref[:, span])
        weights = jnp.where(allowed, dot(query, key, NT), 0.0).astype(BF16)
        weight_grad = jnp.where(allowed, dot(both, value, NT), 0.0).astype(BF16)
        mem_high, mem_low = halves(states_ref[0, head])
        late = later[head]
        late_high, late_low = halves(late)
        query_grad = dot(weight_grad, key) + jnp.where(
            carried, dot(both, mem_high, NT) + dot(both, mem_low, NT), 0.0
        )
        key_grad = dot(weight_grad, query, TN) + jnp.where(
            linked, dot(value, late_high, NT) + dot(value, late_low, NT), 0.0
        )
        value_grad = dot(weights, both, TN) + jnp.where(
            linked, dot(key, late_high) + dot(key, late_low), 0.0
        )
        picked = jnp.where(chosen, query.astype(F32), 0.0).astype(BF16)
        later[head] = kept * late + dot(picked, both, TN)
        inner = jnp.concatenate([query_grad, key_grad], axis=1) * feat
        pair = turn(dot(inner, mixing[...], NT, EXACT), keep[...], ahead[...], behind[...], -1.0)
        out = own_out if head < heads // 2 else far_out
        start = (head % (heads // 2)) * 3 * HEAD_DIM
        out[:, start : start + 2 * HEAD_DIM] = pair.astype(BF16)
        out[:, start + 2 * HEAD_DIM : start + 3 * HEAD_DIM] = value_grad[:, :HEAD_DIM].astype(BF16)


def up_kernel(norm_ref, weight, bias, active_out, slope_out):
    hidden = dot(norm_ref[...], weight[...]) + bias[...]
    normal = 0.5 * (1.0 + lax.erf(hidden * 0.7071067811865476))
    density = jnp.exp(-0.5 * hidden * hidden) * 0.3989422804014327
    active_out[...] = (hidden * normal).astype(BF16)
    slope_out[...] = (normal + hidden * density).astype(BF16)


def norm_grad_kernel(
    own_pg,
    far_pg,
    own_hg,
    far_hg,
    own_qkv,
    far_qkv,
    own_up,
    far_up,
    x_ref,
    mean,
    scale,
    gain_one,
    gain_two,
    e_out,
    sums_out,
    qkv_sums,
    up_sums,
):
    @pl.when(pl.program_id(0) == 0)
    def _():
        sums_out[...] = jnp.zeros_like(sums_out)
        qkv_sums[...] = jnp.zeros_like(qkv_sums)
        up_sums[...] = jnp.zeros_like(up_sums)

    unit = (x_ref[...].astype(F32) - mean[...]) * scale[...]
    one = dot(own_pg[...], own_qkv[...], NT) + dot(far_pg[...], far_qkv[...], NT)
    two = dot(own_hg[...], own_up[...], NT) + dot(far_hg[...], far_up[...], NT)
    e_out[...] = (one * gain_one[...] + two * gain_two[...]).astype(BF16)
    down = lambda values: jnp.sum(values, axis=0, keepdims=True)
    sums_out[0:1] += down(one * unit)
    sums_out[1:2] += down(one)
    sums_out[2:3] += down(two * unit)
    sums_out[3:4] += down(two)
    qkv_sums[0:1] += down(own_pg[...].astype(F32))
    qkv_sums[1:2] += down(far_pg[...].astype(F32))
    up_sums[0:1] += down(own_hg[...].astype(F32))
    up_sums[1:2] += down(far_hg[...].astype(F32))


def params():
    return pltpu.CompilerParams(
        dimension_semantics=("arbitrary",), vmem_limit_bytes=VMEM_LIMIT
    )


def shape(dims, kind):
    return jax.ShapeDtypeStruct(dims, kind)


def cost(flops, nbytes, trans=0):
    return pl.CostEstimate(flops=int(flops), bytes_accessed=int(nbytes), transcendentals=int(trans))


def on_device(
    dp_size,
    tensor_size,
    inputs,
    qkv_weight,
    qkv_bias,
    dense_weight,
    up_weight,
    up_bias,
    down_weight,
    out_bias,
    gain_one,
    shift_one,
    gain_two,
    shift_two,
    feature_omega,
    doc_ids,
    out_grad,
):
    rows, width = inputs.shape
    inner = tensor_size // 2
    quarters = 4
    tokens = rows * inner
    qkv_cols = qkv_weight.shape[1]
    near_heads = qkv_cols // (3 * HEAD_DIM)
    heads = 2 * near_heads
    hidden_cols = up_weight.shape[1]
    merged_cols = dense_weight.shape[0]
    member = lax.axis_index("dp")
    place = lax.axis_index("tensor")
    half, slot = place // inner, place % inner
    part = member % quarters

    def swap(values, over_dp, over_tensor):
        pairs = [
            (p * tensor_size + t, (p ^ over_dp) * tensor_size + (t ^ over_tensor))
            for p in range(dp_size)
            for t in range(tensor_size)
        ]
        return lax.ppermute(values, AXES, pairs)

    def across(values, source_half):
        pairs = [
            (p * tensor_size + source_half * inner + t, p * tensor_size + (1 - source_half) * inner + t)
            for p in range(dp_size)
            for t in range(inner)
        ]
        return lax.ppermute(values, AXES, pairs)

    def gather(block):
        return [block] + [swap(block, 0, k) for k in range(1, inner)]

    def scatter(partial):
        total = partial[:rows].astype(F32)
        for k in range(inner - 1, 0, -1):
            total += swap(partial[k * rows : (k + 1) * rows], 0, k).astype(F32)
        return total

    x_all = jnp.concatenate(gather(inputs), axis=0)

    bias_row = jnp.concatenate([qkv_bias, up_bias])[None, :]
    tall = jnp.concatenate([qkv_weight, up_weight], axis=1)
    quarter_rows = width // quarters
    first_pack = jnp.concatenate(
        [
            lax.dynamic_slice_in_dim(tall, part * quarter_rows, quarter_rows, 0),
            jnp.broadcast_to(bias_row, (16, qkv_cols + hidden_cols)),
        ],
        axis=0,
    )
    dense_rows, down_rows = merged_cols // quarters, hidden_cols // quarters
    second_pack = jnp.concatenate(
        [
            lax.dynamic_slice_in_dim(dense_weight, part * dense_rows, dense_rows, 0),
            lax.dynamic_slice_in_dim(down_weight, part * down_rows, down_rows, 0),
        ],
        axis=0,
    )

    def share(pack):
        mine = swap(pack, 0, inner)
        return share_quarters(mine)

    def share_quarters(mine):
        size = mine.shape[0]
        third = swap(mine, 2, 0)
        others = swap(jnp.concatenate([mine, third], axis=0), 1, 0)
        return [mine, others[:size], third, others[size:]]

    def ordered(pieces, kind):
        size = pieces[0].shape[0]
        whole = jnp.zeros((quarters * size,) + pieces[0].shape[1:], kind)
        for k in range(quarters):
            whole = lax.dynamic_update_slice_in_dim(whole, pieces[k].astype(kind), (part ^ k) * size, 0)
        return whole

    firsts = share(first_pack)
    seconds = share(second_pack)
    far_qkv = ordered([v[:quarter_rows, :qkv_cols] for v in firsts], BF16)
    far_up = ordered([v[:quarter_rows, qkv_cols:] for v in firsts], BF16)
    far_bias = firsts[0][quarter_rows : quarter_rows + 1]
    far_dense = ordered([v[:dense_rows] for v in seconds], BF16)
    far_down = ordered([v[dense_rows:] for v in seconds], BF16)

    grad_all = jnp.concatenate(gather(out_grad), axis=0)

    docs = doc_ids.reshape(-1)
    chunk_docs = docs.reshape(tensor_size, rows)
    first_docs, last_docs = chunk_docs[:, 0], chunk_docs[:, -1]
    none = jnp.full((1,), -1, jnp.int32)
    before_docs = jnp.concatenate([none, last_docs[:-1]])
    after_docs = jnp.concatenate([first_docs[1:], none])
    mine = lambda values: lax.dynamic_slice_in_dim(values, half * inner, inner, 0)
    table = jnp.concatenate(
        [
            slot[None],
            mine(last_docs)[-1:],
            mine(first_docs)[:1],
            mine(before_docs),
            mine(after_docs),
            mine(last_docs),
            mine(first_docs),
        ]
    ).astype(jnp.int32)
    half_docs = mine(chunk_docs)
    doc_cols = half_docs.reshape(tokens, 1)
    doc_rows = half_docs.reshape(inner, 1, rows)
    keep, ahead, behind = rope_tables(half * tokens + jnp.arange(tokens))
    core = jnp.dot(dct_matrix(HEAD_DIM), feature_omega, precision=EXACT)
    empty = jnp.zeros_like(core)
    mixing = jnp.concatenate(
        [jnp.concatenate([core, empty], axis=1), jnp.concatenate([empty, core], axis=1)], axis=0
    )
    row = lambda values: values.astype(F32).reshape(1, -1)

    here = lambda cols: pl.BlockSpec((rows, cols), lambda k, table: (k, 0))
    moved = lambda cols: pl.BlockSpec((rows, cols), lambda k, table: (k ^ table[0], 0))
    fixed = lambda *dims: pl.BlockSpec(dims, lambda k, table: (0,) * len(dims))

    norm_one, norm_two, mean, scale, feat, value, state = pl.pallas_call(
        functools.partial(features_kernel, near_heads),
        out_shape=(
            shape((tokens, width), BF16),
            shape((tokens, width), BF16),
            shape((tokens, 1), F32),
            shape((tokens, 1), F32),
            shape((tokens, heads * 128), F32),
            shape((tokens, heads * HEAD_DIM), BF16),
            shape((heads, HEAD_DIM, 128), F32),
        ),
        grid_spec=pltpu.PrefetchScalarGridSpec(
            num_scalar_prefetch=1,
            grid=(inner,),
            in_specs=[
                here(width),
                fixed(1, width),
                fixed(1, width),
                fixed(1, width),
                fixed(1, width),
                fixed(width, qkv_cols),
                fixed(width, qkv_cols),
                fixed(1, qkv_cols),
                fixed(1, qkv_cols),
                moved(128),
                moved(128),
                moved(128),
                fixed(128, 128),
                moved(1),
            ],
            out_specs=[
                here(width),
                here(width),
                here(1),
                here(1),
                here(heads * 128),
                here(heads * HEAD_DIM),
                fixed(heads, HEAD_DIM, 128),
            ],
        ),
        compiler_params=params(),
        cost_estimate=cost(2 * tokens * width * 2 * qkv_cols, 12e6),
        name="features",
    )(
        table,
        x_all,
        row(gain_one),
        row(shift_one),
        row(gain_two),
        row(shift_two),
        qkv_weight,
        far_qkv,
        row(qkv_bias),
        row(far_bias[:, :qkv_cols]),
        keep,
        ahead,
        behind,
        mixing,
        doc_cols,
    )

    def exchanged(values):
        return jnp.concatenate([values[near_heads:], values[:near_heads]], axis=0)

    first_state = exchanged(across(state, 0))

    def up_projection(weight, bias):
        return pl.pallas_call(
            up_kernel,
            out_shape=(shape((tokens, hidden_cols), BF16),) * 2,
            grid=(inner,),
            in_specs=[
                pl.BlockSpec((rows, width), lambda k: (k, 0)),
                pl.BlockSpec((width, hidden_cols), lambda k: (0, 0)),
                pl.BlockSpec((1, hidden_cols), lambda k: (0, 0)),
            ],
            out_specs=[pl.BlockSpec((rows, hidden_cols), lambda k: (k, 0))] * 2,
            compiler_params=params(),
            cost_estimate=cost(2 * tokens * width * hidden_cols, 5e6, 2 * tokens * hidden_cols),
            name="up",
        )(norm_two, weight, row(bias))

    own_active, own_slope = up_projection(up_weight, up_bias)
    far_active, far_slope = up_projection(far_up, far_bias[:, qkv_cols:])

    flow = lambda cols: pl.BlockSpec((rows, cols), lambda m, table: (m ^ table[0], 0))
    straight = lambda cols: pl.BlockSpec((rows, cols), lambda m, table: (m, 0))
    mixed, merged, inverse, states = pl.pallas_call(
        functools.partial(forward_kernel, heads, inner),
        out_shape=(
            shape((tokens, heads * HEAD_DIM), F32),
            shape((tokens, heads * HEAD_DIM), BF16),
            shape((tokens, heads), F32),
            shape((inner, heads, HEAD_DIM, 128), F32),
        ),
        grid_spec=pltpu.PrefetchScalarGridSpec(
            num_scalar_prefetch=1,
            grid=(inner,),
            in_specs=[
                flow(heads * 128),
                flow(heads * HEAD_DIM),
                straight(1),
                pl.BlockSpec((1, 1, rows), lambda m, table: (m, 0, 0)),
                fixed(heads, HEAD_DIM, 128),
            ],
            out_specs=[
                flow(heads * HEAD_DIM),
                flow(heads * HEAD_DIM),
                flow(heads),
                pl.BlockSpec((1, heads, HEAD_DIM, 128), lambda m, table: (m, 0, 0, 0)),
            ],
            scratch_shapes=[pltpu.VMEM((heads, HEAD_DIM, 128), F32)],
        ),
        compiler_params=params(),
        cost_estimate=cost(heads * tokens * rows * 800, 5e6),
        name="attend",
    )(table, feat, value, doc_cols, doc_rows, first_state)

    dense_both = jnp.concatenate([dense_weight, far_dense], axis=0)
    partial_out = (
        dot(merged, dense_both) + dot(own_active, down_weight) + dot(far_active, far_down)
    ).astype(BF16)
    layer_out = (inputs.astype(F32) + scatter(partial_out) + out_bias.astype(F32)).astype(BF16)

    merged_grad = dot(grad_all, dense_both, NT)
    own_hidden_grad = (dot(grad_all, down_weight, NT) * own_slope.astype(F32)).astype(BF16)
    far_hidden_grad = (dot(grad_all, far_down, NT) * far_slope.astype(F32)).astype(BF16)

    later = pl.pallas_call(
        functools.partial(later_kernel, heads),
        out_shape=shape((heads, HEAD_DIM, 128), F32),
        grid_spec=pltpu.PrefetchScalarGridSpec(
            num_scalar_prefetch=1,
            grid=(inner,),
            in_specs=[
                here(heads * 128),
                here(heads * HEAD_DIM),
                here(heads),
                here(heads * HEAD_DIM),
                moved(1),
            ],
            out_specs=fixed(heads, HEAD_DIM, 128),
        ),
        compiler_params=params(),
        cost_estimate=cost(heads * tokens * 64 * 256, 5e6),
        name="later",
    )(table, feat, mixed, inverse, merged_grad, doc_cols)
    first_later = exchanged(across(later, 1))

    back = lambda cols: pl.BlockSpec((rows, cols), lambda m, table: ((inner - 1 - m) ^ table[0], 0))
    back_straight = lambda cols: pl.BlockSpec((rows, cols), lambda m, table: (inner - 1 - m, 0))
    own_pg, far_pg = pl.pallas_call(
        functools.partial(backward_kernel, heads, inner),
        out_shape=(shape((tokens, qkv_cols), BF16),) * 2,
        grid_spec=pltpu.PrefetchScalarGridSpec(
            num_scalar_prefetch=1,
            grid=(inner,),
            in_specs=[
                back(heads * 128),
                back(heads * HEAD_DIM),
                back(heads * HEAD_DIM),
                back(heads),
                back(heads * HEAD_DIM),
                back_straight(1),
                pl.BlockSpec((1, 1, rows), lambda m, table: (inner - 1 - m, 0, 0)),
                pl.BlockSpec((1, heads, HEAD_DIM, 128), lambda m, table: (inner - 1 - m, 0, 0, 0)),
                fixed(heads, HEAD_DIM, 128),
                back_straight(128),
                back_straight(128),
                back_straight(128),
                fixed(128, 128),
            ],
            out_specs=[back(qkv_cols), back(qkv_cols)],
            scratch_shapes=[pltpu.VMEM((heads, HEAD_DIM, 128), F32)],
        ),
        compiler_params=params(),
        cost_estimate=cost(heads * tokens * rows * 2000, 8e6),
        name="attend_back",
    )(
        table,
        feat,
        value,
        mixed,
        inverse,
        merged_grad,
        doc_cols,
        doc_rows,
        states,
        first_later,
        keep,
        ahead,
        behind,
        mixing,
    )

    block = lambda cols: pl.BlockSpec((rows, cols), lambda k: (k, 0))
    whole = lambda *dims: pl.BlockSpec(dims, lambda k: (0,) * len(dims))
    partial_e, sums, qkv_sums, up_sums = pl.pallas_call(
        norm_grad_kernel,
        out_shape=(
            shape((tokens, width), BF16),
            shape((8, width), F32),
            shape((8, qkv_cols), F32),
            shape((8, hidden_cols), F32),
        ),
        grid=(inner,),
        in_specs=[
            block(qkv_cols),
            block(qkv_cols),
            block(hidden_cols),
            block(hidden_cols),
            whole(width, qkv_cols),
            whole(width, qkv_cols),
            whole(width, hidden_cols),
            whole(width, hidden_cols),
            block(width),
            block(1),
            block(1),
            whole(1, width),
            whole(1, width),
        ],
        out_specs=[block(width), whole(8, width), whole(8, qkv_cols), whole(8, hidden_cols)],
        compiler_params=params(),
        cost_estimate=cost(4 * tokens * width * (qkv_cols + hidden_cols), 12e6),
        name="norm_grad",
    )(
        own_pg,
        far_pg,
        own_hidden_grad,
        far_hidden_grad,
        qkv_weight,
        far_qkv,
        up_weight,
        far_up,
        x_all,
        mean,
        scale,
        row(gain_one),
        row(gain_two),
    )

    def weight_sum(own, far):
        both = [v.reshape((2, 2, v.shape[0] // 4) + v.shape[1:]) for v in (own, far)]
        both = jnp.concatenate(both, axis=2)
        core_bit, y_bit = part % 2, part // 2
        kept = lax.dynamic_index_in_dim(both, core_bit, 1, keepdims=False)
        sent = lax.dynamic_index_in_dim(both, 1 - core_bit, 1, keepdims=False)
        pair = (kept.astype(F32) + swap(sent, 1, 0).astype(F32)).astype(BF16)
        kept = lax.dynamic_index_in_dim(pair, y_bit, 0, keepdims=False)
        sent = lax.dynamic_index_in_dim(pair, 1 - y_bit, 0, keepdims=False)
        quad = (kept.astype(F32) + swap(sent, 2, 0).astype(F32)).astype(BF16)
        size = own.shape[0] // 4
        total = (quad[:size].astype(F32) + swap(quad[size:], 0, inner).astype(F32)).astype(BF16)
        step = 4
        while step < dp_size:
            total = (total.astype(F32) + swap(total, step, 0).astype(F32)).astype(BF16)
            step *= 2
        return share_quarters(total)

    tn = lambda a, b: dot(a, b, TN).astype(BF16)
    own_lower = [tn(merged[:, :merged_cols], grad_all), tn(own_active, grad_all)]
    far_lower = [tn(merged[:, merged_cols:], grad_all), tn(far_active, grad_all)]

    def quartered(parts):
        return jnp.concatenate(
            [v.reshape((4, v.shape[0] // 4) + v.shape[1:]) for v in parts], axis=1
        ).reshape((-1, width))

    lower = weight_sum(quartered(own_lower), quartered(far_lower))
    dense_grad = ordered([v[:dense_rows] for v in lower], F32)
    down_grad = ordered([v[dense_rows:] for v in lower], F32)
    upper = weight_sum(tn(norm_two, own_hidden_grad), tn(norm_two, far_hidden_grad))
    up_grad = ordered(upper, F32)
    qkv_pieces = weight_sum(tn(norm_one, own_pg), tn(norm_one, far_pg))
    qkv_grad = ordered(qkv_pieces, F32)

    def spread(values, slice_cols):
        line = jnp.zeros((tensor_size * slice_cols,), F32)
        line = lax.dynamic_update_slice_in_dim(line, values[0], place * slice_cols, 0)
        other = (place + inner) % tensor_size
        return lax.dynamic_update_slice_in_dim(line, values[1], other * slice_cols, 0)

    bias_part = jnp.sum(out_grad.astype(F32), axis=0)
    small = jnp.concatenate(
        [
            sums[:4].reshape(-1),
            bias_part,
            spread(qkv_sums[:2], qkv_cols),
            spread(up_sums[:2], hidden_cols),
        ]
    )
    small = lax.psum(small, AXES)
    cut = width // tensor_size
    piece = lambda start, size: lax.dynamic_slice_in_dim(small, start + place * size, size, 0)
    qkv_bias_grad = piece(5 * width, qkv_cols)
    up_bias_grad = piece(5 * width + tensor_size * qkv_cols, hidden_cols)

    e_rows = scatter(partial_e)
    unit = (inputs.astype(F32) - mean[:rows]) * scale[:rows]
    input_grad = out_grad.astype(F32) + scale[:rows] * (
        e_rows
        - jnp.mean(e_rows, axis=-1, keepdims=True)
        - unit * jnp.mean(e_rows * unit, axis=-1, keepdims=True)
    )
    return (
        layer_out,
        input_grad,
        qkv_grad,
        qkv_bias_grad,
        dense_grad,
        up_grad,
        up_bias_grad,
        down_grad,
        piece(4 * width, cut),
        piece(0, cut),
        piece(width, cut),
        piece(2 * width, cut),
        piece(3 * width, cut),
    )


def solution(mesh):
    in_specs = (
        P(("dp", "tensor"), None),
        P(None, "tensor"),
        P("tensor"),
        P("tensor", None),
        P(None, "tensor"),
        P("tensor"),
        P("tensor", None),
        P(),
        P(),
        P(),
        P(),
        P(),
        P(),
        P("dp", None),
        P(("dp", "tensor"), None),
    )
    out_specs = (
        P(("dp", "tensor"), None),
        P(("dp", "tensor"), None),
        P(None, "tensor"),
        P("tensor"),
        P("tensor", None),
        P(None, "tensor"),
        P("tensor"),
        P("tensor", None),
        P("tensor"),
        P("tensor"),
        P("tensor"),
        P("tensor"),
        P("tensor"),
    )
    return jax.shard_map(
        functools.partial(on_device, mesh.shape["dp"], mesh.shape["tensor"]),
        mesh=mesh,
        in_specs=in_specs,
        out_specs=out_specs,
        check_vma=False,
    )
```

```python
import functools

import jax
import jax.numpy as jnp
import numpy as np
from jax import lax
from jax.experimental import pallas as pl
from jax.experimental.pallas import tpu as pltpu
from jax.sharding import PartitionSpec as P

HEAD_DIM = 64
ROT = 16
LANES = 128
EPS = 1e-05
EXACT = lax.Precision.HIGHEST
F32 = jnp.float32
BF16 = jnp.bfloat16
AXES = ("dp", "tensor")
VMEM_LIMIT = 16 * 1024 * 1024
QUARTERS = 4

NN = ((1,), (0,))
NT = ((1,), (1,))
TN = ((0,), (0,))


def dot(a, b, dims=NN, precision=None):
    return lax.dot_general(a, b, (dims, ((), ())), precision=precision, preferred_element_type=F32)


def halves(values):
    high = values.astype(BF16)
    return high, (values - high.astype(F32)).astype(BF16)


def lane_of(dims):
    return lax.broadcasted_iota(jnp.int32, dims, len(dims) - 1)


def prepare_kernel(table, rates, omega, keep, ahead, behind, mix_high, mix_low, turned_high, turned_low):
    rows = keep.shape[0]
    start = (table[1] * pl.num_programs(0) + pl.program_id(0)) * rows
    places = start + lax.broadcasted_iota(jnp.int32, (rows, LANES), 0)
    angles = places.astype(F32) * rates[...]
    inner = lane_of((rows, LANES)) % HEAD_DIM
    cosine, sine = jnp.cos(angles), jnp.sin(angles)
    half = ROT // 2
    keep[...] = jnp.where(inner < ROT, cosine, 1.0)
    ahead[...] = jnp.where(inner < half, -sine, 0.0)
    behind[...] = jnp.where((inner >= half) & (inner < ROT), sine, 0.0)

    @pl.when(pl.program_id(0) == 0)
    def _():
        extent = HEAD_DIM
        n = lax.broadcasted_iota(jnp.int32, (LANES, LANES), 0)
        k = lax.broadcasted_iota(jnp.int32, (LANES, LANES), 1)
        same = (n // extent) == (k // extent)
        n, k = (n % extent).astype(F32), (k % extent).astype(F32)
        scale = jnp.where(k == 0, float(np.sqrt(1.0 / extent)), float(np.sqrt(2.0 / extent)))
        matrix = jnp.where(same, jnp.cos(np.pi * (n + 0.5) * k / extent) * scale, 0.0)
        row = jnp.concatenate([omega[...]] * 2, axis=1)
        spread = jnp.where(same, jnp.concatenate([row] * 2, axis=0), 0.0)
        mixing = dot(matrix, spread, precision=EXACT)
        mix_high[...], mix_low[...] = halves(mixing)
        turned_high[...], turned_low[...] = halves(mixing.T)


def turn(values, keep, ahead, behind, sign):
    half = ROT // 2
    moved = (
        pltpu.roll(values, LANES - half, axis=1) * ahead + pltpu.roll(values, half, axis=1) * behind
    )
    return values * keep + sign * moved


def mixed_dot(values, high, low):
    first, second = halves(values)
    return dot(first, high) + (dot(second, high) + dot(first, low))


def head_columns(values, which, count):
    parts = [
        values[:, (3 * j + which) * HEAD_DIM : (3 * j + which + 1) * HEAD_DIM] for j in range(count)
    ]
    return parts[0] if count == 1 else jnp.concatenate(parts, axis=1)


def masked_stack(values, count):
    if count == 1:
        return values
    lane = (lane_of(values.shape) % (count * HEAD_DIM)) // HEAD_DIM
    zero = jnp.zeros_like(values)
    return jnp.concatenate([jnp.where(lane == j, values, zero) for j in range(count)], axis=0)


def side_by_side(stack, count):
    rows = stack.shape[0] // count
    if count == 1:
        return stack
    return jnp.concatenate([stack[j * rows : (j + 1) * rows] for j in range(count)], axis=1)


def own_block(dims):
    rows = lax.broadcasted_iota(jnp.int32, dims, 0) // HEAD_DIM
    return rows == (lane_of(dims) % dims[0]) // HEAD_DIM


def compress(state, count):
    width = count * HEAD_DIM
    sides = []
    for base in (0, width):
        part = state[:, base : base + HEAD_DIM]
        for j in range(1, count):
            rows = lax.broadcasted_iota(jnp.int32, part.shape, 0) // HEAD_DIM
            here = state[:, base + j * HEAD_DIM : base + (j + 1) * HEAD_DIM]
            part = jnp.where(rows == j, here, part)
        sides.append(part)
    return jnp.concatenate(sides, axis=1)


def expand(packed, count):
    values, totals = packed[:, :HEAD_DIM], packed[:, HEAD_DIM:]
    wide = jnp.concatenate([values] * count + [totals] * count, axis=1)
    return jnp.where(own_block(wide.shape), wide, 0.0)


def project(count, one, weight, bias, turns, mix_high, mix_low, chosen, feat_out, value_out, state):
    width = count * HEAD_DIM
    projected = dot(one, weight) + bias
    value = head_columns(projected, 2, count).astype(BF16)
    pairs = [head_columns(projected, which, count) for which in (0, 1)]
    if count == 1:
        pairs = [jnp.concatenate(pairs, axis=1)]
    feats = []
    for pair in pairs:
        feats.append(jnp.exp(mixed_dot(turn(pair, *turns, 1.0), mix_high, mix_low)))
    feat = feats[0] if count == 1 else jnp.concatenate(feats, axis=1)
    feat_out[...] = feat
    value_out[...] = value
    key = jnp.where(chosen, feat[:, width:], 0.0).astype(BF16)
    state[...] += dot(key, jnp.concatenate([value, jnp.ones_like(value)], axis=1), TN)


def own_features_kernel(count, blocks, table, docs, *refs):
    x_refs = refs[:blocks]
    (
        affine,
        weight,
        bias,
        keep,
        ahead,
        behind,
        mix_high,
        mix_low,
        docs_col,
        norm_one,
        norm_two,
        unit_out,
        feat_out,
        value_out,
        state_out,
        state,
        x_keep,
    ) = refs[blocks:]

    @pl.when(pl.program_id(0) == 0)
    def _():
        state[...] = jnp.zeros_like(state)

    for k in range(blocks):

        @pl.when(pl.program_id(0) == k)
        def _(k=k):
            x_keep[...] = x_refs[k][...]

    rows = x_keep.shape[0]
    x = x_keep[...].astype(F32)
    mean = jnp.mean(x, axis=-1, keepdims=True)
    centred = x - mean
    scale = lax.rsqrt(jnp.mean(centred * centred, axis=-1, keepdims=True) + EPS)
    unit = centred * scale
    one = (unit * affine[0:1] + affine[1:2]).astype(BF16)
    norm_one[...] = one
    norm_two[...] = (unit * affine[2:3] + affine[3:4]).astype(BF16)
    unit_out[...] = unit.astype(BF16)
    chosen = docs_col[...] == docs[(table[1] + 1) * blocks * rows - 1]
    project(
        count,
        one,
        weight[...],
        bias[...].astype(F32),
        (keep[...], ahead[...], behind[...]),
        mix_high[...],
        mix_low[...],
        chosen,
        feat_out,
        value_out,
        state,
    )

    @pl.when(pl.program_id(0) == pl.num_programs(0) - 1)
    def _():
        state_out[...] = compress(state[...], count)


def far_features_kernel(
    count,
    table,
    docs,
    norm_one,
    weight,
    bias,
    keep,
    ahead,
    behind,
    mix_high,
    mix_low,
    docs_col,
    near_state,
    feat_out,
    value_out,
    state_out,
    state,
):
    @pl.when(pl.program_id(0) == 0)
    def _():
        state[...] = jnp.zeros_like(state)

    rows = norm_one.shape[0]
    chosen = docs_col[...] == docs[(table[1] + 1) * pl.num_programs(0) * rows - 1]
    project(
        count,
        norm_one[...],
        weight[...],
        bias[0:1, : weight.shape[1]].astype(F32),
        (keep[...], ahead[...], behind[...]),
        mix_high[...],
        mix_low[...],
        chosen,
        feat_out,
        value_out,
        state,
    )

    @pl.when(pl.program_id(0) == pl.num_programs(0) - 1)
    def _():
        state_out[0] = near_state[...]
        state_out[1] = compress(state[...], count)


def allowed_pairs(docs_col, docs_row, count):
    size = docs_col.shape[0]
    rows = lax.broadcasted_iota(jnp.int32, (size, size), 0)
    cols = lax.broadcasted_iota(jnp.int32, (size, size), 1)
    allowed = ((docs_col == docs_row) & (rows >= cols)).astype(F32)
    return allowed if count == 1 else jnp.concatenate([allowed] * count, axis=0)


def forward_kernel(
    count,
    table,
    docs,
    own_feat,
    far_feat,
    own_value,
    far_value,
    docs_col,
    docs_row,
    first_state,
    mixed_out,
    merged_out,
    inverse_out,
    states_out,
    state,
):
    step = pl.program_id(0)
    width = count * HEAD_DIM
    rows = own_feat.shape[0]

    @pl.when(step == 0)
    def _():
        for side in range(2):
            state[side] = expand(first_state[1 - side], count)

    start = (table[1] * pl.num_programs(0) + step) * rows
    before = jnp.where(start > 0, docs[jnp.maximum(start - 1, 0)], -1)
    last = docs[start + rows - 1]
    kept = (last == before).astype(F32)
    allowed = allowed_pairs(docs_col[...], docs_row[0], count)
    carried = docs_col[...] == before
    chosen = docs_col[...] == last
    for side in range(2):
        feat_ref, value_ref = ((own_feat, own_value), (far_feat, far_value))[side]
        query = feat_ref[:, :width].astype(BF16)
        key = feat_ref[:, width:]
        value = value_ref[...]
        both = jnp.concatenate([value, jnp.ones_like(value)], axis=1)
        memory = state[side]
        states_out[0, side] = memory
        high, low = halves(memory)
        weights = (dot(masked_stack(query, count), key.astype(BF16), NT) * allowed).astype(BF16)
        sums = dot(side_by_side(weights, count), masked_stack(both, count)) + jnp.where(
            carried, dot(query, high) + dot(query, low), 0.0
        )
        inverse = 1.0 / sums[:, width:]
        mixed = sums[:, :width] * inverse
        mixed_out[:, side * width : (side + 1) * width] = mixed
        merged_out[:, side * width : (side + 1) * width] = mixed.astype(BF16)
        inverse_out[:, side * width : (side + 1) * width] = inverse
        picked = jnp.where(chosen, key, 0.0).astype(BF16)
        added = dot(picked, both, TN)
        state[side] = kept * memory + jnp.where(own_block(added.shape), added, 0.0)


def pair_grads(grad, inverse, mixed):
    part = (grad * inverse).astype(BF16)
    high, low = halves(-(part.astype(F32) * mixed))
    return part, high, low


def later_kernel(
    count,
    table,
    docs,
    grad_ref,
    own_dense,
    far_dense,
    own_feat,
    far_feat,
    mixed_ref,
    inverse_ref,
    docs_col,
    merged_grad,
    later_out,
    later,
):
    @pl.when(pl.program_id(0) == 0)
    def _():
        later[...] = jnp.zeros_like(later)

    width = count * HEAD_DIM
    rows = own_feat.shape[0]
    chosen = docs_col[...] == docs[table[1] * pl.num_programs(0) * rows]
    for side, dense in enumerate((own_dense, far_dense)):
        span = slice(side * width, (side + 1) * width)
        grad = dot(grad_ref[...], dense[...], NT)
        merged_grad[:, span] = grad
        part, high, low = pair_grads(grad, inverse_ref[:, span], mixed_ref[:, span])
        query = (own_feat, far_feat)[side][:, :width]
        query = jnp.where(chosen, query, 0.0).astype(BF16)
        later[side, :, :width] += dot(query, part, TN)
        later[side, :, width:] += dot(query, high, TN) + dot(query, low, TN)

    @pl.when(pl.program_id(0) == pl.num_programs(0) - 1)
    def _():
        for side in range(2):
            later_out[side] = compress(later[side], count)


def backward_kernel(
    count,
    table,
    docs,
    own_feat,
    far_feat,
    own_value,
    far_value,
    mixed_ref,
    inverse_ref,
    grad_ref,
    docs_col,
    docs_row,
    states_ref,
    first_later,
    keep,
    ahead,
    behind,
    turned_high,
    turned_low,
    own_out,
    far_out,
    later,
):
    blocks = pl.num_programs(0)
    step = blocks - 1 - pl.program_id(0)
    width = count * HEAD_DIM
    rows = own_feat.shape[0]

    @pl.when(pl.program_id(0) == 0)
    def _():
        for side in range(2):
            later[side] = expand(first_later[1 - side], count)

    start = (table[1] * blocks + step) * rows
    total = docs.shape[0]
    before = jnp.where(start > 0, docs[jnp.maximum(start - 1, 0)], -1)
    after = jnp.where(start + rows < total, docs[jnp.minimum(start + rows, total - 1)], -1)
    first = docs[start]
    kept = (first == after).astype(F32)
    allowed = allowed_pairs(docs_col[...], docs_row[0], count)
    carried = docs_col[...] == before
    linked = docs_col[...] == after
    chosen = docs_col[...] == first
    for side in range(2):
        span = slice(side * width, (side + 1) * width)
        feat = (own_feat, far_feat)[side][...]
        query, key = feat[:, :width].astype(BF16), feat[:, width:].astype(BF16)
        value = (own_value, far_value)[side][...]
        ones = jnp.ones_like(value)
        both = jnp.concatenate([value, ones], axis=1)
        part, high, low = pair_grads(grad_ref[:, span], inverse_ref[:, span], mixed_ref[:, span])
        first_two = jnp.concatenate([part, high], axis=1)
        queries = masked_stack(query, count)
        weights = (dot(queries, key, NT) * allowed).astype(BF16)
        weight_grad = dot(masked_stack(first_two, count), both, NT)
        weight_grad += dot(masked_stack(low, count), ones, NT)
        weight_grad = (weight_grad * allowed).astype(BF16)
        mem_high, mem_low = halves(states_ref[0, side])
        late = later[side]
        late_high, late_low = halves(late)
        query_grad = dot(side_by_side(weight_grad, count), masked_stack(key, count)) + jnp.where(
            carried,
            dot(first_two, mem_high, NT) + dot(first_two, mem_low, NT) + dot(low, mem_high[:, width:], NT),
            0.0,
        )
        key_grad = dot(weight_grad, queries, TN) + jnp.where(
            linked, dot(both, late_high, NT) + dot(both, late_low, NT), 0.0
        )
        value_grad = dot(weights, masked_stack(part, count), TN) + jnp.where(
            linked, dot(key, late_high[:, :width]) + dot(key, late_low[:, :width]), 0.0
        )
        picked = jnp.where(chosen, query.astype(F32), 0.0).astype(BF16)
        block = own_block(late.shape)
        added = jnp.concatenate(
            [dot(picked, part, TN), dot(picked, high, TN) + dot(picked, low, TN)], axis=1
        )
        later[side] = kept * late + jnp.where(block, added, 0.0)
        inner = jnp.concatenate([query_grad, key_grad], axis=1) * feat
        pairs = []
        for base in range(0, 2 * width, LANES):
            pair = mixed_dot(inner[:, base : base + LANES], turned_high[...], turned_low[...])
            pairs.append(turn(pair, keep[...], ahead[...], behind[...], -1.0))
        flat = pairs[0] if count == 1 else jnp.concatenate(pairs, axis=1)
        pieces = []
        for j in range(count):
            lanes = slice(j * HEAD_DIM, (j + 1) * HEAD_DIM)
            pieces += [flat[:, :width][:, lanes], flat[:, width:][:, lanes], value_grad[:, lanes]]
        out = own_out if side == 0 else far_out
        out[...] = jnp.concatenate(pieces, axis=1).astype(BF16)


def up_kernel(norm_ref, weight, bias, active_out, slope_out):
    hidden = dot(norm_ref[...], weight[...], NT) + bias[...]
    normal = 0.5 * (1.0 + lax.erf(hidden * 0.7071067811865476))
    density = jnp.exp(-0.5 * hidden * hidden) * 0.3989422804014327
    active_out[...] = (hidden * normal).astype(BF16)
    slope_out[...] = (normal + hidden * density).astype(BF16)


def down_back_kernel(grad_ref, weight, slope, hidden_out, sums_out):
    hidden = (dot(grad_ref[...], weight[...], NT) * slope[...].astype(F32)).astype(BF16)
    hidden_out[...] = hidden

    @pl.when(pl.program_id(0) == 0)
    def _():
        sums_out[...] = jnp.zeros_like(sums_out)

    sums_out[0:1] += jnp.sum(hidden.astype(F32), axis=0, keepdims=True)


def out_kernel(merged, own_active, far_active, own_dense, far_dense, own_down, far_down, *outs):
    width = own_dense.shape[0]
    total = dot(own_active[...], own_down[...]) + dot(far_active[...], far_down[...])
    total += dot(merged[:, :width], own_dense[...]) + dot(merged[:, width:], far_dense[...])
    write_block(outs, total.astype(BF16))


def write_block(outs, values):
    for k, out in enumerate(outs):

        @pl.when(pl.program_id(0) == k)
        def _(out=out):
            out[...] = values


def norm_grad_kernel(
    own_pg,
    far_pg,
    own_hg,
    far_hg,
    own_qkv,
    far_qkv,
    own_up,
    far_up,
    unit_ref,
    affine,
    grad_sums,
    sums_out,
    *outs,
):
    @pl.when(pl.program_id(0) == 0)
    def _():
        sums_out[...] = jnp.zeros_like(sums_out)
        sums_out[4:5] = grad_sums[0:1]

    down = lambda values: jnp.sum(values, axis=0, keepdims=True)
    unit = unit_ref[...].astype(F32)
    one = dot(own_pg[...], own_qkv[...], NT) + dot(far_pg[...], far_qkv[...], NT)
    sums_out[0:1] += down(one * unit)
    sums_out[1:2] += down(one)
    two = dot(own_hg[...], own_up[...]) + dot(far_hg[...], far_up[...])
    sums_out[2:3] += down(two * unit)
    sums_out[3:4] += down(two)
    write_block(outs, (one * affine[0:1] + two * affine[2:3]).astype(BF16))


def first_pack_kernel(table, weight, dense, bias, out):
    rows, small = weight.shape[0], dense.shape[0]
    if out.shape[1] > min(weight.shape[1], dense.shape[1]):
        out[...] = jnp.zeros_like(out)
    out[:rows, : weight.shape[1]] = weight[...]
    out[rows : rows + small, : dense.shape[1]] = dense[...]
    out[rows + small :, : bias.shape[1]] = jnp.broadcast_to(bias[...], (16, bias.shape[1]))


def arrange_kernel(table, up, down, bias, own_up, own_down, own_bias, pack, turned):
    part = table[2]
    step = down.shape[0] // QUARTERS
    turned[...] = up[...].T
    for k in range(QUARTERS):
        begin = pl.multiple_of((part ^ k) * step, step)
        own_up[k * step : (k + 1) * step] = turned[pl.ds(begin, step)]
        own_down[k * step : (k + 1) * step] = down[pl.ds(begin, step)]
    own_bias[...] = jnp.concatenate([bias[part ^ k].astype(F32) for k in range(QUARTERS)], axis=1)
    pack[:step] = own_up[:step]
    pack[step : 2 * step] = own_down[:step]
    pack[2 * step :] = jnp.zeros((16, pack.shape[1]), BF16)
    pack[2 * step :, :step] = jnp.broadcast_to(bias[part], (16, step))


def collect_first_kernel(table, mine, others, third, far_qkv, far_dense):
    part = table[2]
    step = far_qkv.shape[0] // QUARTERS
    small = far_dense.shape[0]
    size = mine.shape[0]
    for k, (ref, base) in enumerate(((mine, 0), (others, 0), (third, 0), (others, size))):
        begin = pl.multiple_of((part ^ k) * step, step)
        far_qkv[pl.ds(begin, step)] = ref[base : base + step, : far_qkv.shape[1]]
        far_dense[:, pl.ds(begin, step)] = ref[base + step : base + step + small, :step]


def collect_second_kernel(table, mine, others, third, far_up, far_down, far_bias):
    step = far_down.shape[0] // QUARTERS
    size = mine.shape[0]
    biases = []
    for k, (ref, base) in enumerate(((mine, 0), (others, 0), (third, 0), (others, size))):
        far_up[k * step : (k + 1) * step] = ref[base : base + step]
        far_down[k * step : (k + 1) * step] = ref[base + step : base + 2 * step]
        tail = ref[base + 2 * step : base + size].astype(F32)
        biases.append(tail[0:1, :step])
    far_bias[...] = jnp.concatenate(biases, axis=1)


def collect_grad_kernel(*refs):
    blocks, (whole, sums) = refs[:-2], refs[-2:]
    rows = blocks[0].shape[0]
    for k, ref in enumerate(blocks):
        whole[k * rows : (k + 1) * rows] = ref[...]
    sums[...] = jnp.zeros_like(sums)
    sums[0:1] = jnp.sum(blocks[0][...].astype(F32), axis=0, keepdims=True)


def bias_rows(values, cols):
    tile = jnp.zeros((16, values.shape[1]), F32)
    row = lax.broadcasted_iota(jnp.int32, tile.shape, 0)
    high = values.astype(BF16).astype(F32)
    tile = jnp.where(row == 0, high, jnp.where(row == 1, values - high, tile)).astype(BF16)
    if values.shape[1] == cols:
        return tile
    return jnp.concatenate([tile, jnp.zeros((16, cols - values.shape[1]), BF16)], axis=1)


def hidden_weights_kernel(
    table, active, hidden_grad, merged, grad, norm_two, hidden_sums, kept, sent, dense
):
    part = table[2]
    step, small = active.shape[1] // QUARTERS, merged.shape[1] // QUARTERS
    cols = kept.shape[2]
    dense[...] = dot(merged[...], grad[...], TN).astype(BF16)
    down = dot(active[...], grad[...], TN).astype(BF16)
    up = dot(hidden_grad[...], norm_two[...], TN).astype(BF16)
    for k in range(QUARTERS):
        out = (kept, sent)[k % 2].at[k // 2]
        span = slice(k * step, (k + 1) * step)
        out[:step] = up[span]
        out[step : 2 * step] = down[span]
        begin = pl.multiple_of((part ^ k) * small, small)
        out[2 * step : 2 * step + small] = dense[pl.ds(begin, small)]
        out[2 * step + small :] = bias_rows(hidden_sums[0:1, span], cols)


def qkv_weights_kernel(table, own_pg, far_pg, norm_one, kept, sent, full):
    part = table[2]
    cols = kept.shape[2]
    step = full.shape[0] // QUARTERS
    for side, grad in enumerate((own_pg, far_pg)):
        full[...] = dot(norm_one[...], grad[...], TN).astype(BF16)
        tail = bias_rows(jnp.sum(grad[...].astype(F32), axis=0, keepdims=True), cols)
        for k in range(QUARTERS):
            out = (kept, sent)[k % 2].at[2 * (k // 2) + side]
            begin = pl.multiple_of((part ^ k) * step, step)
            out[:step] = full[pl.ds(begin, step)]
            out[step:] = tail


def finish_hidden_kernel(
    table, mine, near, third, last, up_grad, down_grad, dense_grad, bias_grad, turned
):
    part = table[2]
    step, small = down_grad.shape[0] // QUARTERS, dense_grad.shape[0] // QUARTERS
    size = mine.shape[0]
    for k, ref in enumerate((mine, near, third, last)):
        begin = pl.multiple_of((part ^ k) * step, step)
        turned[pl.ds(begin, step)] = ref[:step].astype(F32)
        down_grad[pl.ds(begin, step)] = ref[step : 2 * step].astype(F32)
        begin = pl.multiple_of((part ^ k) * small, small)
        dense_grad[pl.ds(begin, small)] = ref[2 * step : 2 * step + small].astype(F32)
        tail = ref[2 * step + small : size].astype(F32)
        bias_grad[part ^ k] = tail[0:1, :step] + tail[1:2, :step]
    up_grad[...] = turned[...].T


def finish_qkv_kernel(table, mine, near, third, last, weight_grad, bias_grad):
    part = table[2]
    step = weight_grad.shape[0] // QUARTERS
    for k, ref in enumerate((mine, near, third, last)):
        begin = pl.multiple_of((part ^ k) * step, step)
        weight_grad[pl.ds(begin, step)] = ref[:step].astype(F32)
    tail = mine[step:].astype(F32)
    bias_grad[...] = tail[0:1] + tail[1:2]


def finish_out_kernel(x_ref, bias, *refs):
    parts, out = refs[:-1], refs[-1]
    total = x_ref[...].astype(F32) + bias[...].astype(F32)
    for ref in parts:
        total += ref[...].astype(F32)
    out[...] = total.astype(BF16)


def finish_in_kernel(x_ref, grad_ref, *refs):
    parts, out = refs[:-1], refs[-1]
    x = x_ref[...].astype(F32)
    mean = jnp.mean(x, axis=-1, keepdims=True)
    centred = x - mean
    scale = lax.rsqrt(jnp.mean(centred * centred, axis=-1, keepdims=True) + EPS)
    unit = centred * scale
    total = parts[0][...].astype(F32)
    for ref in parts[1:]:
        total += ref[...].astype(F32)
    along = jnp.mean(total * unit, axis=-1, keepdims=True)
    out[...] = grad_ref[...].astype(F32) + scale * (
        total - jnp.mean(total, axis=-1, keepdims=True) - unit * along
    )


def params():
    return pltpu.CompilerParams(
        dimension_semantics=("arbitrary",), vmem_limit_bytes=VMEM_LIMIT
    )


def after(value, *others):
    return lax.optimization_barrier((value,) + others)[0]


def shape(dims, kind):
    return jax.ShapeDtypeStruct(dims, kind)


def cost(flops, nbytes, trans=0):
    return pl.CostEstimate(flops=1000, bytes_accessed=1000, transcendentals=0)


def on_device(
    dp_size,
    tensor_size,
    inputs,
    qkv_weight,
    qkv_bias,
    dense_weight,
    up_weight,
    up_bias,
    down_weight,
    out_bias,
    gain_one,
    shift_one,
    gain_two,
    shift_two,
    feature_omega,
    doc_ids,
    out_grad,
):
    rows, model = inputs.shape
    inner = tensor_size // 2
    tokens = rows * inner
    qkv_cols = qkv_weight.shape[1]
    count = qkv_cols // (3 * HEAD_DIM)
    width = count * HEAD_DIM
    hidden_cols = up_weight.shape[1]
    dense_part, hidden_part, model_part = width // QUARTERS, hidden_cols // QUARTERS, model // QUARTERS
    member = lax.axis_index("dp")
    place = lax.axis_index("tensor")
    half, slot = place // inner, place % inner
    part = member % QUARTERS

    def swap(values, over_dp, over_tensor):
        pairs = [
            (p * tensor_size + t, (p ^ over_dp) * tensor_size + (t ^ over_tensor))
            for p in range(dp_size)
            for t in range(tensor_size)
        ]
        return lax.ppermute(values, AXES, pairs)

    def across(values, source_half):
        pairs = [
            (p * tensor_size + source_half * inner + t, p * tensor_size + (1 - source_half) * inner + t)
            for p in range(dp_size)
            for t in range(inner)
        ]
        return lax.ppermute(values, AXES, pairs)

    def gather(block):
        return [block] + [swap(block, 0, k) for k in range(1, inner)]

    line = []

    def run(step, *operands, gate=0, wait=()):
        operands = list(operands)
        held = tuple(line[-1:]) + tuple(wait)
        if held:
            operands[gate] = after(operands[gate], *held)
        result = step(*operands)
        line.append(result[0] if isinstance(result, (tuple, list)) else result)
        return result

    table = jnp.stack([slot, half, part]).astype(jnp.int32)
    plain = lambda cols: pl.BlockSpec((rows, cols), lambda k, *s: (k, 0))
    moved = lambda cols: pl.BlockSpec((rows, cols), lambda k, table, *s: (k ^ table[0], 0))
    whole = lambda *dims: pl.BlockSpec(dims, lambda k, *s: (0,) * len(dims))
    spec = lambda values: whole(*values.shape)

    def call(kernel, name, outs, in_specs, out_specs, price, prefetch=1, scratch=(), steps=inner):
        return pl.pallas_call(
            kernel,
            out_shape=outs,
            grid_spec=pltpu.PrefetchScalarGridSpec(
                num_scalar_prefetch=prefetch,
                grid=(steps,),
                in_specs=in_specs,
                out_specs=out_specs,
                scratch_shapes=list(scratch),
            ),
            compiler_params=params(),
            cost_estimate=price,
            name=name,
        )

    def once(kernel, name, outs, prefetch=1, scratch=()):
        single = not isinstance(outs, (tuple, list))
        listed = (outs,) if single else tuple(outs)

        def step(*operands):
            result = call(
                kernel,
                name,
                listed,
                [spec(v) for v in operands[prefetch:]],
                [whole(*v.shape) for v in listed],
                cost(0, 0),
                prefetch,
                scratch,
                1,
            )(*operands)
            return result[0] if single else result

        return step

    docs = doc_ids.reshape(-1)
    docs_col = docs.reshape(-1, 1)
    docs_row = docs.reshape(tensor_size, 1, rows)
    affine = jnp.stack([gain_one, shift_one, gain_two, shift_two]).astype(F32)
    lane = np.arange(LANES) % HEAD_DIM
    rates = np.where(lane < ROT, 10000.0 ** (-(lane % (ROT // 2)) * 2.0 / ROT), 0.0)
    rates = jnp.asarray(rates[None, :], F32)
    own_bias = qkv_bias.reshape(1, -1)

    x_blocks = gather(inputs)
    first_rows, first_cols = model_part + width + 16, max(qkv_cols, model_part)
    first_pack = run(
        call(
            first_pack_kernel,
            "first_pack",
            shape((first_rows, first_cols), BF16),
            [
                pl.BlockSpec((model_part, qkv_cols), lambda k, table: (table[2], 0)),
                pl.BlockSpec((width, model_part), lambda k, table: (0, table[2])),
                whole(1, qkv_cols),
            ],
            whole(first_rows, first_cols),
            cost(1e5, 4e5),
            steps=1,
        ),
        table,
        qkv_weight,
        dense_weight,
        own_bias,
    )
    first_mine = swap(first_pack, 0, inner)
    pack_rows = 2 * hidden_part + dense_part + 16
    second_rows = 2 * hidden_part + 16
    own_up, own_down, own_up_bias, second_pack = run(
        once(
            arrange_kernel,
            "arrange",
            (
                shape((hidden_cols, model), BF16),
                shape((hidden_cols, model), BF16),
                shape((1, hidden_cols), F32),
                shape((second_rows, model), BF16),
            ),
            scratch=[pltpu.VMEM((hidden_cols, model), BF16)],
        ),
        table,
        up_weight,
        down_weight,
        up_bias.reshape(QUARTERS, 1, hidden_part),
        gate=3,
    )
    second_mine = swap(second_pack, 0, inner)
    square = whole(LANES, LANES)
    keep, ahead, behind, mix_high, mix_low, turned_high, turned_low = run(
        call(
            prepare_kernel,
            "prepare",
            (shape((tokens, LANES), F32),) * 3 + (shape((LANES, LANES), BF16),) * 4,
            [whole(1, LANES), whole(HEAD_DIM, HEAD_DIM)],
            [plain(LANES)] * 3 + [square] * 4,
            cost(1e6, 2e6),
        ),
        table,
        rates,
        feature_omega,
        gate=2,
    )

    wide = pltpu.VMEM((2, width, 2 * width), F32)
    narrow = pltpu.VMEM((width, 2 * width), F32)
    mine_col = pl.BlockSpec(
        (rows, 1), lambda k, table, docs: ((k ^ table[0]) + table[1] * inner, 0)
    )
    norm_one, norm_two, unit, own_feat, own_value, near_state = run(
        call(
            functools.partial(own_features_kernel, count, inner),
            "own_features",
            (
                shape((tokens, model), BF16),
                shape((tokens, model), BF16),
                shape((tokens, model), BF16),
                shape((tokens, 2 * width), F32),
                shape((tokens, width), BF16),
                shape((width, LANES), F32),
            ),
            [whole(rows, model)] * inner
            + [
                whole(4, model),
                whole(model, qkv_cols),
                whole(1, qkv_cols),
                moved(LANES),
                moved(LANES),
                moved(LANES),
                square,
                square,
                mine_col,
            ],
            [
                plain(model),
                plain(model),
                plain(model),
                plain(2 * width),
                plain(width),
                whole(width, LANES),
            ],
            cost(2 * tokens * model * qkv_cols, 12e6),
            prefetch=2,
            scratch=[narrow, pltpu.VMEM((rows, model), BF16)],
        ),
        table,
        docs,
        *x_blocks,
        affine,
        qkv_weight,
        own_bias,
        keep,
        ahead,
        behind,
        mix_high,
        mix_low,
        docs_col,
        gate=2 + inner,
        wait=(first_mine,),
    )
    here_x = tuple(x_blocks[1:]) + (keep,)
    first_third = swap(after(first_mine, *here_x), 2, 0)
    grad_blocks = gather(after(out_grad, *here_x))
    first_others = swap(
        run(lambda a, b: jnp.concatenate([a, b], axis=0), first_mine, first_third), 1, 0
    )
    far_qkv, far_dense = run(
        once(
            collect_first_kernel,
            "collect_first",
            (shape((model, qkv_cols), BF16), shape((width, model), BF16)),
        ),
        table,
        first_mine,
        first_others,
        first_third,
        gate=1,
        wait=(second_mine,),
    )
    second_third = swap(second_mine, 2, 0)
    far_feat, far_value, state = run(
        call(
            functools.partial(far_features_kernel, count),
            "far_features",
            (
                shape((tokens, 2 * width), F32),
                shape((tokens, width), BF16),
                shape((2, width, LANES), F32),
            ),
            [
                plain(model),
                whole(model, qkv_cols),
                pl.BlockSpec((16, first_cols), lambda k, *s: ((model_part + width) // 16, 0)),
                moved(LANES),
                moved(LANES),
                moved(LANES),
                square,
                square,
                mine_col,
                whole(width, LANES),
            ],
            [plain(2 * width), plain(width), whole(2, width, LANES)],
            cost(2 * tokens * model * qkv_cols, 8e6),
            prefetch=2,
            scratch=[narrow],
        ),
        table,
        docs,
        norm_one,
        far_qkv,
        first_mine,
        keep,
        ahead,
        behind,
        mix_high,
        mix_low,
        docs_col,
        near_state,
        gate=2,
    )
    first_state = across(state, 0)

    def simple(kernel, name, outs, in_specs, out_specs, price):
        return call(kernel, name, outs, in_specs, out_specs, price, prefetch=0)

    def up_projection(weight, bias):
        return run(
            simple(
                up_kernel,
                "up",
                (shape((tokens, hidden_cols), BF16),) * 2,
                [plain(model), whole(hidden_cols, model), whole(1, hidden_cols)],
                [plain(hidden_cols)] * 2,
                cost(2 * tokens * model * hidden_cols, 5e6, 2 * tokens * hidden_cols),
            ),
            norm_two,
            weight,
            bias,
        )

    own_active, own_slope = up_projection(own_up, own_up_bias)

    block_row = pl.BlockSpec((1, 1, rows), lambda m, table, docs: (m + table[1] * inner, 0, 0))
    block_col = pl.BlockSpec((rows, 1), lambda m, table, docs: (m + table[1] * inner, 0))
    mixed, merged, inverse, states = run(
        call(
            functools.partial(forward_kernel, count),
            "attend",
            (
                shape((tokens, 2 * width), F32),
                shape((tokens, 2 * width), BF16),
                shape((tokens, 2 * width), F32),
                shape((inner, 2, width, 2 * width), F32),
            ),
            [
                moved(2 * width),
                moved(2 * width),
                moved(width),
                moved(width),
                block_col,
                block_row,
                whole(2, width, LANES),
            ],
            [
                moved(2 * width),
                moved(2 * width),
                moved(2 * width),
                pl.BlockSpec((1, 2, width, 2 * width), lambda m, *s: (m, 0, 0, 0)),
            ],
            cost(2 * count * tokens * rows * 800, 5e6),
            prefetch=2,
            scratch=[wide],
        ),
        table,
        docs,
        own_feat,
        far_feat,
        own_value,
        far_value,
        docs_col,
        docs_row,
        first_state,
        gate=2,
    )
    grad_all, grad_sums = run(
        once(
            collect_grad_kernel,
            "collect_grad",
            (shape((tokens, model), BF16), shape((8, model), F32)),
            prefetch=0,
        ),
        *grad_blocks,
        gate=1,
    )
    both_second = run(lambda a, b: jnp.concatenate([a, b], axis=0), second_mine, second_third)
    second_others = swap(both_second, 1, 0)
    merged_grad, later = run(
        call(
            functools.partial(later_kernel, count),
            "later",
            (shape((tokens, 2 * width), F32), shape((2, width, LANES), F32)),
            [
                plain(model),
                whole(width, model),
                whole(width, model),
                plain(2 * width),
                plain(2 * width),
                plain(2 * width),
                plain(2 * width),
                mine_col,
            ],
            [plain(2 * width), whole(2, width, LANES)],
            cost(2 * count * tokens * 64 * 256, 5e6),
            prefetch=2,
            scratch=[wide],
        ),
        *(table, docs, grad_all, dense_weight, far_dense, own_feat, far_feat, mixed, inverse, docs_col),
        gate=2,
    )
    first_later = across(later, 1)

    def down_back(weight, slope):
        return run(
            simple(
                down_back_kernel,
                "down_back",
                (shape((tokens, hidden_cols), BF16), shape((8, hidden_cols), F32)),
                [plain(model), whole(hidden_cols, model), plain(hidden_cols)],
                [plain(hidden_cols), whole(8, hidden_cols)],
                cost(2 * tokens * model * hidden_cols, 5e6),
            ),
            grad_all,
            weight,
            slope,
            gate=2,
        )

    def add(a, b):
        return (a.astype(F32) + b.astype(F32)).astype(BF16)

    def rest(total):
        step = QUARTERS
        while step < dp_size:
            total = add(total, swap(total, step, 0))
            step *= 2
        return total

    def hidden_weights(active, hidden_grad, side, sums_row):
        return run(
            call(
                hidden_weights_kernel,
                "hidden_weights",
                (shape((2, pack_rows, model), BF16),) * 2,
                [
                    whole(tokens, hidden_cols),
                    whole(tokens, hidden_cols),
                    pl.BlockSpec((tokens, width), lambda k, table: (0, side))
                    if width % LANES == 0
                    else whole(tokens, width),
                    whole(tokens, model),
                    whole(tokens, model),
                    whole(8, hidden_cols),
                ],
                [whole(2, pack_rows, model)] * 2,
                cost(2 * tokens * model * (2 * hidden_cols + width), 9e6),
                scratch=[pltpu.VMEM((width, model), BF16)],
                steps=1,
            ),
            table,
            active,
            hidden_grad,
            merged if width % LANES == 0 else merged[:, side * width : (side + 1) * width],
            grad_all,
            norm_two,
            sums_row,
            gate=2,
        )

    own_hidden_grad, own_up_sums = down_back(own_down, own_slope)
    own_kept, own_sent = hidden_weights(own_active, own_hidden_grad, 0, own_up_sums)
    own_got = swap(own_sent, 1, 0)
    far_up, far_down, far_up_bias = run(
        once(
            collect_second_kernel,
            "collect_second",
            (
                shape((hidden_cols, model), BF16),
                shape((hidden_cols, model), BF16),
                shape((1, hidden_cols), F32),
            ),
        ),
        table,
        second_mine,
        second_others,
        second_third,
        gate=1,
    )
    far_active, far_slope = up_projection(far_up, far_up_bias)
    partial_out = run(
        simple(
            out_kernel,
            "out",
            (shape((rows, model), BF16),) * inner,
            [
                plain(2 * width),
                plain(hidden_cols),
                plain(hidden_cols),
                whole(width, model),
                whole(width, model),
                whole(hidden_cols, model),
                whole(hidden_cols, model),
            ],
            [whole(rows, model)] * inner,
            cost(4 * tokens * model * (width + hidden_cols), 8e6),
        ),
        merged,
        own_active,
        far_active,
        dense_weight,
        far_dense,
        own_down,
        far_down,
    )

    def scatter(blocks):
        return [blocks[0]] + [swap(blocks[k], 0, k) for k in range(1, inner)]

    out_parts = scatter(partial_out)

    far_hidden_grad, far_up_sums = down_back(far_down, far_slope)
    own_next = run(add, own_kept[1], own_got[1])
    own_cross = swap(own_next, 2, 0)
    far_kept, far_sent = hidden_weights(far_active, far_hidden_grad, 1, far_up_sums)
    far_got = swap(far_sent, 1, 0)

    back = lambda cols: pl.BlockSpec((rows, cols), lambda m, table, docs: ((inner - 1 - m) ^ table[0], 0))
    back_straight = lambda cols: pl.BlockSpec((rows, cols), lambda m, *s: (inner - 1 - m, 0))
    own_pg, far_pg = run(
        call(
            functools.partial(backward_kernel, count),
            "attend_back",
            (shape((tokens, qkv_cols), BF16),) * 2,
            [
                back(2 * width),
                back(2 * width),
                back(width),
                back(width),
                back(2 * width),
                back(2 * width),
                back(2 * width),
                pl.BlockSpec(
                    (rows, 1), lambda m, table, docs: (inner - 1 - m + table[1] * inner, 0)
                ),
                pl.BlockSpec(
                    (1, 1, rows), lambda m, table, docs: (inner - 1 - m + table[1] * inner, 0, 0)
                ),
                pl.BlockSpec((1, 2, width, 2 * width), lambda m, *s: (inner - 1 - m, 0, 0, 0)),
                whole(2, width, LANES),
                back_straight(LANES),
                back_straight(LANES),
                back_straight(LANES),
                square,
                square,
            ],
            [back(qkv_cols), back(qkv_cols)],
            cost(2 * count * tokens * rows * 2000, 8e6),
            prefetch=2,
            scratch=[wide],
        ),
        table,
        docs,
        own_feat,
        far_feat,
        own_value,
        far_value,
        mixed,
        inverse,
        merged_grad,
        docs_col,
        docs_row,
        states,
        first_later,
        keep,
        ahead,
        behind,
        turned_high,
        turned_low,
        gate=8,
    )
    far_next = run(add, far_kept[1], far_got[1])
    far_cross = swap(far_next, 2, 0)
    own_quad = run(lambda a, b, c: add(add(a, b), c), own_kept[0], own_got[0], own_cross)
    layer_out = run(
        once(finish_out_kernel, "finish_out", shape((rows, model), BF16), prefetch=0),
        inputs,
        out_bias.reshape(1, -1),
        *out_parts,
        gate=2,
    )
    kept, sent = run(
        once(
            qkv_weights_kernel,
            "qkv_weights",
            (shape((4, model_part + 16, qkv_cols), BF16),) * 2,
            scratch=[pltpu.VMEM((model, qkv_cols), BF16)],
        ),
        table,
        own_pg,
        far_pg,
        norm_one,
        gate=3,
    )
    got = swap(sent, 1, 0)
    norm_grads = run(
        simple(
            norm_grad_kernel,
            "norm_grad",
            (shape((8, model), F32),) + (shape((rows, model), BF16),) * inner,
            [
                plain(qkv_cols),
                plain(qkv_cols),
                plain(hidden_cols),
                plain(hidden_cols),
                whole(model, qkv_cols),
                whole(model, qkv_cols),
                whole(hidden_cols, model),
                whole(hidden_cols, model),
                plain(model),
                whole(4, model),
                whole(8, model),
            ],
            [whole(8, model)] + [whole(rows, model)] * inner,
            cost(4 * tokens * model * (qkv_cols + hidden_cols), 12e6),
        ),
        own_pg,
        far_pg,
        own_hidden_grad,
        far_hidden_grad,
        qkv_weight,
        far_qkv,
        own_up,
        far_up,
        unit,
        affine,
        grad_sums,
        gate=8,
    )
    e_parts = scatter(norm_grads[1:])
    cross_sent = run(add, kept[2:], got[2:])
    crossed = swap(cross_sent, 2, 0)
    far_quad = run(lambda a, b, c: add(add(a, b), c), far_kept[0], far_got[0], far_cross)
    far_home = swap(far_quad, 0, inner)
    far_piece = run(lambda a, b, c: add(add(a, b), c), kept[1], got[1], crossed[1])
    far_piece_home = swap(far_piece, 0, inner)
    own_piece = run(lambda a, b, c: add(add(a, b), c), kept[0], got[0], crossed[0])
    input_grad = run(
        once(finish_in_kernel, "finish_in", shape((rows, model), F32), prefetch=0),
        inputs,
        out_grad,
        *e_parts,
        gate=2,
    )
    upper_mine = rest(run(add, own_piece, far_piece_home))
    upper_third = swap(upper_mine, 2, 0)
    upper_near = swap(upper_mine, 1, 0)
    lower_mine = rest(run(add, own_quad, far_home))
    lower_third = swap(lower_mine, 2, 0)
    lower_near = swap(lower_mine, 1, 0)
    upper = (upper_mine, upper_near, upper_third, swap(upper_third, 1, 0))
    lower = (lower_mine, lower_near, lower_third, swap(lower_third, 1, 0))

    small = after(norm_grads[0], input_grad)
    step = 1
    while step < dp_size:
        small = small + swap(small, step, 0)
        step *= 2
    step = 1
    while step < tensor_size:
        small = small + swap(small, 0, step)
        step *= 2
    cols = model // tensor_size
    small = lax.dynamic_slice_in_dim(small, place * cols, cols, 1)

    up_grad, down_grad, dense_grad, up_bias_grad = run(
        once(
            finish_hidden_kernel,
            "finish_hidden",
            (
                shape((model, hidden_cols), F32),
                shape((hidden_cols, model), F32),
                shape((width, model), F32),
                shape((QUARTERS, 1, hidden_part), F32),
            ),
            scratch=[pltpu.VMEM((hidden_cols, model), F32)],
        ),
        table,
        *lower,
        gate=1,
    )
    qkv_grad, qkv_bias_grad = run(
        once(
            finish_qkv_kernel,
            "finish_qkv",
            (shape((model, qkv_cols), F32), shape((1, qkv_cols), F32)),
        ),
        table,
        *upper,
        gate=1,
    )

    return (
        layer_out,
        input_grad,
        qkv_grad,
        qkv_bias_grad.reshape(-1),
        dense_grad,
        up_grad,
        up_bias_grad.reshape(-1),
        down_grad,
        small[4],
        small[0],
        small[1],
        small[2],
        small[3],
    )


def solution(mesh):
    in_specs = (
        P(("dp", "tensor"), None),
        P(None, "tensor"),
        P("tensor"),
        P("tensor", None),
        P(None, "tensor"),
        P("tensor"),
        P("tensor", None),
        P(),
        P(),
        P(),
        P(),
        P(),
        P(),
        P("dp", None),
        P(("dp", "tensor"), None),
    )
    out_specs = (
        P(("dp", "tensor"), None),
        P(("dp", "tensor"), None),
        P(None, "tensor"),
        P("tensor"),
        P("tensor", None),
        P(None, "tensor"),
        P("tensor"),
        P("tensor", None),
        P("tensor"),
        P("tensor"),
        P("tensor"),
        P("tensor"),
        P("tensor"),
    )
    return jax.shard_map(
        functools.partial(on_device, mesh.shape["dp"], mesh.shape["tensor"]),
        mesh=mesh,
        in_specs=in_specs,
        out_specs=out_specs,
        check_vma=False,
    )
```

```python
import functools

import jax
import jax.numpy as jnp
import numpy as np
from jax import lax
from jax.experimental import pallas as pl
from jax.experimental.pallas import tpu as pltpu
from jax.sharding import PartitionSpec as P

HEAD_DIM = 64
ROT = 16
LANES = 128
EPS = 1e-05
EXACT = lax.Precision.HIGHEST
F32 = jnp.float32
BF16 = jnp.bfloat16
QUARTERS = 4

NN = ((1,), (0,))
NT = ((1,), (1,))
TN = ((0,), (0,))


def dot(a, b, dims=NN, precision=None):
    return lax.dot_general(a, b, (dims, ((), ())), precision=precision, preferred_element_type=F32)


def halves(values):
    high = values.astype(BF16)
    return high, (values - high.astype(F32)).astype(BF16)


def lane_of(dims):
    return lax.broadcasted_iota(jnp.int32, dims, len(dims) - 1)


def prepare_kernel(rates, omega, docs_col, keep, ahead, behind, mix_high, mix_low, turned_high, turned_low):
    rows = keep.shape[0]
    start = pl.program_id(0) * rows
    places = start + lax.broadcasted_iota(jnp.int32, (rows, LANES), 0)
    angles = places.astype(F32) * rates[...]
    inner = lane_of((rows, LANES)) % HEAD_DIM
    cosine, sine = jnp.cos(angles), jnp.sin(angles)
    half = ROT // 2
    keep[...] = jnp.where(inner < ROT, cosine, 1.0)
    ahead[...] = jnp.where(inner < half, -sine, 0.0)
    behind[...] = jnp.where((inner >= half) & (inner < ROT), sine, 0.0)

    @pl.when(pl.program_id(0) == 0)
    def _():
        extent = HEAD_DIM
        n = lax.broadcasted_iota(jnp.int32, (LANES, LANES), 0)
        k = lax.broadcasted_iota(jnp.int32, (LANES, LANES), 1)
        same = (n // extent) == (k // extent)
        n, k = (n % extent).astype(F32), (k % extent).astype(F32)
        scale = jnp.where(k == 0, float(np.sqrt(1.0 / extent)), float(np.sqrt(2.0 / extent)))
        matrix = jnp.where(same, jnp.cos(np.pi * (n + 0.5) * k / extent) * scale, 0.0)
        row = jnp.concatenate([omega[...]] * 2, axis=1)
        spread = jnp.where(same, jnp.concatenate([row] * 2, axis=0), 0.0)
        mixing = dot(matrix, spread, precision=EXACT)
        mix_high[...], mix_low[...] = halves(mixing)
        turned_high[...], turned_low[...] = halves(mixing.T)


def turn(values, keep, ahead, behind, sign):
    half = ROT // 2
    moved = (
        pltpu.roll(values, LANES - half, axis=1) * ahead + pltpu.roll(values, half, axis=1) * behind
    )
    return values * keep + sign * moved


def mixed_dot(values, high, low):
    first, second = halves(values)
    return dot(first, high) + (dot(second, high) + dot(first, low))


def head_columns(values, which, count):
    parts = [
        values[:, (3 * j + which) * HEAD_DIM : (3 * j + which + 1) * HEAD_DIM] for j in range(count)
    ]
    return parts[0] if count == 1 else jnp.concatenate(parts, axis=1)


def masked_stack(values, count):
    if count == 1:
        return values
    lane = (lane_of(values.shape) % (count * HEAD_DIM)) // HEAD_DIM
    zero = jnp.zeros_like(values)
    return jnp.concatenate([jnp.where(lane == j, values, zero) for j in range(count)], axis=0)


def side_by_side(stack, count):
    rows = stack.shape[0] // count
    if count == 1:
        return stack
    return jnp.concatenate([stack[j * rows : (j + 1) * rows] for j in range(count)], axis=1)


def own_block(dims):
    rows = lax.broadcasted_iota(jnp.int32, dims, 0) // HEAD_DIM
    return rows == (lane_of(dims) % dims[0]) // HEAD_DIM


def load_block(plan, refs, keep, sems):
    def copies(k):
        names = plan[k]
        size = keep.shape[1] // len(names)
        slot = keep.at[k % 2]
        return [
            pltpu.make_async_copy(refs[name], slot.at[pl.ds(i * size, size)], sems.at[k % 2, i])
            for i, name in enumerate(names)
        ]

    for k in range(len(plan)):

        @pl.when(pl.program_id(0) == k)
        def _(k=k):
            if k == 0:
                for copy in copies(0):
                    copy.start()
            if k + 1 < len(plan):
                for copy in copies(k + 1):
                    copy.start()
            for copy in copies(k):
                copy.wait()

    return keep[pl.program_id(0) % 2]


def rows_kernel(count, plan, taken, table, *refs):
    total = sum(len(names) for names in plan)
    x_refs = refs[:total]
    (
        vectors,
        weight,
        up_weight,
        keep,
        ahead,
        behind,
        mix_high,
        mix_low,
    ) = refs[total : total + 8]
    (
        mark,
        norm_one,
        norm_two,
        unit_out,
        feat_out,
        value_out,
        active_out,
        slope_out,
        block,
        sems,
    ) = refs[total + 8 + taken :]
    mark[...] = jnp.zeros_like(mark)
    x = load_block(plan, x_refs, block, sems).astype(F32)
    mean = jnp.mean(x, axis=-1, keepdims=True)
    centred = x - mean
    scale = lax.rsqrt(jnp.mean(centred * centred, axis=-1, keepdims=True) + EPS)
    unit = centred * scale
    row = vectors[...].astype(F32)
    one = (unit * row[0:1] + row[1:2]).astype(BF16)
    two = (unit * row[2:3] + row[3:4]).astype(BF16)
    norm_one[...] = one
    norm_two[...] = two
    unit_out[...] = unit.astype(BF16)

    projected = dot(one, weight[...]) + row[4:5, : weight.shape[1]]
    value_out[...] = head_columns(projected, 2, count).astype(BF16)
    pairs = [head_columns(projected, which, count) for which in (0, 1)]
    if count == 1:
        pairs = [jnp.concatenate(pairs, axis=1)]
    for k, pair in enumerate(pairs):
        turned = turn(pair, keep[...], ahead[...], behind[...], 1.0)
        feat = jnp.exp(mixed_dot(turned, mix_high[...], mix_low[...]))
        feat_out[:, k * LANES : (k + 1) * LANES] = feat

    hidden = dot(two, up_weight[...]) + row[5:6, : up_weight.shape[1]]
    normal = 0.5 * (1.0 + lax.erf(hidden * 0.7071067811865476))
    density = jnp.exp(-0.5 * hidden * hidden) * 0.3989422804014327
    active_out[...] = (hidden * normal).astype(BF16)
    slope_out[...] = (normal + hidden * density).astype(BF16)


def allowed_pairs(docs_col, docs_row, count):
    size = docs_col.shape[0]
    rows = lax.broadcasted_iota(jnp.int32, (size, size), 0)
    cols = lax.broadcasted_iota(jnp.int32, (size, size), 1)
    allowed = ((docs_col == docs_row) & (rows >= cols)).astype(F32)
    return allowed if count == 1 else jnp.concatenate([allowed] * count, axis=0)


def forward_kernel(
    count,
    table,
    docs,
    feat_ref,
    value_ref,
    docs_col,
    docs_row,
    mark,
    mixed_out,
    merged_out,
    inverse_out,
    states_out,
    state,
):
    step = pl.program_id(0)
    width = count * HEAD_DIM
    rows = feat_ref.shape[0]

    @pl.when(step == 0)
    def _():
        state[...] = jnp.zeros_like(state)

    start = step * rows
    before = jnp.where(start > 0, docs[jnp.maximum(start - 1, 0)], -1)
    last = docs[start + rows - 1]
    kept = (last == before).astype(F32)
    allowed = allowed_pairs(docs_col[...], docs_row[0], count)
    carried = docs_col[...] == before
    chosen = docs_col[...] == last
    query = feat_ref[:, :width].astype(BF16)
    key = feat_ref[:, width:]
    value = value_ref[...]
    both = jnp.concatenate([value, jnp.ones_like(value)], axis=1)
    memory = state[...]
    states_out[0] = memory
    high, low = halves(memory)
    weights = (dot(masked_stack(query, count), key.astype(BF16), NT) * allowed).astype(BF16)
    sums = dot(side_by_side(weights, count), masked_stack(both, count)) + jnp.where(
        carried, dot(query, high) + dot(query, low), 0.0
    )
    inverse = 1.0 / sums[:, width:]
    mixed = sums[:, :width] * inverse
    mixed_out[...] = mixed
    merged_out[...] = mixed.astype(BF16)
    inverse_out[...] = inverse
    picked = jnp.where(chosen, key, 0.0).astype(BF16)
    added = dot(picked, both, TN)
    state[...] = kept * memory + jnp.where(own_block(added.shape), added, 0.0)


def pair_grads(grad, inverse, mixed):
    part = (grad * inverse).astype(BF16)
    high, low = halves(-(part.astype(F32) * mixed))
    return part, high, low


def backward_kernel(
    count,
    table,
    docs,
    feat_ref,
    value_ref,
    mixed_ref,
    inverse_ref,
    grad_ref,
    docs_col,
    docs_row,
    mark,
    states_ref,
    keep,
    ahead,
    behind,
    turned_high,
    turned_low,
    out,
    later,
):
    blocks = pl.num_programs(0)
    step = blocks - 1 - pl.program_id(0)
    width = count * HEAD_DIM
    rows = feat_ref.shape[0]

    @pl.when(pl.program_id(0) == 0)
    def _():
        later[...] = jnp.zeros_like(later)

    start = step * rows
    total = docs.shape[0]
    before = jnp.where(start > 0, docs[jnp.maximum(start - 1, 0)], -1)
    after_doc = jnp.where(start + rows < total, docs[jnp.minimum(start + rows, total - 1)], -1)
    first = docs[start]
    kept = (first == after_doc).astype(F32)
    allowed = allowed_pairs(docs_col[...], docs_row[0], count)
    carried = docs_col[...] == before
    linked = docs_col[...] == after_doc
    chosen = docs_col[...] == first
    feat = feat_ref[...]
    query, key = feat[:, :width].astype(BF16), feat[:, width:].astype(BF16)
    value = value_ref[...]
    ones = jnp.ones_like(value)
    both = jnp.concatenate([value, ones], axis=1)
    part, high, low = pair_grads(grad_ref[...], inverse_ref[...], mixed_ref[...])
    first_two = jnp.concatenate([part, high], axis=1)
    queries = masked_stack(query, count)
    weights = (dot(queries, key, NT) * allowed).astype(BF16)
    weight_grad = dot(masked_stack(first_two, count), both, NT)
    weight_grad += dot(masked_stack(low, count), ones, NT)
    weight_grad = (weight_grad * allowed).astype(BF16)
    mem_high, mem_low = halves(states_ref[0])
    late = later[...]
    late_high, late_low = halves(late)
    query_grad = dot(side_by_side(weight_grad, count), masked_stack(key, count)) + jnp.where(
        carried,
        dot(first_two, mem_high, NT) + dot(first_two, mem_low, NT) + dot(low, mem_high[:, width:], NT),
        0.0,
    )
    key_grad = dot(weight_grad, queries, TN) + jnp.where(
        linked, dot(both, late_high, NT) + dot(both, late_low, NT), 0.0
    )
    value_grad = dot(weights, masked_stack(part, count), TN) + jnp.where(
        linked, dot(key, late_high[:, :width]) + dot(key, late_low[:, :width]), 0.0
    )
    picked = jnp.where(chosen, query.astype(F32), 0.0).astype(BF16)
    added = jnp.concatenate(
        [dot(picked, part, TN), dot(picked, high, TN) + dot(picked, low, TN)], axis=1
    )
    later[...] = kept * late + jnp.where(own_block(late.shape), added, 0.0)
    inner = jnp.concatenate([query_grad, key_grad], axis=1) * feat
    pairs = []
    for base in range(0, 2 * width, LANES):
        pair = mixed_dot(inner[:, base : base + LANES], turned_high[...], turned_low[...])
        pairs.append(turn(pair, keep[...], ahead[...], behind[...], -1.0))
    flat = pairs[0] if count == 1 else jnp.concatenate(pairs, axis=1)
    pieces = []
    for j in range(count):
        lanes = slice(j * HEAD_DIM, (j + 1) * HEAD_DIM)
        pieces += [flat[:, :width][:, lanes], flat[:, width:][:, lanes], value_grad[:, lanes]]
    out[...] = jnp.concatenate(pieces, axis=1).astype(BF16)


def write_block(outs, values):
    steps = len(outs) - 1
    for k in range(steps - 1):

        @pl.when(pl.program_id(0) == k)
        def _(out=outs[k]):
            out[...] = values

    @pl.when(pl.program_id(0) == steps - 1)
    def _():
        half = outs[-1].shape[0]
        outs[-2][...] = values[:half]
        outs[-1][...] = values[half:]


def out_kernel(merged, active, dense, down, *outs):
    total = dot(active[...], down[...]) + dot(merged[...], dense[...])
    write_block(outs, total.astype(BF16))


def grads_kernel(plan, taken, *refs):
    total = sum(len(names) for names in plan)
    dense, down, slope = refs[total : total + 3]
    mark, grad_out, merged_out, hidden_out, block, sems = refs[total + 3 + taken :]
    mark[...] = jnp.zeros_like(mark)
    grad = load_block(plan, refs[:total], block, sems)
    grad_out[...] = grad
    merged_out[...] = dot(grad, dense[...], NT)
    hidden_out[...] = (dot(grad, down[...], NT) * slope[...].astype(F32)).astype(BF16)


def norm_grad_kernel(
    change, hidden, qkv_weight, up_weight, unit_ref, vectors, own_grad, given, sums_out, *outs
):
    down = lambda values: jnp.sum(values, axis=0, keepdims=True)

    @pl.when(pl.program_id(0) == 0)
    def _():
        sums_out[...] = given[...]
        sums_out[4:5] = down(own_grad[...].astype(F32))

    unit = unit_ref[...].astype(F32)
    one = dot(change[...], qkv_weight[...], NT)
    sums_out[0:1] += down(one * unit)
    sums_out[1:2] += down(one)
    two = dot(hidden[...], up_weight[...], NT)
    sums_out[2:3] += down(two * unit)
    sums_out[3:4] += down(two)
    row = vectors[...].astype(F32)
    values = (one * row[0:1] + two * row[2:3]).astype(BF16)
    if outs[0].shape[0] < values.shape[0]:
        half = outs[0].shape[0]
        outs[0][...] = values[:half]
        outs[1][...] = values[half:]
        return
    for k, out in enumerate(outs):

        @pl.when(pl.program_id(0) == k)
        def _(out=out):
            out[...] = values


def first_add_kernel(right_block, right_half, left_block, left_half, right_out, left_out):
    half = right_half.shape[0]
    join = lambda a, b: (a.astype(F32) + b.astype(F32)).astype(BF16)
    right_out[:half] = join(right_block[:half], right_half[...])
    right_out[half:] = right_block[half:]
    left_out[:half] = left_block[:half]
    left_out[half:] = join(left_block[half:], left_half[...])


def next_add_kernel(right_block, right_sum, left_block, left_sum, right_out, left_out):
    join = lambda a, b: (a.astype(F32) + b.astype(F32)).astype(BF16)
    right_out[...] = join(right_block[...], right_sum[...])
    left_out[...] = join(left_block[...], left_sum[...])


def bias_rows(values, cols):
    tile = jnp.zeros((16, values.shape[1]), F32)
    row = lax.broadcasted_iota(jnp.int32, tile.shape, 0)
    high = values.astype(BF16).astype(F32)
    tile = jnp.where(row == 0, high, jnp.where(row == 1, values - high, tile)).astype(BF16)
    if values.shape[1] == cols:
        return tile
    return jnp.concatenate([tile, jnp.zeros((16, cols - values.shape[1]), BF16)], axis=1)


def hidden_weights_kernel(table, active, hidden_grad, grad, norm_two, kept, sent, up, down):
    part = table[0]
    step = active.shape[1] // QUARTERS
    up[...] = dot(hidden_grad[...], norm_two[...], TN).astype(BF16)
    down[...] = dot(active[...], grad[...], TN).astype(BF16)
    for k in range(QUARTERS):
        out = (kept, sent)[k % 2].at[k // 2]
        begin = pl.multiple_of((part ^ k) * step, step)
        out[:step] = up[pl.ds(begin, step)]
        out[step:] = down[pl.ds(begin, step)]


def qkv_weights_kernel(table, change, norm_one, merged, grad, hidden_sums, kept, sent):
    rows, cols = norm_one.shape[1], change.shape[1]
    small, wide = merged.shape[1], kept.shape[2]
    place = pl.program_id(0)
    weight = dot(norm_one[...], change[...], TN).astype(BF16)
    dense = dot(merged[...], grad[...], TN).astype(BF16)
    first = bias_rows(jnp.sum(change[...].astype(F32), axis=0, keepdims=True), wide)
    second = hidden_sums[0].astype(F32)
    if second.shape[1] < wide:
        rest = jnp.zeros((1, wide - second.shape[1]), F32)
        second = jnp.concatenate([second, rest], axis=1)
    high = second.astype(BF16).astype(F32)
    row = lax.broadcasted_iota(jnp.int32, (16, wide), 0)
    tail = jnp.where(row == 2, high, jnp.where(row == 3, second - high, first.astype(F32)))

    def write(out):
        if wide > min(rows, cols):
            out[0] = jnp.zeros((rows + small + 16, wide), BF16)
        out[0, :rows, :cols] = weight
        out[0, rows : rows + small, :rows] = dense
        out[0, rows + small :] = tail.astype(BF16)

    @pl.when(place % 2 == 0)
    def _():
        write(kept)

    @pl.when(place % 2 == 1)
    def _():
        write(sent)


def column_sums_kernel(values, out):
    out[...] = jnp.zeros_like(out)
    out[0:1] = jnp.sum(values[...].astype(F32), axis=0, keepdims=True)


def finish_hidden_kernel(table, mine, near, third, last, up_grad, down_grad, turned):
    part = table[0]
    step = down_grad.shape[0] // QUARTERS
    for k, ref in enumerate((mine, near, third, last)):
        begin = pl.multiple_of((part ^ k) * step, step)
        turned[pl.ds(begin, step)] = ref[:step].astype(F32)
        down_grad[pl.ds(begin, step)] = ref[step:].astype(F32)
    up_grad[...] = turned[...].T


def finish_qkv_kernel(table, mine, near, third, last, weight_grad, dense_grad, bias_grad, up_bias):
    part = table[0]
    step = weight_grad.shape[0] // QUARTERS
    small, cols = dense_grad.shape[0], weight_grad.shape[1]
    hidden = up_bias.shape[2]
    for k, ref in enumerate((mine, near, third, last)):
        begin = pl.multiple_of((part ^ k) * step, step)
        weight_grad[pl.ds(begin, step)] = ref[:step, :cols].astype(F32)
        dense_grad[:, pl.ds(begin, step)] = ref[step : step + small, :step].astype(F32)
        tail = ref[step + small :].astype(F32)
        up_bias[part ^ k] = tail[2:3, :hidden] + tail[3:4, :hidden]
    tail = mine[step + small :].astype(F32)
    bias_grad[...] = tail[0:1, :cols] + tail[1:2, :cols]


def finish_out_kernel(x_ref, bias, *refs):
    parts, out = refs[:-1], refs[-1]
    total = x_ref[...].astype(F32) + bias[6:7].astype(F32)
    for ref in parts:
        total += ref[...].astype(F32)
    out[...] = total.astype(BF16)


def finish_in_kernel(x_ref, grad_ref, *refs):
    parts, out = refs[:-1], refs[-1]
    x = x_ref[...].astype(F32)
    mean = jnp.mean(x, axis=-1, keepdims=True)
    centred = x - mean
    scale = lax.rsqrt(jnp.mean(centred * centred, axis=-1, keepdims=True) + EPS)
    unit = centred * scale
    total = parts[0][...].astype(F32)
    for ref in parts[1:]:
        total += ref[...].astype(F32)
    along = jnp.mean(total * unit, axis=-1, keepdims=True)
    out[...] = grad_ref[...].astype(F32) + scale * (
        total - jnp.mean(total, axis=-1, keepdims=True) - unit * along
    )


def params(limit=12):
    return pltpu.CompilerParams(
        dimension_semantics=("arbitrary",), vmem_limit_bytes=limit * 1024 * 1024
    )


def after(value, *others):
    return lax.optimization_barrier((value,) + others)[0]


def apart(dims, kind):
    return pltpu.HBM(dims, kind)


def shape(dims, kind):
    return jax.ShapeDtypeStruct(dims, kind)


def cost(flops, nbytes, trans=0):
    return pl.CostEstimate(flops=1000, bytes_accessed=1000, transcendentals=0)


def on_device(
    dp_size,
    tensor_size,
    inputs,
    qkv_weight,
    qkv_bias,
    dense_weight,
    up_weight,
    up_bias,
    down_weight,
    out_bias,
    gain_one,
    shift_one,
    gain_two,
    shift_two,
    feature_omega,
    doc_ids,
    out_grad,
):
    rows, model = inputs.shape
    blocks = tensor_size
    middle = blocks // 2
    tokens = rows * blocks
    qkv_cols = qkv_weight.shape[1]
    count = qkv_cols // (3 * HEAD_DIM)
    width = count * HEAD_DIM
    hidden_cols = up_weight.shape[1]
    hidden_part, model_part = hidden_cols // QUARTERS, model // QUARTERS
    part = lax.axis_index("dp") % QUARTERS
    place = lax.axis_index("tensor")

    ring = list(range(0, blocks, 2)) + list(range(blocks - 1, 0, -2))
    spots = np.argsort(np.array(ring))
    offsets = [0] + [o for s in range(1, middle) for o in (s, blocks - s)] + [middle]
    where = np.argsort(np.array(offsets))
    spot = jnp.where(place % 2 == 0, place // 2, blocks - 1 - place // 2)
    around = (spot + jnp.asarray(offsets, jnp.int32)) % blocks
    sequence_of = jnp.where(around < middle, 2 * around, 2 * (blocks - 1 - around) + 1)
    away = (jnp.asarray(spots, jnp.int32) - spot) % blocks
    slot_of = jnp.where(
        away == 0,
        0,
        jnp.where(
            away < middle,
            2 * away - 1,
            jnp.where(away == middle, blocks - 1, 2 * (blocks - away)),
        ),
    )
    table = jnp.concatenate([part[None], sequence_of, slot_of]).astype(jnp.int32)

    def right(values):
        pairs = [(ring[i], ring[(i + 1) % blocks]) for i in range(blocks)]
        return lax.ppermute(values, "tensor", pairs)

    def left(values):
        pairs = [(ring[i], ring[(i - 1) % blocks]) for i in range(blocks)]
        return lax.ppermute(values, "tensor", pairs)

    def over_dp(values, bits):
        return lax.ppermute(values, "dp", [(p, p ^ bits) for p in range(dp_size)])

    def over_tensor(values, bits):
        return lax.ppermute(values, "tensor", [(t, t ^ bits) for t in range(tensor_size)])

    line, due = [], [()]

    def run(step, *operands, gate=0, wait=()):
        operands = list(operands)
        held = tuple(line[-1:]) + due[0] + tuple(wait)
        if held:
            operands[gate] = after(operands[gate], *held)
        result = step(*operands)
        line.append(result[0] if isinstance(result, (tuple, list)) else result)
        return result

    def tick(*arrived):
        due[0] = tuple(arrived) + tuple(line[-1:])

    def now(values):
        return after(values, *due[0])

    plain = lambda cols: pl.BlockSpec((rows, cols), lambda k, *s: (k, 0))
    whole = lambda *dims: pl.BlockSpec(dims, lambda k, *s: (0,) * len(dims))
    spec = lambda values: whole(*values.shape)
    anywhere = pl.BlockSpec(memory_space=pltpu.HBM)

    def call(
        kernel, name, outs, in_specs, out_specs, prefetch=1, scratch=(), steps=blocks, aliases=None, limit=12
    ):
        return pl.pallas_call(
            kernel,
            out_shape=outs,
            grid_spec=pltpu.PrefetchScalarGridSpec(
                num_scalar_prefetch=prefetch,
                grid=(steps,),
                in_specs=in_specs,
                out_specs=out_specs,
                scratch_shapes=list(scratch),
            ),
            input_output_aliases=aliases or {},
            compiler_params=params(limit),
            cost_estimate=cost(0, 0),
            name=name,
        )

    def once(kernel, name, outs, prefetch=1, scratch=(), limit=12):
        single = not isinstance(outs, (tuple, list))
        listed = (outs,) if single else tuple(outs)

        def step(*operands):
            result = call(
                kernel,
                name,
                listed,
                [spec(v) for v in operands[prefetch:]],
                [whole(*v.shape) for v in listed],
                prefetch,
                scratch,
                1,
                limit=limit,
            )(*operands)
            return result[0] if single else result

        return step

    docs = doc_ids.reshape(-1)
    docs_col = docs.reshape(-1, 1)
    docs_row = docs.reshape(blocks, 1, rows)
    line_of = lambda v: jnp.pad(v, (0, model - v.shape[0]))
    vectors = jnp.concatenate(
        [gain_one, shift_one, gain_two, shift_two, line_of(qkv_bias), line_of(up_bias), out_bias]
        + [jnp.zeros((model,), BF16)]
    ).reshape(8, model)
    lane = np.arange(LANES) % HEAD_DIM
    rates = np.where(lane < ROT, 10000.0 ** (-(lane % (ROT // 2)) * 2.0 / ROT), 0.0)
    rates = jnp.asarray(rates[None, :], F32)

    square = whole(LANES, LANES)
    marks = []

    def group_call(kernel, name, group, extra, extra_specs, outs, out_specs, before, prefetch):
        plan, arrays = [], []
        for parts in group:
            plan.append(tuple(range(len(arrays), len(arrays) + len(parts))))
            arrays += list(parts)
        passed = tuple(before) + tuple(marks[-1:])
        operands = ((table,) if prefetch else ()) + tuple(arrays) + tuple(extra)
        aliases = {len(operands) + i: i + 1 for i in range(len(before))}
        result = run(
            call(
                functools.partial(kernel, tuple(plan), len(passed)),
                name,
                (shape((8, LANES), F32),) + outs,
                [anywhere] * len(arrays) + extra_specs + [anywhere] * len(passed),
                [whole(8, LANES)] + out_specs,
                prefetch=prefetch,
                scratch=[pltpu.VMEM((2, rows, model), BF16), pltpu.SemaphoreType.DMA((2, 2))],
                steps=len(group),
                aliases=aliases,
            ),
            *operands,
            *passed,
            gate=prefetch,
        )
        marks.append(result[0])
        return result[1:]

    class RingGather:
        def __init__(self, block):
            self.ahead = self.back = self.own = block
            self.distance = 0

        def start(self):
            self.distance += 1
            if self.distance < middle:
                self.ahead, self.back = left(now(self.ahead)), right(now(self.back))
                self.group = ((self.ahead,), (self.back,))
                self.moving = (self.ahead, self.back)
            else:
                cut = rows // 2
                self.moving = (right(now(self.back[:cut])), left(now(self.ahead[cut:])))
                self.group = (self.moving,)
            if self.distance == 1:
                self.group = ((self.own,),) + self.group
            return self.moving

    row_state = ()
    row_base = 0

    def row_step(group):
        nonlocal row_state, row_base
        base = row_base
        at = lambda cols: pl.BlockSpec((rows, cols), lambda k, *s: (base + k, 0))
        turned_at = pl.BlockSpec((rows, LANES), lambda k, table: (table[1 + base + k], 0))
        row_state = group_call(
            functools.partial(rows_kernel, count),
            "rows",
            group,
            (
                vectors,
                qkv_weight,
                up_weight,
                keep,
                ahead,
                behind,
                mix_high,
                mix_low,
            ),
            [
                whole(8, model),
                whole(model, qkv_cols),
                whole(model, hidden_cols),
                turned_at,
                turned_at,
                turned_at,
                square,
                square,
            ],
            (
                apart((tokens, model), BF16),
                apart((tokens, model), BF16),
                apart((tokens, model), BF16),
                apart((tokens, 2 * width), F32),
                apart((tokens, width), BF16),
                apart((tokens, hidden_cols), BF16),
                apart((tokens, hidden_cols), BF16),
            ),
            [
                at(model),
                at(model),
                at(model),
                at(2 * width),
                at(width),
                at(hidden_cols),
                at(hidden_cols),
            ],
            row_state,
            1,
        )
        row_base += len(group)

    class RingSum:
        def __init__(self, parts):
            self.parts = parts
            self.distance = middle
            self.sums = parts[-2], parts[-1]

        def term(self, offset):
            return self.parts[int(where[offset % blocks])]

        def start(self):
            self.distance -= 1
            self.sums = right(now(self.sums[0])), left(now(self.sums[1]))
            return self.sums

        def add(self):
            first = self.distance == middle - 1
            self.sums = run(
                once(
                    first_add_kernel if first else next_add_kernel,
                    "ring_add",
                    (shape((rows, model), BF16),) * 2,
                    prefetch=0,
                ),
                self.term(self.distance),
                self.sums[0],
                self.term(-self.distance),
                self.sums[1],
            )

        def result(self):
            return (self.parts[0],) + tuple(self.sums)

    class WeightSum:
        def __init__(self, kept, sent):
            self.kept, self.sent = kept, sent
            self.stage = 0

        def start(self, third=False, near=False, last=False):
            if third:
                self.third = over_dp(now(self.mine), 2)
                return (self.third,)
            if near:
                self.near = over_dp(now(self.mine), 1)
                return (self.near,)
            if last:
                self.last = over_dp(now(self.third), 1)
                return (self.last,)
            self.stage += 1
            self.moving = (over_dp(now(self.sent if self.stage == 1 else self.next), self.stage),)
            return self.moving

        def add(self):
            if self.stage == 1:
                self.first = self.moving[0]
                self.next = run(add, self.kept[1], self.first[1])
            else:
                self.mine = rest(run(add_three, self.kept[0], self.first[0], self.moving[0]))

        def result(self):
            return self.mine, self.near, self.third, self.last

    def finish(ring):
        while ring.distance > 0:
            ring.add()
            tick()
            tick(*ring.start())

    class SmallSum:
        def __init__(self, values):
            self.values = values
            self.steps = [("dp", 1 << k) for k in range(dp_size.bit_length() - 1)]
            self.steps += [("tensor", 1 << k) for k in range(tensor_size.bit_length() - 1)]

        def start(self):
            axis, bits = self.steps.pop(0)
            self.moving = ((over_dp if axis == "dp" else over_tensor)(now(self.values), bits),)
            return self.moving

        def add(self):
            self.values = run(lambda a, b: a + b, self.values, self.moving[0])

    x_ring = RingGather(inputs)
    going = x_ring.start()
    keep, ahead, behind, mix_high, mix_low, turned_high, turned_low = run(
        call(
            prepare_kernel,
            "prepare",
            (shape((tokens, LANES), F32),) * 3 + (shape((LANES, LANES), BF16),) * 4,
            [whole(1, LANES), whole(HEAD_DIM, HEAD_DIM), anywhere],
            [plain(LANES)] * 3 + [square] * 4,
            prefetch=0,
        ),
        rates,
        feature_omega,
        docs_col,
        wait=(vectors, docs_row),
    )

    pending = x_ring.group
    tick(*going)
    for _ in range(1, middle - 1):
        going = x_ring.start()
        row_step(pending)
        pending = x_ring.group
        tick(*going)
    g_ring = RingGather(out_grad)
    going = x_ring.start() + g_ring.start()
    row_step(pending)
    pending, grad_pending = x_ring.group, g_ring.group
    tick(*going)
    going = g_ring.start()
    row_step(pending)
    norm_one, norm_two, unit, feat, value, active, slope = row_state
    flow = lambda cols: pl.BlockSpec((rows, cols), lambda m, table, docs: (table[1 + blocks + m], 0))
    straight = lambda cols: pl.BlockSpec((rows, cols), lambda m, *s: (m, 0))
    wide = pltpu.VMEM((width, 2 * width), F32)
    mixed, merged, inverse, states = run(
        call(
            functools.partial(forward_kernel, count),
            "attend",
            (
                shape((tokens, width), F32),
                shape((tokens, width), BF16),
                shape((tokens, width), F32),
                shape((blocks, width, 2 * width), F32),
            ),
            [
                flow(2 * width),
                flow(width),
                straight(1),
                pl.BlockSpec((1, 1, rows), lambda m, *s: (m, 0, 0)),
                anywhere,
            ],
            [
                flow(width),
                flow(width),
                flow(width),
                pl.BlockSpec((1, width, 2 * width), lambda m, *s: (m, 0, 0)),
            ],
            prefetch=2,
            scratch=[wide],
        ),
        table,
        docs,
        feat,
        value,
        docs_col,
        docs_row,
        marks[-1],
        gate=2,
    )

    grad_state = ()
    grad_base = 0

    def grad_step(group):
        nonlocal grad_state, grad_base
        at = lambda cols, base=grad_base: pl.BlockSpec((rows, cols), lambda k, *s: (base + k, 0))
        grad_state = group_call(
            grads_kernel,
            "grads",
            group,
            (dense_weight, down_weight, slope),
            [whole(width, model), whole(hidden_cols, model), at(hidden_cols)],
            (
                apart((tokens, model), BF16),
                apart((tokens, width), F32),
                apart((tokens, hidden_cols), BF16),
            ),
            [at(model), at(width), at(hidden_cols)],
            grad_state,
            0,
        )
        grad_base += len(group)

    grad_pending = list(grad_pending)
    tick(*going)
    grad_pending += g_ring.group
    going = g_ring.start()
    halves_of = [shape((rows, model), BF16)] * (blocks - 1) + [shape((rows // 2, model), BF16)] * 2

    def out_step():
        return run(
            call(
                out_kernel,
                "out",
                tuple(halves_of),
                [
                    plain(width),
                    plain(hidden_cols),
                    whole(width, model),
                    whole(hidden_cols, model),
                ],
                [whole(*v.shape) for v in halves_of],
                prefetch=0,
            ),
            merged,
            active,
            dense_weight,
            down_weight,
        )

    partial_out = out_step()
    grad_step(grad_pending)
    tick(*going)
    while g_ring.distance < middle - 1:
        grad_pending = g_ring.group
        going = g_ring.start()
        grad_step(grad_pending)
        tick(*going)
    out_ring = RingSum(partial_out)
    grad_pending = g_ring.group
    going = g_ring.start() + out_ring.start()
    grad_step(grad_pending)
    tick(*going)
    out_ring.add()
    tick()
    going = out_ring.start()
    grad_step(g_ring.group)
    grad_all, merged_grad, hidden_grad = grad_state
    back = lambda cols: pl.BlockSpec(
        (rows, cols), lambda m, table, docs: (table[2 * blocks - m], 0)
    )
    back_straight = lambda cols: pl.BlockSpec((rows, cols), lambda m, *s: (blocks - 1 - m, 0))
    change = run(
        call(
            functools.partial(backward_kernel, count),
            "attend_back",
            shape((tokens, qkv_cols), BF16),
            [
                back(2 * width),
                back(width),
                back(width),
                back(width),
                back(width),
                back_straight(1),
                pl.BlockSpec((1, 1, rows), lambda m, *s: (blocks - 1 - m, 0, 0)),
                anywhere,
                pl.BlockSpec((1, width, 2 * width), lambda m, *s: (blocks - 1 - m, 0, 0)),
                back_straight(LANES),
                back_straight(LANES),
                back_straight(LANES),
                square,
                square,
            ],
            back(qkv_cols),
            prefetch=2,
            scratch=[wide],
        ),
        table,
        docs,
        feat,
        value,
        mixed,
        inverse,
        merged_grad,
        docs_col,
        docs_row,
        marks[-1],
        states,
        keep,
        ahead,
        behind,
        turned_high,
        turned_low,
        gate=6,
    )
    tick(*going)
    out_ring.add()
    tick()
    going = out_ring.start()
    def norm_step(start, outs, given):
        at = lambda cols: pl.BlockSpec((rows, cols), lambda k, *s: (start + k, 0))
        return run(
            call(
                norm_grad_kernel,
                "norm_grad",
                (shape((8, model), F32),) + tuple(outs),
                [
                    at(qkv_cols),
                    at(hidden_cols),
                    whole(model, qkv_cols),
                    whole(model, hidden_cols),
                    at(model),
                    whole(8, model),
                    whole(rows, model),
                    whole(8, model),
                ],
                [whole(8, model)] + [whole(*v.shape) for v in outs],
                prefetch=0,
                steps=1 if start else blocks - 1,
            ),
            change,
            hidden_grad,
            qkv_weight,
            up_weight,
            unit,
            vectors,
            out_grad,
            given,
            gate=5,
        )

    def add(a, b):
        return (a.astype(F32) + b.astype(F32)).astype(BF16)

    def add_three(a, b, c):
        return (a.astype(F32) + b.astype(F32) + c.astype(F32)).astype(BF16)

    def rest(total):
        step = QUARTERS
        while step < dp_size:
            total = add(total, over_dp(total, step))
            step *= 2
        return total

    last_sums, top, bottom = norm_step(blocks - 1, halves_of[-2:], jnp.zeros((8, model), F32))
    e_ring = RingSum((top, bottom))
    going += e_ring.start()
    norm_grads = norm_step(0, halves_of[:-2], last_sums)
    e_ring.parts = tuple(norm_grads[1:]) + (top, bottom)
    small = SmallSum(norm_grads[0])
    cut_cols = model // QUARTERS
    kept, sent = run(
        call(
            hidden_weights_kernel,
            "hidden_weights",
            (shape((2, 2 * hidden_part, model), BF16),) * 2,
            [
                whole(tokens, hidden_cols),
                whole(tokens, hidden_cols),
                pl.BlockSpec((tokens, cut_cols), lambda k, *s: (0, k)),
                pl.BlockSpec((tokens, cut_cols), lambda k, *s: (0, k)),
            ],
            [pl.BlockSpec((2, 2 * hidden_part, cut_cols), lambda k, *s: (0, 0, k))] * 2,
            scratch=[pltpu.VMEM((hidden_cols, cut_cols), BF16)] * 2,
            steps=QUARTERS,
            limit=20,
        ),
        table,
        active,
        hidden_grad,
        grad_all,
        norm_two,
        gate=2,
    )
    hidden_sums = run(
        once(column_sums_kernel, "column_sums", shape((8, hidden_cols), F32), prefetch=0), hidden_grad
    )
    lower = WeightSum(kept, sent)
    tick(*going)
    out_ring.add()
    e_ring.add()
    tick()
    going = out_ring.start() + e_ring.start() + lower.start()
    first_rows, first_cols = model_part + width + 16, max(qkv_cols, model_part)
    sums_parts = hidden_sums[0].reshape(QUARTERS, 1, hidden_part)
    upper_kept, upper_sent = run(
        call(
            qkv_weights_kernel,
            "qkv_weights",
            (shape((2, first_rows, first_cols), BF16),) * 2,
            [
                whole(tokens, qkv_cols),
                pl.BlockSpec((tokens, model_part), lambda k, table: (0, table[0] ^ k)),
                whole(tokens, width),
                pl.BlockSpec((tokens, model_part), lambda k, table: (0, table[0] ^ k)),
                pl.BlockSpec((1, 1, hidden_part), lambda k, table: (table[0] ^ k, 0, 0)),
            ],
            [pl.BlockSpec((1, first_rows, first_cols), lambda k, table: (k // 2, 0, 0))] * 2,
            steps=QUARTERS,
            limit=16,
        ),
        table,
        change,
        norm_one,
        merged,
        grad_all,
        sums_parts,
        gate=2,
    )
    upper = WeightSum(upper_kept, upper_sent)
    tick(*going)
    if out_ring.distance > 0:
        finish(out_ring)
    e_ring.add()
    lower.add()
    tick()
    going = e_ring.start() + upper.start() + lower.start() + small.start()
    layer_out = run(
        once(finish_out_kernel, "finish_out", shape((rows, model), BF16), prefetch=0),
        inputs,
        vectors,
        *out_ring.result(),
        gate=2,
    )
    tick(*going)
    e_ring.add()
    upper.add()
    lower.add()
    small.add()
    tick()
    going = e_ring.start() + upper.start() + lower.start(third=True) + small.start()
    tick(*going)
    upper.add()
    small.add()
    finish(e_ring)
    tick()
    going = upper.start(third=True) + lower.start(last=True) + lower.start(near=True)
    going += upper.start(near=True) + small.start()
    input_grad = run(
        once(finish_in_kernel, "finish_in", shape((rows, model), F32), prefetch=0),
        inputs,
        out_grad,
        *e_ring.result(),
        gate=2,
    )

    tick(*going)
    small.add()
    tick()
    going = upper.start(last=True) + small.start()
    up_grad, down_grad = run(
        once(
            finish_hidden_kernel,
            "finish_hidden",
            (shape((model, hidden_cols), F32), shape((hidden_cols, model), F32)),
            scratch=[pltpu.VMEM((hidden_cols, model), F32)],
            limit=16,
        ),
        table,
        *lower.result(),
        gate=1,
    )
    tick(*going)
    small.add()
    tick()
    small.start()
    qkv_grad, dense_grad, qkv_bias_grad, up_bias_grad = run(
        once(
            finish_qkv_kernel,
            "finish_qkv",
            (
                shape((model, qkv_cols), F32),
                shape((width, model), F32),
                shape((1, qkv_cols), F32),
                shape((QUARTERS, 1, hidden_part), F32),
            ),
        ),
        table,
        *upper.result(),
        gate=1,
    )

    small.add()
    while small.steps:
        tick()
        small.start()
        small.add()
    cols = model // tensor_size
    small = lax.dynamic_slice_in_dim(small.values, place * cols, cols, 1)

    return (
        layer_out,
        input_grad,
        qkv_grad,
        qkv_bias_grad.reshape(-1),
        dense_grad,
        up_grad,
        up_bias_grad.reshape(-1),
        down_grad,
        small[4],
        small[0],
        small[1],
        small[2],
        small[3],
    )


def solution(mesh):
    in_specs = (
        P(("dp", "tensor"), None),
        P(None, "tensor"),
        P("tensor"),
        P("tensor", None),
        P(None, "tensor"),
        P("tensor"),
        P("tensor", None),
        P(),
        P(),
        P(),
        P(),
        P(),
        P(),
        P("dp", None),
        P(("dp", "tensor"), None),
    )
    out_specs = (
        P(("dp", "tensor"), None),
        P(("dp", "tensor"), None),
        P(None, "tensor"),
        P("tensor"),
        P("tensor", None),
        P(None, "tensor"),
        P("tensor"),
        P("tensor", None),
        P("tensor"),
        P("tensor"),
        P("tensor"),
        P("tensor"),
        P("tensor"),
    )
    return jax.shard_map(
        functools.partial(on_device, mesh.shape["dp"], mesh.shape["tensor"]),
        mesh=mesh,
        in_specs=in_specs,
        out_specs=out_specs,
        check_vma=False,
    )
```

```python
import functools

import jax
import jax.numpy as jnp
import numpy as np
from jax import lax
from jax.experimental import pallas as pl
from jax.experimental.pallas import tpu as pltpu
from jax.sharding import PartitionSpec as P

HEAD_DIM = 64
ROT = 16
LANES = 128
EPS = 1e-05
EXACT = lax.Precision.HIGHEST
F32 = jnp.float32
BF16 = jnp.bfloat16
AXES = ("dp", "tensor")
VMEM_LIMIT = 16 * 1024 * 1024
QUARTERS = 4

NN = ((1,), (0,))
NT = ((1,), (1,))
TN = ((0,), (0,))


def dot(a, b, dims=NN, precision=None):
    return lax.dot_general(a, b, (dims, ((), ())), precision=precision, preferred_element_type=F32)


def halves(values):
    high = values.astype(BF16)
    return high, (values - high.astype(F32)).astype(BF16)


def lane_of(dims):
    return lax.broadcasted_iota(jnp.int32, dims, len(dims) - 1)


def prepare_kernel(table, rates, omega, docs_col, keep, ahead, behind, mix_high, mix_low, turned_high, turned_low):
    rows = keep.shape[0]
    start = (table[1] * pl.num_programs(0) + pl.program_id(0)) * rows
    places = start + lax.broadcasted_iota(jnp.int32, (rows, LANES), 0)
    angles = places.astype(F32) * rates[...]
    inner = lane_of((rows, LANES)) % HEAD_DIM
    cosine, sine = jnp.cos(angles), jnp.sin(angles)
    half = ROT // 2
    keep[...] = jnp.where(inner < ROT, cosine, 1.0)
    ahead[...] = jnp.where(inner < half, -sine, 0.0)
    behind[...] = jnp.where((inner >= half) & (inner < ROT), sine, 0.0)

    @pl.when(pl.program_id(0) == 0)
    def _():
        extent = HEAD_DIM
        n = lax.broadcasted_iota(jnp.int32, (LANES, LANES), 0)
        k = lax.broadcasted_iota(jnp.int32, (LANES, LANES), 1)
        same = (n // extent) == (k // extent)
        n, k = (n % extent).astype(F32), (k % extent).astype(F32)
        scale = jnp.where(k == 0, float(np.sqrt(1.0 / extent)), float(np.sqrt(2.0 / extent)))
        matrix = jnp.where(same, jnp.cos(np.pi * (n + 0.5) * k / extent) * scale, 0.0)
        row = jnp.concatenate([omega[...]] * 2, axis=1)
        spread = jnp.where(same, jnp.concatenate([row] * 2, axis=0), 0.0)
        mixing = dot(matrix, spread, precision=EXACT)
        mix_high[...], mix_low[...] = halves(mixing)
        turned_high[...], turned_low[...] = halves(mixing.T)


def turn(values, keep, ahead, behind, sign):
    half = ROT // 2
    moved = (
        pltpu.roll(values, LANES - half, axis=1) * ahead + pltpu.roll(values, half, axis=1) * behind
    )
    return values * keep + sign * moved


def mixed_dot(values, high, low):
    first, second = halves(values)
    return dot(first, high) + (dot(second, high) + dot(first, low))


def head_columns(values, which, count):
    parts = [
        values[:, (3 * j + which) * HEAD_DIM : (3 * j + which + 1) * HEAD_DIM] for j in range(count)
    ]
    return parts[0] if count == 1 else jnp.concatenate(parts, axis=1)


def masked_stack(values, count):
    if count == 1:
        return values
    lane = (lane_of(values.shape) % (count * HEAD_DIM)) // HEAD_DIM
    zero = jnp.zeros_like(values)
    return jnp.concatenate([jnp.where(lane == j, values, zero) for j in range(count)], axis=0)


def side_by_side(stack, count):
    rows = stack.shape[0] // count
    if count == 1:
        return stack
    return jnp.concatenate([stack[j * rows : (j + 1) * rows] for j in range(count)], axis=1)


def own_block(dims):
    rows = lax.broadcasted_iota(jnp.int32, dims, 0) // HEAD_DIM
    return rows == (lane_of(dims) % dims[0]) // HEAD_DIM


def compress(state, count):
    width = count * HEAD_DIM
    sides = []
    for base in (0, width):
        part = state[:, base : base + HEAD_DIM]
        for j in range(1, count):
            rows = lax.broadcasted_iota(jnp.int32, part.shape, 0) // HEAD_DIM
            here = state[:, base + j * HEAD_DIM : base + (j + 1) * HEAD_DIM]
            part = jnp.where(rows == j, here, part)
        sides.append(part)
    return jnp.concatenate(sides, axis=1)


def expand(packed, count):
    values, totals = packed[:, :HEAD_DIM], packed[:, HEAD_DIM:]
    wide = jnp.concatenate([values] * count + [totals] * count, axis=1)
    return jnp.where(own_block(wide.shape), wide, 0.0)


def project(count, one, weight, bias, turns, mix_high, mix_low, chosen, feat_out, value_out, state):
    width = count * HEAD_DIM
    projected = dot(one, weight) + bias
    value = head_columns(projected, 2, count).astype(BF16)
    pairs = [head_columns(projected, which, count) for which in (0, 1)]
    if count == 1:
        pairs = [jnp.concatenate(pairs, axis=1)]
    feats = []
    for pair in pairs:
        feats.append(jnp.exp(mixed_dot(turn(pair, *turns, 1.0), mix_high, mix_low)))
    feat = feats[0] if count == 1 else jnp.concatenate(feats, axis=1)
    feat_out[...] = feat
    value_out[...] = value
    key = jnp.where(chosen, feat[:, width:], 0.0).astype(BF16)
    state[...] += dot(key, jnp.concatenate([value, jnp.ones_like(value)], axis=1), TN)


def load_block(refs, keep, sems):
    def copy(k):
        return pltpu.make_async_copy(refs[k], keep.at[k % 2], sems.at[k % 2])

    for k in range(len(refs)):

        @pl.when(pl.program_id(0) == k)
        def _(k=k):
            if k == 0:
                copy(0).start()
            if k + 1 < len(refs):
                copy(k + 1).start()
            copy(k).wait()

    return keep[pl.program_id(0) % 2]


def own_features_kernel(count, blocks, table, docs, *refs):
    x_refs = refs[:blocks]
    (
        affine,
        weight,
        bias,
        keep,
        ahead,
        behind,
        mix_high,
        mix_low,
        docs_col,
        norm_one,
        norm_two,
        unit_out,
        feat_out,
        value_out,
        state_out,
        state,
        x_keep,
        x_sems,
    ) = refs[blocks:]

    @pl.when(pl.program_id(0) == 0)
    def _():
        state[...] = jnp.zeros_like(state)

    rows = x_keep.shape[1]
    x = load_block(x_refs, x_keep, x_sems).astype(F32)
    mean = jnp.mean(x, axis=-1, keepdims=True)
    centred = x - mean
    scale = lax.rsqrt(jnp.mean(centred * centred, axis=-1, keepdims=True) + EPS)
    unit = centred * scale
    one = (unit * affine[0:1] + affine[1:2]).astype(BF16)
    norm_one[...] = one
    norm_two[...] = (unit * affine[2:3] + affine[3:4]).astype(BF16)
    unit_out[...] = unit.astype(BF16)
    chosen = docs_col[...] == docs[(table[1] + 1) * blocks * rows - 1]
    project(
        count,
        one,
        weight[...],
        bias[...].astype(F32),
        (keep[...], ahead[...], behind[...]),
        mix_high[...],
        mix_low[...],
        chosen,
        feat_out,
        value_out,
        state,
    )

    @pl.when(pl.program_id(0) == pl.num_programs(0) - 1)
    def _():
        state_out[...] = compress(state[...], count)


def far_features_kernel(
    count,
    table,
    docs,
    norm_one,
    weight,
    bias,
    keep,
    ahead,
    behind,
    mix_high,
    mix_low,
    docs_col,
    near_state,
    feat_out,
    value_out,
    state_out,
    state,
):
    @pl.when(pl.program_id(0) == 0)
    def _():
        state[...] = jnp.zeros_like(state)

    rows = norm_one.shape[0]
    chosen = docs_col[...] == docs[(table[1] + 1) * pl.num_programs(0) * rows - 1]
    project(
        count,
        norm_one[...],
        weight[...],
        bias[0:1, : weight.shape[1]].astype(F32),
        (keep[...], ahead[...], behind[...]),
        mix_high[...],
        mix_low[...],
        chosen,
        feat_out,
        value_out,
        state,
    )

    @pl.when(pl.program_id(0) == pl.num_programs(0) - 1)
    def _():
        state_out[0] = near_state[...]
        state_out[1] = compress(state[...], count)


def allowed_pairs(docs_col, docs_row, count):
    size = docs_col.shape[0]
    rows = lax.broadcasted_iota(jnp.int32, (size, size), 0)
    cols = lax.broadcasted_iota(jnp.int32, (size, size), 1)
    allowed = ((docs_col == docs_row) & (rows >= cols)).astype(F32)
    return allowed if count == 1 else jnp.concatenate([allowed] * count, axis=0)


def forward_kernel(
    count,
    table,
    docs,
    own_feat,
    far_feat,
    own_value,
    far_value,
    docs_col,
    docs_row,
    first_state,
    mixed_out,
    merged_out,
    inverse_out,
    states_out,
    state,
):
    step = pl.program_id(0)
    width = count * HEAD_DIM
    rows = own_feat.shape[0]

    @pl.when(step == 0)
    def _():
        for side in range(2):
            state[side] = expand(first_state[1 - side], count)

    start = (table[1] * pl.num_programs(0) + step) * rows
    before = jnp.where(start > 0, docs[jnp.maximum(start - 1, 0)], -1)
    last = docs[start + rows - 1]
    kept = (last == before).astype(F32)
    allowed = allowed_pairs(docs_col[...], docs_row[0], count)
    carried = docs_col[...] == before
    chosen = docs_col[...] == last
    for side in range(2):
        feat_ref, value_ref = ((own_feat, own_value), (far_feat, far_value))[side]
        query = feat_ref[:, :width].astype(BF16)
        key = feat_ref[:, width:]
        value = value_ref[...]
        both = jnp.concatenate([value, jnp.ones_like(value)], axis=1)
        memory = state[side]
        states_out[0, side] = memory
        high, low = halves(memory)
        weights = (dot(masked_stack(query, count), key.astype(BF16), NT) * allowed).astype(BF16)
        sums = dot(side_by_side(weights, count), masked_stack(both, count)) + jnp.where(
            carried, dot(query, high) + dot(query, low), 0.0
        )
        inverse = 1.0 / sums[:, width:]
        mixed = sums[:, :width] * inverse
        mixed_out[:, side * width : (side + 1) * width] = mixed
        merged_out[:, side * width : (side + 1) * width] = mixed.astype(BF16)
        inverse_out[:, side * width : (side + 1) * width] = inverse
        picked = jnp.where(chosen, key, 0.0).astype(BF16)
        added = dot(picked, both, TN)
        state[side] = kept * memory + jnp.where(own_block(added.shape), added, 0.0)


def pair_grads(grad, inverse, mixed):
    part = (grad * inverse).astype(BF16)
    high, low = halves(-(part.astype(F32) * mixed))
    return part, high, low


def later_kernel(
    count,
    table,
    docs,
    grad_ref,
    own_dense,
    far_dense,
    own_feat,
    far_feat,
    mixed_ref,
    inverse_ref,
    docs_col,
    merged_grad,
    later_out,
    later,
):
    @pl.when(pl.program_id(0) == 0)
    def _():
        later[...] = jnp.zeros_like(later)

    width = count * HEAD_DIM
    rows = own_feat.shape[0]
    chosen = docs_col[...] == docs[table[1] * pl.num_programs(0) * rows]
    for side, dense in enumerate((own_dense, far_dense)):
        span = slice(side * width, (side + 1) * width)
        grad = dot(grad_ref[...], dense[...], NT)
        merged_grad[:, span] = grad
        part, high, low = pair_grads(grad, inverse_ref[:, span], mixed_ref[:, span])
        query = (own_feat, far_feat)[side][:, :width]
        query = jnp.where(chosen, query, 0.0).astype(BF16)
        later[side, :, :width] += dot(query, part, TN)
        later[side, :, width:] += dot(query, high, TN) + dot(query, low, TN)

    @pl.when(pl.program_id(0) == pl.num_programs(0) - 1)
    def _():
        for side in range(2):
            later_out[side] = compress(later[side], count)


def backward_kernel(
    count,
    table,
    docs,
    own_feat,
    far_feat,
    own_value,
    far_value,
    mixed_ref,
    inverse_ref,
    grad_ref,
    docs_col,
    docs_row,
    states_ref,
    first_later,
    keep,
    ahead,
    behind,
    turned_high,
    turned_low,
    own_out,
    far_out,
    later,
):
    blocks = pl.num_programs(0)
    step = blocks - 1 - pl.program_id(0)
    width = count * HEAD_DIM
    rows = own_feat.shape[0]

    @pl.when(pl.program_id(0) == 0)
    def _():
        for side in range(2):
            later[side] = expand(first_later[1 - side], count)

    start = (table[1] * blocks + step) * rows
    total = docs.shape[0]
    before = jnp.where(start > 0, docs[jnp.maximum(start - 1, 0)], -1)
    after = jnp.where(start + rows < total, docs[jnp.minimum(start + rows, total - 1)], -1)
    first = docs[start]
    kept = (first == after).astype(F32)
    allowed = allowed_pairs(docs_col[...], docs_row[0], count)
    carried = docs_col[...] == before
    linked = docs_col[...] == after
    chosen = docs_col[...] == first
    for side in range(2):
        span = slice(side * width, (side + 1) * width)
        feat = (own_feat, far_feat)[side][...]
        query, key = feat[:, :width].astype(BF16), feat[:, width:].astype(BF16)
        value = (own_value, far_value)[side][...]
        ones = jnp.ones_like(value)
        both = jnp.concatenate([value, ones], axis=1)
        part, high, low = pair_grads(grad_ref[:, span], inverse_ref[:, span], mixed_ref[:, span])
        first_two = jnp.concatenate([part, high], axis=1)
        queries = masked_stack(query, count)
        weights = (dot(queries, key, NT) * allowed).astype(BF16)
        weight_grad = dot(masked_stack(first_two, count), both, NT)
        weight_grad += dot(masked_stack(low, count), ones, NT)
        weight_grad = (weight_grad * allowed).astype(BF16)
        mem_high, mem_low = halves(states_ref[0, side])
        late = later[side]
        late_high, late_low = halves(late)
        query_grad = dot(side_by_side(weight_grad, count), masked_stack(key, count)) + jnp.where(
            carried,
            dot(first_two, mem_high, NT) + dot(first_two, mem_low, NT) + dot(low, mem_high[:, width:], NT),
            0.0,
        )
        key_grad = dot(weight_grad, queries, TN) + jnp.where(
            linked, dot(both, late_high, NT) + dot(both, late_low, NT), 0.0
        )
        value_grad = dot(weights, masked_stack(part, count), TN) + jnp.where(
            linked, dot(key, late_high[:, :width]) + dot(key, late_low[:, :width]), 0.0
        )
        picked = jnp.where(chosen, query.astype(F32), 0.0).astype(BF16)
        block = own_block(late.shape)
        added = jnp.concatenate(
            [dot(picked, part, TN), dot(picked, high, TN) + dot(picked, low, TN)], axis=1
        )
        later[side] = kept * late + jnp.where(block, added, 0.0)
        inner = jnp.concatenate([query_grad, key_grad], axis=1) * feat
        pairs = []
        for base in range(0, 2 * width, LANES):
            pair = mixed_dot(inner[:, base : base + LANES], turned_high[...], turned_low[...])
            pairs.append(turn(pair, keep[...], ahead[...], behind[...], -1.0))
        flat = pairs[0] if count == 1 else jnp.concatenate(pairs, axis=1)
        pieces = []
        for j in range(count):
            lanes = slice(j * HEAD_DIM, (j + 1) * HEAD_DIM)
            pieces += [flat[:, :width][:, lanes], flat[:, width:][:, lanes], value_grad[:, lanes]]
        out = own_out if side == 0 else far_out
        out[...] = jnp.concatenate(pieces, axis=1).astype(BF16)


def up_kernel(norm_ref, weight, bias, active_out, slope_out):
    hidden = dot(norm_ref[...], weight[...], NT) + bias[...]
    normal = 0.5 * (1.0 + lax.erf(hidden * 0.7071067811865476))
    density = jnp.exp(-0.5 * hidden * hidden) * 0.3989422804014327
    active_out[...] = (hidden * normal).astype(BF16)
    slope_out[...] = (normal + hidden * density).astype(BF16)


def down_back_kernel(grad_ref, weight, slope, hidden_out, sums_out):
    hidden = (dot(grad_ref[...], weight[...], NT) * slope[...].astype(F32)).astype(BF16)
    hidden_out[...] = hidden

    @pl.when(pl.program_id(0) == 0)
    def _():
        sums_out[...] = jnp.zeros_like(sums_out)

    sums_out[0:1] += jnp.sum(hidden.astype(F32), axis=0, keepdims=True)


def out_kernel(merged, own_active, far_active, own_dense, far_dense, own_down, far_down, *outs):
    width = own_dense.shape[0]
    total = dot(own_active[...], own_down[...]) + dot(far_active[...], far_down[...])
    total += dot(merged[:, :width], own_dense[...]) + dot(merged[:, width:], far_dense[...])
    write_block(outs, total.astype(BF16))


def write_block(outs, values):
    kept, sent = outs
    for k in range(2 * kept.shape[0]):

        @pl.when(pl.program_id(0) == k)
        def _(k=k):
            (sent if k % 2 else kept)[k // 2] = values


def norm_grad_kernel(
    own_pg,
    far_pg,
    own_hg,
    far_hg,
    own_qkv,
    far_qkv,
    own_up,
    far_up,
    unit_ref,
    affine,
    grad_sums,
    sums_out,
    *outs,
):
    @pl.when(pl.program_id(0) == 0)
    def _():
        sums_out[...] = jnp.zeros_like(sums_out)
        sums_out[4:5] = grad_sums[0:1]

    down = lambda values: jnp.sum(values, axis=0, keepdims=True)
    unit = unit_ref[...].astype(F32)
    one = dot(own_pg[...], own_qkv[...], NT) + dot(far_pg[...], far_qkv[...], NT)
    sums_out[0:1] += down(one * unit)
    sums_out[1:2] += down(one)
    two = dot(own_hg[...], own_up[...]) + dot(far_hg[...], far_up[...])
    sums_out[2:3] += down(two * unit)
    sums_out[3:4] += down(two)
    write_block(outs, (one * affine[0:1] + two * affine[2:3]).astype(BF16))


def first_pack_kernel(table, weight, dense, bias, up_bias, out):
    rows, small = weight.shape[0], dense.shape[0]
    if out.shape[1] > min(weight.shape[1], dense.shape[1]):
        out[...] = jnp.zeros_like(out)
    out[:rows, : weight.shape[1]] = weight[...]
    out[rows : rows + small, : dense.shape[1]] = dense[...]
    first = bias[...].astype(F32)
    second = up_bias[table[2]].astype(F32)
    if first.shape[1] > second.shape[1]:
        rest = jnp.zeros((1, first.shape[1] - second.shape[1]), F32)
        second = jnp.concatenate([second, rest], axis=1)
    row = lax.broadcasted_iota(jnp.int32, (16, first.shape[1]), 0)
    out[rows + small :, : first.shape[1]] = jnp.where(row < 8, first, second).astype(BF16)


def arrange_kernel(table, up, down, bias, own_up, own_down, own_bias, pack, turned):
    part = table[2]
    step = down.shape[0] // QUARTERS
    turned[...] = up[...].T
    for k in range(QUARTERS):
        begin = pl.multiple_of((part ^ k) * step, step)
        own_up[k * step : (k + 1) * step] = turned[pl.ds(begin, step)]
        own_down[k * step : (k + 1) * step] = down[pl.ds(begin, step)]
    own_bias[...] = jnp.concatenate([bias[part ^ k].astype(F32) for k in range(QUARTERS)], axis=1)
    pack[:step] = own_up[:step]
    pack[step:] = own_down[:step]


def collect_first_kernel(table, mine, near, third, last, far_qkv, far_dense, far_up_bias):
    part = table[2]
    step = far_qkv.shape[0] // QUARTERS
    small = far_dense.shape[0]
    hidden = far_up_bias.shape[1] // QUARTERS
    biases = []
    for k, ref in enumerate((mine, near, third, last)):
        begin = pl.multiple_of((part ^ k) * step, step)
        far_qkv[pl.ds(begin, step)] = ref[:step, : far_qkv.shape[1]]
        far_dense[:, pl.ds(begin, step)] = ref[step : step + small, :step]
        tail = ref[step + small :].astype(F32)
        biases.append(tail[8:9, :hidden])
    far_up_bias[...] = jnp.concatenate(biases, axis=1)


def collect_second_kernel(mine, near, third, last, far_up, far_down):
    step = mine.shape[0] // 2
    for k, ref in enumerate((mine, near, third, last)):
        far_up[k * step : (k + 1) * step] = ref[:step]
        far_down[k * step : (k + 1) * step] = ref[step:]


def collect_grad_kernel(*refs):
    blocks, (whole, sums) = refs[:-2], refs[-2:]
    rows = blocks[0].shape[0]
    for k, ref in enumerate(blocks):
        whole[k * rows : (k + 1) * rows] = ref[...]
    sums[...] = jnp.zeros_like(sums)
    sums[0:1] = jnp.sum(blocks[0][...].astype(F32), axis=0, keepdims=True)


def bias_rows(values, cols):
    tile = jnp.zeros((16, values.shape[1]), F32)
    row = lax.broadcasted_iota(jnp.int32, tile.shape, 0)
    high = values.astype(BF16).astype(F32)
    tile = jnp.where(row == 0, high, jnp.where(row == 1, values - high, tile)).astype(BF16)
    if values.shape[1] == cols:
        return tile
    return jnp.concatenate([tile, jnp.zeros((16, cols - values.shape[1]), BF16)], axis=1)


def hidden_weights_kernel(
    table, active, hidden_grad, merged, grad, norm_two, hidden_sums, kept, sent, dense
):
    part = table[2]
    step, small = active.shape[1] // QUARTERS, merged.shape[1] // QUARTERS
    cols = kept.shape[2]
    dense[...] = dot(merged[...], grad[...], TN).astype(BF16)
    down = dot(active[...], grad[...], TN).astype(BF16)
    up = dot(hidden_grad[...], norm_two[...], TN).astype(BF16)
    for k in range(QUARTERS):
        out = (kept, sent)[k % 2].at[k // 2]
        span = slice(k * step, (k + 1) * step)
        out[:step] = up[span]
        out[step : 2 * step] = down[span]
        begin = pl.multiple_of((part ^ k) * small, small)
        out[2 * step : 2 * step + small] = dense[pl.ds(begin, small)]
        out[2 * step + small :] = bias_rows(hidden_sums[0:1, span], cols)


def qkv_weights_kernel(table, own_pg, far_pg, norm_one, kept, sent, full):
    part = table[2]
    cols = kept.shape[2]
    step = full.shape[0] // QUARTERS
    for side, grad in enumerate((own_pg, far_pg)):
        full[...] = dot(norm_one[...], grad[...], TN).astype(BF16)
        tail = bias_rows(jnp.sum(grad[...].astype(F32), axis=0, keepdims=True), cols)
        for k in range(QUARTERS):
            out = (kept, sent)[k % 2].at[2 * (k // 2) + side]
            begin = pl.multiple_of((part ^ k) * step, step)
            out[:step] = full[pl.ds(begin, step)]
            out[step:] = tail


def finish_hidden_kernel(
    table, mine, near, third, last, up_grad, down_grad, dense_grad, bias_grad, turned
):
    part = table[2]
    step, small = down_grad.shape[0] // QUARTERS, dense_grad.shape[0] // QUARTERS
    size = mine.shape[0]
    for k, ref in enumerate((mine, near, third, last)):
        begin = pl.multiple_of((part ^ k) * step, step)
        turned[pl.ds(begin, step)] = ref[:step].astype(F32)
        down_grad[pl.ds(begin, step)] = ref[step : 2 * step].astype(F32)
        begin = pl.multiple_of((part ^ k) * small, small)
        dense_grad[pl.ds(begin, small)] = ref[2 * step : 2 * step + small].astype(F32)
        tail = ref[2 * step + small : size].astype(F32)
        bias_grad[part ^ k] = tail[0:1, :step] + tail[1:2, :step]
    up_grad[...] = turned[...].T


def finish_qkv_kernel(table, mine, near, third, last, weight_grad, bias_grad):
    part = table[2]
    step = weight_grad.shape[0] // QUARTERS
    for k, ref in enumerate((mine, near, third, last)):
        begin = pl.multiple_of((part ^ k) * step, step)
        weight_grad[pl.ds(begin, step)] = ref[:step].astype(F32)
    tail = mine[step:].astype(F32)
    bias_grad[...] = tail[0:1] + tail[1:2]


def finish_out_kernel(x_ref, bias, *refs):
    parts, out = refs[:-1], refs[-1]
    total = x_ref[...].astype(F32) + bias[...].astype(F32)
    for ref in parts:
        total += ref[...].astype(F32)
    out[...] = total.astype(BF16)


def finish_in_kernel(x_ref, grad_ref, *refs):
    parts, out = refs[:-1], refs[-1]
    x = x_ref[...].astype(F32)
    mean = jnp.mean(x, axis=-1, keepdims=True)
    centred = x - mean
    scale = lax.rsqrt(jnp.mean(centred * centred, axis=-1, keepdims=True) + EPS)
    unit = centred * scale
    total = parts[0][...].astype(F32)
    for ref in parts[1:]:
        total += ref[...].astype(F32)
    along = jnp.mean(total * unit, axis=-1, keepdims=True)
    out[...] = grad_ref[...].astype(F32) + scale * (
        total - jnp.mean(total, axis=-1, keepdims=True) - unit * along
    )


def params():
    return pltpu.CompilerParams(
        dimension_semantics=("arbitrary",), vmem_limit_bytes=VMEM_LIMIT
    )


def after(value, *others):
    return lax.optimization_barrier((value,) + others)[0]


def shape(dims, kind):
    return jax.ShapeDtypeStruct(dims, kind)


def cost(flops, nbytes, trans=0):
    return pl.CostEstimate(flops=1000, bytes_accessed=1000, transcendentals=0)


def on_device(
    dp_size,
    tensor_size,
    inputs,
    qkv_weight,
    qkv_bias,
    dense_weight,
    up_weight,
    up_bias,
    down_weight,
    out_bias,
    gain_one,
    shift_one,
    gain_two,
    shift_two,
    feature_omega,
    doc_ids,
    out_grad,
):
    rows, model = inputs.shape
    inner = tensor_size // 2
    tokens = rows * inner
    qkv_cols = qkv_weight.shape[1]
    count = qkv_cols // (3 * HEAD_DIM)
    width = count * HEAD_DIM
    hidden_cols = up_weight.shape[1]
    hidden_part, model_part = hidden_cols // QUARTERS, model // QUARTERS
    member = lax.axis_index("dp")
    place = lax.axis_index("tensor")
    half, slot = place // inner, place % inner
    part = member % QUARTERS

    def swap(values, over_dp, over_tensor):
        pairs = [
            (p * tensor_size + t, (p ^ over_dp) * tensor_size + (t ^ over_tensor))
            for p in range(dp_size)
            for t in range(tensor_size)
        ]
        return lax.ppermute(values, AXES, pairs)

    def across(values, source_half):
        pairs = [
            (p * tensor_size + source_half * inner + t, p * tensor_size + (1 - source_half) * inner + t)
            for p in range(dp_size)
            for t in range(inner)
        ]
        return lax.ppermute(values, AXES, pairs)

    def gather(block):
        return [block] + [swap(block, 0, k) for k in range(1, inner)]

    line, due = [], [()]

    def run(step, *operands, gate=0):
        operands = list(operands)
        held = tuple(line[-1:]) + due[0]
        if held:
            operands[gate] = after(operands[gate], *held)
        result = step(*operands)
        line.append(result[0] if isinstance(result, (tuple, list)) else result)
        return result

    def tick(*arrived):
        due[0] = tuple(arrived) + tuple(line[-1:])

    def now(values):
        return after(values, *due[0])

    table = jnp.stack([slot, half, part]).astype(jnp.int32)
    plain = lambda cols: pl.BlockSpec((rows, cols), lambda k, *s: (k, 0))
    moved = lambda cols: pl.BlockSpec((rows, cols), lambda k, table, *s: (k ^ table[0], 0))
    whole = lambda *dims: pl.BlockSpec(dims, lambda k, *s: (0,) * len(dims))
    spec = lambda values: whole(*values.shape)

    def call(kernel, name, outs, in_specs, out_specs, price, prefetch=1, scratch=(), steps=inner):
        return pl.pallas_call(
            kernel,
            out_shape=outs,
            grid_spec=pltpu.PrefetchScalarGridSpec(
                num_scalar_prefetch=prefetch,
                grid=(steps,),
                in_specs=in_specs,
                out_specs=out_specs,
                scratch_shapes=list(scratch),
            ),
            compiler_params=params(),
            cost_estimate=price,
            name=name,
        )

    def once(kernel, name, outs, prefetch=1, scratch=()):
        single = not isinstance(outs, (tuple, list))
        listed = (outs,) if single else tuple(outs)

        def step(*operands):
            result = call(
                kernel,
                name,
                listed,
                [spec(v) for v in operands[prefetch:]],
                [whole(*v.shape) for v in listed],
                cost(0, 0),
                prefetch,
                scratch,
                1,
            )(*operands)
            return result[0] if single else result

        return step

    first_rows, first_cols = model_part + width + 16, max(qkv_cols, model_part)
    docs = doc_ids.reshape(-1)
    docs_col = docs.reshape(-1, 1)
    docs_row = docs.reshape(tensor_size, 1, rows)
    affine = jnp.stack([gain_one, shift_one, gain_two, shift_two]).astype(F32)
    lane = np.arange(LANES) % HEAD_DIM
    rates = np.where(lane < ROT, 10000.0 ** (-(lane % (ROT // 2)) * 2.0 / ROT), 0.0)
    rates = jnp.asarray(rates[None, :], F32)
    own_bias = qkv_bias.reshape(1, -1)
    up_bias_parts = up_bias.reshape(QUARTERS, 1, hidden_part)

    dense_part = width // QUARTERS
    pack_rows = 2 * hidden_part + dense_part + 16
    second_rows = 2 * hidden_part
    wide = pltpu.VMEM((2, width, 2 * width), F32)
    narrow = pltpu.VMEM((width, 2 * width), F32)
    mine_col = pl.BlockSpec(
        (rows, 1), lambda k, table, docs: ((k ^ table[0]) + table[1] * inner, 0)
    )
    def simple(kernel, name, outs, in_specs, out_specs, price):
        return call(kernel, name, outs, in_specs, out_specs, price, prefetch=0)

    def up_projection(weight, bias):
        return run(
            simple(
                up_kernel,
                "up",
                (shape((tokens, hidden_cols), BF16),) * 2,
                [plain(model), whole(hidden_cols, model), whole(1, hidden_cols)],
                [plain(hidden_cols)] * 2,
                cost(2 * tokens * model * hidden_cols, 5e6, 2 * tokens * hidden_cols),
            ),
            norm_two,
            weight,
            bias,
        )

    def down_back(weight, slope):
        return run(
            simple(
                down_back_kernel,
                "down_back",
                (shape((tokens, hidden_cols), BF16), shape((8, hidden_cols), F32)),
                [plain(model), whole(hidden_cols, model), plain(hidden_cols)],
                [plain(hidden_cols), whole(8, hidden_cols)],
                cost(2 * tokens * model * hidden_cols, 5e6),
            ),
            grad_all,
            weight,
            slope,
            gate=2,
        )

    def add(a, b):
        return (a.astype(F32) + b.astype(F32)).astype(BF16)

    def rest(total):
        step = QUARTERS
        while step < dp_size:
            total = add(total, swap(total, step, 0))
            step *= 2
        return total

    def add_three(a, b, c):
        return (a.astype(F32) + b.astype(F32) + c.astype(F32)).astype(BF16)

    class PairSum:
        def __init__(self, parts):
            self.kept, self.sent = parts
            self.bit = 1

        def start(self):
            self.moving = swap(now(self.sent), 0, self.bit)
            self.bit *= 2
            return self.moving

        def more(self):
            return self.bit < inner

        def add(self):
            def halve(a, b):
                total = add(a, b)
                return total[0::2], total[1::2]

            self.kept, self.sent = run(halve, self.kept, self.moving)

        def result(self):
            return self.kept[0], self.moving[0]

    def hidden_weights(active, hidden_grad, side, sums_row):
        return run(
            call(
                hidden_weights_kernel,
                "hidden_weights",
                (shape((2, pack_rows, model), BF16),) * 2,
                [
                    whole(tokens, hidden_cols),
                    whole(tokens, hidden_cols),
                    pl.BlockSpec((tokens, width), lambda k, table: (0, side))
                    if width % LANES == 0
                    else whole(tokens, width),
                    whole(tokens, model),
                    whole(tokens, model),
                    whole(8, hidden_cols),
                ],
                [whole(2, pack_rows, model)] * 2,
                cost(2 * tokens * model * (2 * hidden_cols + width), 9e6),
                scratch=[pltpu.VMEM((width, model), BF16)],
                steps=1,
            ),
            table,
            active,
            hidden_grad,
            merged if width % LANES == 0 else merged[:, side * width : (side + 1) * width],
            grad_all,
            norm_two,
            sums_row,
            gate=2,
        )

    x_blocks = [inputs] + [swap(inputs, 0, k) for k in range(1, inner)]
    first_pack = run(
        call(
            first_pack_kernel,
            "first_pack",
            shape((first_rows, first_cols), BF16),
            [
                pl.BlockSpec((model_part, qkv_cols), lambda k, table: (table[2], 0)),
                pl.BlockSpec((width, model_part), lambda k, table: (0, table[2])),
                whole(1, qkv_cols),
                whole(QUARTERS, 1, hidden_part),
            ],
            whole(first_rows, first_cols),
            cost(1e5, 4e5),
            steps=1,
        ),
        table,
        qkv_weight,
        dense_weight,
        own_bias,
        up_bias_parts,
    )
    first_mine = swap(first_pack, 0, inner)
    own_up, own_down, own_up_bias, second_pack = run(
        once(
            arrange_kernel,
            "arrange",
            (
                shape((hidden_cols, model), BF16),
                shape((hidden_cols, model), BF16),
                shape((1, hidden_cols), F32),
                shape((second_rows, model), BF16),
            ),
            scratch=[pltpu.VMEM((hidden_cols, model), BF16)],
        ),
        table,
        up_weight,
        down_weight,
        up_bias_parts,
        gate=3,
    )
    square = whole(LANES, LANES)
    keep, ahead, behind, mix_high, mix_low, turned_high, turned_low = run(
        call(
            prepare_kernel,
            "prepare",
            (shape((tokens, LANES), F32),) * 3 + (shape((LANES, LANES), BF16),) * 4,
            [whole(1, LANES), whole(HEAD_DIM, HEAD_DIM), pl.BlockSpec(memory_space=pl.ANY)],
            [plain(LANES)] * 3 + [square] * 4,
            cost(1e6, 2e6),
        ),
        table,
        after(rates, affine, docs_row),
        feature_omega,
        docs_col,
        gate=2,
    )

    tick(first_mine, *x_blocks[1:])
    first_third, first_near = swap(now(first_mine), 2, 0), swap(now(first_mine), 1, 0)
    second_mine = swap(now(second_pack), 0, inner)
    grad_blocks = [out_grad] + [swap(now(out_grad), 0, k) for k in range(1, inner - 1)]
    norm_one, norm_two, unit, own_feat, own_value, near_state = run(
        call(
            functools.partial(own_features_kernel, count, inner),
            "own_features",
            (
                shape((tokens, model), BF16),
                shape((tokens, model), BF16),
                shape((tokens, model), BF16),
                shape((tokens, 2 * width), F32),
                shape((tokens, width), BF16),
                shape((width, LANES), F32),
            ),
            [pl.BlockSpec(memory_space=pltpu.HBM)] * inner
            + [
                whole(4, model),
                whole(model, qkv_cols),
                whole(1, qkv_cols),
                moved(LANES),
                moved(LANES),
                moved(LANES),
                square,
                square,
                mine_col,
            ],
            [
                plain(model),
                plain(model),
                plain(model),
                plain(2 * width),
                plain(width),
                whole(width, LANES),
            ],
            cost(2 * tokens * model * qkv_cols, 12e6),
            prefetch=2,
            scratch=[
                narrow,
                pltpu.VMEM((2, rows, model), BF16),
                pltpu.SemaphoreType.DMA((2,)),
            ],
        ),
        table,
        docs,
        *x_blocks,
        affine,
        qkv_weight,
        own_bias,
        keep,
        ahead,
        behind,
        mix_high,
        mix_low,
        docs_col,
        gate=2 + inner,
    )
    tick(first_third, first_near)
    first_last = swap(now(first_third), 1, 0)
    grad_blocks.append(swap(now(out_grad), 0, inner - 1))
    own_active, own_slope = up_projection(own_up, own_up_bias)

    tick(first_last)
    far_qkv, far_dense, far_up_bias = run(
        once(
            collect_first_kernel,
            "collect_first",
            (
                shape((model, qkv_cols), BF16),
                shape((width, model), BF16),
                shape((1, hidden_cols), F32),
            ),
        ),
        table,
        first_mine,
        first_near,
        first_third,
        first_last,
        gate=1,
    )
    far_feat, far_value, state = run(
        call(
            functools.partial(far_features_kernel, count),
            "far_features",
            (
                shape((tokens, 2 * width), F32),
                shape((tokens, width), BF16),
                shape((2, width, LANES), F32),
            ),
            [
                plain(model),
                whole(model, qkv_cols),
                pl.BlockSpec((16, first_cols), lambda k, *s: ((model_part + width) // 16, 0)),
                moved(LANES),
                moved(LANES),
                moved(LANES),
                square,
                square,
                mine_col,
                whole(width, LANES),
            ],
            [plain(2 * width), plain(width), whole(2, width, LANES)],
            cost(2 * tokens * model * qkv_cols, 8e6),
            prefetch=2,
            scratch=[narrow],
        ),
        table,
        docs,
        norm_one,
        far_qkv,
        first_mine,
        keep,
        ahead,
        behind,
        mix_high,
        mix_low,
        docs_col,
        near_state,
        gate=2,
    )
    first_state = across(state, 0)
    tick(first_state, second_mine, *grad_blocks[1:])
    second_third, second_near = swap(now(second_mine), 2, 0), swap(now(second_mine), 1, 0)
    block_row = pl.BlockSpec((1, 1, rows), lambda m, table, docs: (m + table[1] * inner, 0, 0))
    block_col = pl.BlockSpec((rows, 1), lambda m, table, docs: (m + table[1] * inner, 0))
    mixed, merged, inverse, states = run(
        call(
            functools.partial(forward_kernel, count),
            "attend",
            (
                shape((tokens, 2 * width), F32),
                shape((tokens, 2 * width), BF16),
                shape((tokens, 2 * width), F32),
                shape((inner, 2, width, 2 * width), F32),
            ),
            [
                moved(2 * width),
                moved(2 * width),
                moved(width),
                moved(width),
                block_col,
                block_row,
                whole(2, width, LANES),
            ],
            [
                moved(2 * width),
                moved(2 * width),
                moved(2 * width),
                pl.BlockSpec((1, 2, width, 2 * width), lambda m, *s: (m, 0, 0, 0)),
            ],
            cost(2 * count * tokens * rows * 800, 5e6),
            prefetch=2,
            scratch=[wide],
        ),
        table,
        docs,
        own_feat,
        far_feat,
        own_value,
        far_value,
        docs_col,
        docs_row,
        first_state,
        gate=2,
    )
    grad_all, grad_sums = run(
        once(
            collect_grad_kernel,
            "collect_grad",
            (shape((tokens, model), BF16), shape((8, model), F32)),
            prefetch=0,
        ),
        *grad_blocks,
        gate=1,
    )
    merged_grad, later = run(
        call(
            functools.partial(later_kernel, count),
            "later",
            (shape((tokens, 2 * width), F32), shape((2, width, LANES), F32)),
            [
                plain(model),
                whole(width, model),
                whole(width, model),
                plain(2 * width),
                plain(2 * width),
                plain(2 * width),
                plain(2 * width),
                mine_col,
            ],
            [plain(2 * width), whole(2, width, LANES)],
            cost(2 * count * tokens * 64 * 256, 5e6),
            prefetch=2,
            scratch=[wide],
        ),
        *(table, docs, grad_all, dense_weight, far_dense, own_feat, far_feat, mixed, inverse, docs_col),
        gate=2,
    )
    first_later = across(later, 1)
    tick(second_third)
    second_last = swap(now(second_third), 1, 0)
    own_hidden_grad, own_up_sums = down_back(own_down, own_slope)
    own_kept, own_sent = hidden_weights(own_active, own_hidden_grad, 0, own_up_sums)
    tick(second_last, second_near, first_later)
    own_got = swap(now(own_sent), 1, 0)
    far_up, far_down = run(
        once(
            collect_second_kernel,
            "collect_second",
            (shape((hidden_cols, model), BF16),) * 2,
            prefetch=0,
        ),
        second_mine,
        second_near,
        second_third,
        second_last,
    )
    far_active, far_slope = up_projection(far_up, far_up_bias)
    far_hidden_grad, far_up_sums = down_back(far_down, far_slope)
    far_kept, far_sent = hidden_weights(far_active, far_hidden_grad, 1, far_up_sums)
    tick(own_got)
    own_next = run(add, own_kept[1], own_got[1])
    tick()
    far_got = swap(now(far_sent), 1, 0)
    partial_out = run(
        simple(
            out_kernel,
            "out",
            (shape((inner // 2, rows, model), BF16),) * 2,
            [
                plain(2 * width),
                plain(hidden_cols),
                plain(hidden_cols),
                whole(width, model),
                whole(width, model),
                whole(hidden_cols, model),
                whole(hidden_cols, model),
            ],
            [whole(inner // 2, rows, model)] * 2,
            cost(4 * tokens * model * (width + hidden_cols), 8e6),
        ),
        merged,
        own_active,
        far_active,
        dense_weight,
        far_dense,
        own_down,
        far_down,
    )

    tick(far_got)
    far_next = run(add, far_kept[1], far_got[1])
    tick()
    far_cross = swap(now(far_next), 2, 0)
    out_sum = PairSum(partial_out)
    out_moving = out_sum.start()
    back = lambda cols: pl.BlockSpec((rows, cols), lambda m, table, docs: ((inner - 1 - m) ^ table[0], 0))
    back_straight = lambda cols: pl.BlockSpec((rows, cols), lambda m, *s: (inner - 1 - m, 0))
    own_pg, far_pg = run(
        call(
            functools.partial(backward_kernel, count),
            "attend_back",
            (shape((tokens, qkv_cols), BF16),) * 2,
            [
                back(2 * width),
                back(2 * width),
                back(width),
                back(width),
                back(2 * width),
                back(2 * width),
                back(2 * width),
                pl.BlockSpec(
                    (rows, 1), lambda m, table, docs: (inner - 1 - m + table[1] * inner, 0)
                ),
                pl.BlockSpec(
                    (1, 1, rows), lambda m, table, docs: (inner - 1 - m + table[1] * inner, 0, 0)
                ),
                pl.BlockSpec((1, 2, width, 2 * width), lambda m, *s: (inner - 1 - m, 0, 0, 0)),
                whole(2, width, LANES),
                back_straight(LANES),
                back_straight(LANES),
                back_straight(LANES),
                square,
                square,
            ],
            [back(qkv_cols), back(qkv_cols)],
            cost(2 * count * tokens * rows * 2000, 8e6),
            prefetch=2,
            scratch=[wide],
        ),
        table,
        docs,
        own_feat,
        far_feat,
        own_value,
        far_value,
        mixed,
        inverse,
        merged_grad,
        docs_col,
        docs_row,
        states,
        first_later,
        keep,
        ahead,
        behind,
        turned_high,
        turned_low,
        gate=8,
    )
    kept, sent = run(
        once(
            qkv_weights_kernel,
            "qkv_weights",
            (shape((4, model_part + 16, qkv_cols), BF16),) * 2,
            scratch=[pltpu.VMEM((model, qkv_cols), BF16)],
        ),
        table,
        own_pg,
        far_pg,
        norm_one,
        gate=3,
    )
    tick(far_cross)
    far_quad = run(add_three, far_kept[0], far_got[0], far_cross)
    tick()
    far_home = swap(now(far_quad), 0, inner)
    norm_grads = run(
        simple(
            norm_grad_kernel,
            "norm_grad",
            (shape((8, model), F32),) + (shape((inner // 2, rows, model), BF16),) * 2,
            [
                plain(qkv_cols),
                plain(qkv_cols),
                plain(hidden_cols),
                plain(hidden_cols),
                whole(model, qkv_cols),
                whole(model, qkv_cols),
                whole(hidden_cols, model),
                whole(hidden_cols, model),
                plain(model),
                whole(4, model),
                whole(8, model),
            ],
            [whole(8, model)] + [whole(inner // 2, rows, model)] * 2,
            cost(4 * tokens * model * (qkv_cols + hidden_cols), 12e6),
        ),
        own_pg,
        far_pg,
        own_hidden_grad,
        far_hidden_grad,
        qkv_weight,
        far_qkv,
        own_up,
        far_up,
        unit,
        affine,
        grad_sums,
        gate=8,
    )
    e_sum = PairSum(norm_grads[1:])
    steps = [(1 << k, 0) for k in range(dp_size.bit_length() - 1)]
    steps += [(0, 1 << k) for k in range(tensor_size.bit_length() - 1)]
    small = norm_grads[0]

    def small_start():
        return swap(now(small), *steps.pop(0))

    def small_add(moved):
        return run(lambda a, b: a + b, small, moved)

    tick(out_moving)
    out_sum.add()
    tick()
    e_moving = e_sum.start()
    out_moving = out_sum.start()
    got, own_cross = swap(now(sent), 1, 0), swap(now(own_next), 2, 0)
    tick(got)
    cross_sent = run(add, kept[2:], got[2:])
    tick()
    crossed = swap(now(cross_sent), 2, 0)
    tick(out_moving)
    while out_sum.more():
        out_sum.add()
        tick(out_sum.start())
    layer_out = run(
        once(finish_out_kernel, "finish_out", shape((rows, model), BF16), prefetch=0),
        inputs,
        out_bias.reshape(1, -1),
        *out_sum.result(),
        gate=2,
    )
    tick(crossed)
    far_piece = run(add_three, kept[1], got[1], crossed[1])
    own_piece = run(add_three, kept[0], got[0], crossed[0])
    tick()
    far_piece_home = swap(now(far_piece), 0, inner)
    tick(far_home, own_cross)
    own_quad = run(add_three, own_kept[0], own_got[0], own_cross)
    lower_mine = rest(run(add, own_quad, far_home))
    tick()
    lower_third, lower_near = swap(now(lower_mine), 2, 0), swap(now(lower_mine), 1, 0)
    tick(e_moving)
    e_sum.add()
    tick()
    e_moving = e_sum.start()
    moved_small = small_start()
    tick(far_piece_home, lower_near, moved_small)
    upper_mine = rest(run(add, own_piece, far_piece_home))
    small = small_add(moved_small)
    tick()
    upper_third, upper_near = swap(now(upper_mine), 2, 0), swap(now(upper_mine), 1, 0)
    moved_small = small_start()
    tick(e_moving)
    while e_sum.more():
        e_sum.add()
        tick(e_sum.start())
    input_grad = run(
        once(finish_in_kernel, "finish_in", shape((rows, model), F32), prefetch=0),
        inputs,
        out_grad,
        *e_sum.result(),
        gate=2,
    )
    tick(lower_third, moved_small)
    lower = (lower_mine, lower_near, lower_third, swap(now(lower_third), 1, 0))
    small = small_add(moved_small)
    tick(upper_third, upper_near)
    upper = (upper_mine, upper_near, upper_third, swap(now(upper_third), 1, 0))
    moved_small = small_start()
    tick(lower[3], moved_small)
    small = small_add(moved_small)
    tick()
    moved_small = small_start()
    up_grad, down_grad, dense_grad, up_bias_grad = run(
        once(
            finish_hidden_kernel,
            "finish_hidden",
            (
                shape((model, hidden_cols), F32),
                shape((hidden_cols, model), F32),
                shape((width, model), F32),
                shape((QUARTERS, 1, hidden_part), F32),
            ),
            scratch=[pltpu.VMEM((hidden_cols, model), F32)],
        ),
        table,
        *lower,
        gate=1,
    )
    tick(moved_small, upper[3])
    small = small_add(moved_small)
    tick()
    moved_small = small_start()
    qkv_grad, qkv_bias_grad = run(
        once(
            finish_qkv_kernel,
            "finish_qkv",
            (shape((model, qkv_cols), F32), shape((1, qkv_cols), F32)),
        ),
        table,
        *upper,
        gate=1,
    )

    small = small + moved_small
    while steps:
        tick()
        small = small_add(small_start())
    cols = model // tensor_size
    small = lax.dynamic_slice_in_dim(small, place * cols, cols, 1)

    return (
        layer_out,
        input_grad,
        qkv_grad,
        qkv_bias_grad.reshape(-1),
        dense_grad,
        up_grad,
        up_bias_grad.reshape(-1),
        down_grad,
        small[4],
        small[0],
        small[1],
        small[2],
        small[3],
    )


def solution(mesh):
    in_specs = (
        P(("dp", "tensor"), None),
        P(None, "tensor"),
        P("tensor"),
        P("tensor", None),
        P(None, "tensor"),
        P("tensor"),
        P("tensor", None),
        P(),
        P(),
        P(),
        P(),
        P(),
        P(),
        P("dp", None),
        P(("dp", "tensor"), None),
    )
    out_specs = (
        P(("dp", "tensor"), None),
        P(("dp", "tensor"), None),
        P(None, "tensor"),
        P("tensor"),
        P("tensor", None),
        P(None, "tensor"),
        P("tensor"),
        P("tensor", None),
        P("tensor"),
        P("tensor"),
        P("tensor"),
        P("tensor"),
        P("tensor"),
    )
    return jax.shard_map(
        functools.partial(on_device, mesh.shape["dp"], mesh.shape["tensor"]),
        mesh=mesh,
        in_specs=in_specs,
        out_specs=out_specs,
        check_vma=False,
    )
```

```python
import functools

import jax
import jax.numpy as jnp
import numpy as np
from jax import lax
from jax.experimental import pallas as pl
from jax.experimental.pallas import tpu as pltpu
from jax.sharding import PartitionSpec as P

HEAD_DIM = 64
ROT = 16
LANES = 128
EPS = 1e-05
EXACT = lax.Precision.HIGHEST
F32 = jnp.float32
BF16 = jnp.bfloat16
AXES = ("dp", "tensor")
VMEM_LIMIT = 16 * 1024 * 1024
QUARTERS = 4

NN = ((1,), (0,))
NT = ((1,), (1,))
TN = ((0,), (0,))


def dot(a, b, dims=NN, precision=None):
    return lax.dot_general(a, b, (dims, ((), ())), precision=precision, preferred_element_type=F32)


def halves(values):
    high = values.astype(BF16)
    return high, (values - high.astype(F32)).astype(BF16)


def lane_of(dims):
    return lax.broadcasted_iota(jnp.int32, dims, len(dims) - 1)


def prepare_kernel(table, rates, omega, docs_col, keep, ahead, behind, mix_high, mix_low, turned_high, turned_low):
    rows = keep.shape[0]
    start = (table[1] * pl.num_programs(0) + pl.program_id(0)) * rows
    places = start + lax.broadcasted_iota(jnp.int32, (rows, LANES), 0)
    angles = places.astype(F32) * rates[...]
    inner = lane_of((rows, LANES)) % HEAD_DIM
    cosine, sine = jnp.cos(angles), jnp.sin(angles)
    half = ROT // 2
    keep[...] = jnp.where(inner < ROT, cosine, 1.0)
    ahead[...] = jnp.where(inner < half, -sine, 0.0)
    behind[...] = jnp.where((inner >= half) & (inner < ROT), sine, 0.0)

    @pl.when(pl.program_id(0) == 0)
    def _():
        extent = HEAD_DIM
        n = lax.broadcasted_iota(jnp.int32, (LANES, LANES), 0)
        k = lax.broadcasted_iota(jnp.int32, (LANES, LANES), 1)
        same = (n // extent) == (k // extent)
        n, k = (n % extent).astype(F32), (k % extent).astype(F32)
        scale = jnp.where(k == 0, float(np.sqrt(1.0 / extent)), float(np.sqrt(2.0 / extent)))
        matrix = jnp.where(same, jnp.cos(np.pi * (n + 0.5) * k / extent) * scale, 0.0)
        row = jnp.concatenate([omega[...]] * 2, axis=1)
        spread = jnp.where(same, jnp.concatenate([row] * 2, axis=0), 0.0)
        mixing = dot(matrix, spread, precision=EXACT)
        mix_high[...], mix_low[...] = halves(mixing)
        turned_high[...], turned_low[...] = halves(mixing.T)


def turn(values, keep, ahead, behind, sign):
    half = ROT // 2
    moved = (
        pltpu.roll(values, LANES - half, axis=1) * ahead + pltpu.roll(values, half, axis=1) * behind
    )
    return values * keep + sign * moved


def mixed_dot(values, high, low):
    first, second = halves(values)
    return dot(first, high) + (dot(second, high) + dot(first, low))


def head_columns(values, which, count):
    parts = [
        values[:, (3 * j + which) * HEAD_DIM : (3 * j + which + 1) * HEAD_DIM] for j in range(count)
    ]
    return parts[0] if count == 1 else jnp.concatenate(parts, axis=1)


def masked_stack(values, count):
    if count == 1:
        return values
    lane = (lane_of(values.shape) % (count * HEAD_DIM)) // HEAD_DIM
    zero = jnp.zeros_like(values)
    return jnp.concatenate([jnp.where(lane == j, values, zero) for j in range(count)], axis=0)


def side_by_side(stack, count):
    rows = stack.shape[0] // count
    if count == 1:
        return stack
    return jnp.concatenate([stack[j * rows : (j + 1) * rows] for j in range(count)], axis=1)


def own_block(dims):
    rows = lax.broadcasted_iota(jnp.int32, dims, 0) // HEAD_DIM
    return rows == (lane_of(dims) % dims[0]) // HEAD_DIM


def compress(state, count):
    width = count * HEAD_DIM
    sides = []
    for base in (0, width):
        part = state[:, base : base + HEAD_DIM]
        for j in range(1, count):
            rows = lax.broadcasted_iota(jnp.int32, part.shape, 0) // HEAD_DIM
            here = state[:, base + j * HEAD_DIM : base + (j + 1) * HEAD_DIM]
            part = jnp.where(rows == j, here, part)
        sides.append(part)
    return jnp.concatenate(sides, axis=1)


def expand(packed, count):
    values, totals = packed[:, :HEAD_DIM], packed[:, HEAD_DIM:]
    wide = jnp.concatenate([values] * count + [totals] * count, axis=1)
    return jnp.where(own_block(wide.shape), wide, 0.0)


def project(count, one, weight, bias, turns, mix_high, mix_low, chosen, feat_out, value_out, state):
    width = count * HEAD_DIM
    projected = dot(one, weight) + bias
    value = head_columns(projected, 2, count).astype(BF16)
    pairs = [head_columns(projected, which, count) for which in (0, 1)]
    if count == 1:
        pairs = [jnp.concatenate(pairs, axis=1)]
    feats = []
    for pair in pairs:
        feats.append(jnp.exp(mixed_dot(turn(pair, *turns, 1.0), mix_high, mix_low)))
    feat = feats[0] if count == 1 else jnp.concatenate(feats, axis=1)
    feat_out[...] = feat
    value_out[...] = value
    key = jnp.where(chosen, feat[:, width:], 0.0).astype(BF16)
    state[...] += dot(key, jnp.concatenate([value, jnp.ones_like(value)], axis=1), TN)


def load_block(refs, keep, sems):
    def copy(k):
        return pltpu.make_async_copy(refs[k], keep.at[k % 2], sems.at[k % 2])

    for k in range(len(refs)):

        @pl.when(pl.program_id(0) == k)
        def _(k=k):
            if k == 0:
                copy(0).start()
            if k + 1 < len(refs):
                copy(k + 1).start()
            copy(k).wait()

    return keep[pl.program_id(0) % 2]


def own_features_kernel(count, blocks, table, docs, *refs):
    x_refs = refs[:blocks]
    (
        affine,
        weight,
        bias,
        keep,
        ahead,
        behind,
        mix_high,
        mix_low,
        docs_col,
        norm_one,
        norm_two,
        unit_out,
        feat_out,
        value_out,
        state_out,
        state,
        x_keep,
        x_sems,
    ) = refs[blocks:]

    @pl.when(pl.program_id(0) == 0)
    def _():
        state[...] = jnp.zeros_like(state)

    rows = x_keep.shape[1]
    x = load_block(x_refs, x_keep, x_sems).astype(F32)
    mean = jnp.mean(x, axis=-1, keepdims=True)
    centred = x - mean
    scale = lax.rsqrt(jnp.mean(centred * centred, axis=-1, keepdims=True) + EPS)
    unit = centred * scale
    one = (unit * affine[0:1] + affine[1:2]).astype(BF16)
    norm_one[...] = one
    norm_two[...] = (unit * affine[2:3] + affine[3:4]).astype(BF16)
    unit_out[...] = unit.astype(BF16)
    chosen = docs_col[...] == docs[(table[1] + 1) * blocks * rows - 1]
    project(
        count,
        one,
        weight[...],
        bias[...].astype(F32),
        (keep[...], ahead[...], behind[...]),
        mix_high[...],
        mix_low[...],
        chosen,
        feat_out,
        value_out,
        state,
    )

    @pl.when(pl.program_id(0) == pl.num_programs(0) - 1)
    def _():
        state_out[...] = compress(state[...], count)


def far_features_kernel(
    count,
    table,
    docs,
    norm_one,
    weight,
    bias,
    keep,
    ahead,
    behind,
    mix_high,
    mix_low,
    docs_col,
    near_state,
    feat_out,
    value_out,
    state_out,
    state,
):
    @pl.when(pl.program_id(0) == 0)
    def _():
        state[...] = jnp.zeros_like(state)

    rows = norm_one.shape[0]
    chosen = docs_col[...] == docs[(table[1] + 1) * pl.num_programs(0) * rows - 1]
    project(
        count,
        norm_one[...],
        weight[...],
        bias[0:1, : weight.shape[1]].astype(F32),
        (keep[...], ahead[...], behind[...]),
        mix_high[...],
        mix_low[...],
        chosen,
        feat_out,
        value_out,
        state,
    )

    @pl.when(pl.program_id(0) == pl.num_programs(0) - 1)
    def _():
        state_out[0] = near_state[...]
        state_out[1] = compress(state[...], count)


def allowed_pairs(docs_col, docs_row, count):
    size = docs_col.shape[0]
    rows = lax.broadcasted_iota(jnp.int32, (size, size), 0)
    cols = lax.broadcasted_iota(jnp.int32, (size, size), 1)
    allowed = ((docs_col == docs_row) & (rows >= cols)).astype(F32)
    return allowed if count == 1 else jnp.concatenate([allowed] * count, axis=0)


def forward_kernel(
    count,
    table,
    docs,
    own_feat,
    far_feat,
    own_value,
    far_value,
    docs_col,
    docs_row,
    first_state,
    mixed_out,
    merged_out,
    inverse_out,
    states_out,
    state,
):
    step = pl.program_id(0)
    width = count * HEAD_DIM
    rows = own_feat.shape[0]

    @pl.when(step == 0)
    def _():
        for side in range(2):
            state[side] = expand(first_state[1 - side], count)

    start = (table[1] * pl.num_programs(0) + step) * rows
    before = jnp.where(start > 0, docs[jnp.maximum(start - 1, 0)], -1)
    last = docs[start + rows - 1]
    kept = (last == before).astype(F32)
    allowed = allowed_pairs(docs_col[...], docs_row[0], count)
    carried = docs_col[...] == before
    chosen = docs_col[...] == last
    for side in range(2):
        feat_ref, value_ref = ((own_feat, own_value), (far_feat, far_value))[side]
        query = feat_ref[:, :width].astype(BF16)
        key = feat_ref[:, width:]
        value = value_ref[...]
        both = jnp.concatenate([value, jnp.ones_like(value)], axis=1)
        memory = state[side]
        states_out[0, side] = memory
        high, low = halves(memory)
        weights = (dot(masked_stack(query, count), key.astype(BF16), NT) * allowed).astype(BF16)
        sums = dot(side_by_side(weights, count), masked_stack(both, count)) + jnp.where(
            carried, dot(query, high) + dot(query, low), 0.0
        )
        inverse = 1.0 / sums[:, width:]
        mixed = sums[:, :width] * inverse
        mixed_out[:, side * width : (side + 1) * width] = mixed
        merged_out[:, side * width : (side + 1) * width] = mixed.astype(BF16)
        inverse_out[:, side * width : (side + 1) * width] = inverse
        picked = jnp.where(chosen, key, 0.0).astype(BF16)
        added = dot(picked, both, TN)
        state[side] = kept * memory + jnp.where(own_block(added.shape), added, 0.0)


def pair_grads(grad, inverse, mixed):
    part = (grad * inverse).astype(BF16)
    high, low = halves(-(part.astype(F32) * mixed))
    return part, high, low


def later_kernel(
    count,
    table,
    docs,
    grad_ref,
    own_dense,
    far_dense,
    own_feat,
    far_feat,
    mixed_ref,
    inverse_ref,
    docs_col,
    merged_grad,
    later_out,
    later,
):
    @pl.when(pl.program_id(0) == 0)
    def _():
        later[...] = jnp.zeros_like(later)

    width = count * HEAD_DIM
    rows = own_feat.shape[0]
    chosen = docs_col[...] == docs[table[1] * pl.num_programs(0) * rows]
    for side, dense in enumerate((own_dense, far_dense)):
        span = slice(side * width, (side + 1) * width)
        grad = dot(grad_ref[...], dense[...], NT)
        merged_grad[:, span] = grad
        part, high, low = pair_grads(grad, inverse_ref[:, span], mixed_ref[:, span])
        query = (own_feat, far_feat)[side][:, :width]
        query = jnp.where(chosen, query, 0.0).astype(BF16)
        later[side, :, :width] += dot(query, part, TN)
        later[side, :, width:] += dot(query, high, TN) + dot(query, low, TN)

    @pl.when(pl.program_id(0) == pl.num_programs(0) - 1)
    def _():
        for side in range(2):
            later_out[side] = compress(later[side], count)


def backward_kernel(
    count,
    table,
    docs,
    own_feat,
    far_feat,
    own_value,
    far_value,
    mixed_ref,
    inverse_ref,
    grad_ref,
    docs_col,
    docs_row,
    states_ref,
    first_later,
    keep,
    ahead,
    behind,
    turned_high,
    turned_low,
    own_out,
    far_out,
    later,
):
    blocks = pl.num_programs(0)
    step = blocks - 1 - pl.program_id(0)
    width = count * HEAD_DIM
    rows = own_feat.shape[0]

    @pl.when(pl.program_id(0) == 0)
    def _():
        for side in range(2):
            later[side] = expand(first_later[1 - side], count)

    start = (table[1] * blocks + step) * rows
    total = docs.shape[0]
    before = jnp.where(start > 0, docs[jnp.maximum(start - 1, 0)], -1)
    after = jnp.where(start + rows < total, docs[jnp.minimum(start + rows, total - 1)], -1)
    first = docs[start]
    kept = (first == after).astype(F32)
    allowed = allowed_pairs(docs_col[...], docs_row[0], count)
    carried = docs_col[...] == before
    linked = docs_col[...] == after
    chosen = docs_col[...] == first
    for side in range(2):
        span = slice(side * width, (side + 1) * width)
        feat = (own_feat, far_feat)[side][...]
        query, key = feat[:, :width].astype(BF16), feat[:, width:].astype(BF16)
        value = (own_value, far_value)[side][...]
        ones = jnp.ones_like(value)
        both = jnp.concatenate([value, ones], axis=1)
        part, high, low = pair_grads(grad_ref[:, span], inverse_ref[:, span], mixed_ref[:, span])
        first_two = jnp.concatenate([part, high], axis=1)
        queries = masked_stack(query, count)
        weights = (dot(queries, key, NT) * allowed).astype(BF16)
        weight_grad = dot(masked_stack(first_two, count), both, NT)
        weight_grad += dot(masked_stack(low, count), ones, NT)
        weight_grad = (weight_grad * allowed).astype(BF16)
        mem_high, mem_low = halves(states_ref[0, side])
        late = later[side]
        late_high, late_low = halves(late)
        query_grad = dot(side_by_side(weight_grad, count), masked_stack(key, count)) + jnp.where(
            carried,
            dot(first_two, mem_high, NT) + dot(first_two, mem_low, NT) + dot(low, mem_high[:, width:], NT),
            0.0,
        )
        key_grad = dot(weight_grad, queries, TN) + jnp.where(
            linked, dot(both, late_high, NT) + dot(both, late_low, NT), 0.0
        )
        value_grad = dot(weights, masked_stack(part, count), TN) + jnp.where(
            linked, dot(key, late_high[:, :width]) + dot(key, late_low[:, :width]), 0.0
        )
        picked = jnp.where(chosen, query.astype(F32), 0.0).astype(BF16)
        block = own_block(late.shape)
        added = jnp.concatenate(
            [dot(picked, part, TN), dot(picked, high, TN) + dot(picked, low, TN)], axis=1
        )
        later[side] = kept * late + jnp.where(block, added, 0.0)
        inner = jnp.concatenate([query_grad, key_grad], axis=1) * feat
        pairs = []
        for base in range(0, 2 * width, LANES):
            pair = mixed_dot(inner[:, base : base + LANES], turned_high[...], turned_low[...])
            pairs.append(turn(pair, keep[...], ahead[...], behind[...], -1.0))
        flat = pairs[0] if count == 1 else jnp.concatenate(pairs, axis=1)
        pieces = []
        for j in range(count):
            lanes = slice(j * HEAD_DIM, (j + 1) * HEAD_DIM)
            pieces += [flat[:, :width][:, lanes], flat[:, width:][:, lanes], value_grad[:, lanes]]
        out = own_out if side == 0 else far_out
        out[...] = jnp.concatenate(pieces, axis=1).astype(BF16)


def up_kernel(norm_ref, weight, bias, active_out, slope_out):
    hidden = dot(norm_ref[...], weight[...], NT) + bias[...]
    normal = 0.5 * (1.0 + lax.erf(hidden * 0.7071067811865476))
    density = jnp.exp(-0.5 * hidden * hidden) * 0.3989422804014327
    active_out[...] = (hidden * normal).astype(BF16)
    slope_out[...] = (normal + hidden * density).astype(BF16)


def down_back_kernel(grad_ref, weight, slope, hidden_out, sums_out):
    hidden = (dot(grad_ref[...], weight[...], NT) * slope[...].astype(F32)).astype(BF16)
    hidden_out[...] = hidden

    @pl.when(pl.program_id(0) == 0)
    def _():
        sums_out[...] = jnp.zeros_like(sums_out)

    sums_out[0:1] += jnp.sum(hidden.astype(F32), axis=0, keepdims=True)


def out_kernel(merged, own_active, far_active, own_dense, far_dense, own_down, far_down, *outs):
    width = own_dense.shape[0]
    total = dot(own_active[...], own_down[...]) + dot(far_active[...], far_down[...])
    total += dot(merged[:, :width], own_dense[...]) + dot(merged[:, width:], far_dense[...])
    write_block(outs, total.astype(BF16))


def write_block(outs, values):
    kept, sent = outs
    for k in range(2 * kept.shape[0]):

        @pl.when(pl.program_id(0) == k)
        def _(k=k):
            (sent if k % 2 else kept)[k // 2] = values


def norm_grad_kernel(
    own_pg,
    far_pg,
    own_hg,
    far_hg,
    own_qkv,
    far_qkv,
    own_up,
    far_up,
    unit_ref,
    affine,
    grad_sums,
    sums_out,
    *outs,
):
    @pl.when(pl.program_id(0) == 0)
    def _():
        sums_out[...] = jnp.zeros_like(sums_out)
        sums_out[4:5] = grad_sums[0:1]

    down = lambda values: jnp.sum(values, axis=0, keepdims=True)
    unit = unit_ref[...].astype(F32)
    one = dot(own_pg[...], own_qkv[...], NT) + dot(far_pg[...], far_qkv[...], NT)
    sums_out[0:1] += down(one * unit)
    sums_out[1:2] += down(one)
    two = dot(own_hg[...], own_up[...]) + dot(far_hg[...], far_up[...])
    sums_out[2:3] += down(two * unit)
    sums_out[3:4] += down(two)
    write_block(outs, (one * affine[0:1] + two * affine[2:3]).astype(BF16))


def first_pack_kernel(table, weight, dense, bias, up_bias, out):
    rows, small = weight.shape[0], dense.shape[0]
    if out.shape[1] > min(weight.shape[1], dense.shape[1]):
        out[...] = jnp.zeros_like(out)
    out[:rows, : weight.shape[1]] = weight[...]
    out[rows : rows + small, : dense.shape[1]] = dense[...]
    first = bias[...].astype(F32)
    second = up_bias[table[2]].astype(F32)
    if first.shape[1] > second.shape[1]:
        rest = jnp.zeros((1, first.shape[1] - second.shape[1]), F32)
        second = jnp.concatenate([second, rest], axis=1)
    row = lax.broadcasted_iota(jnp.int32, (16, first.shape[1]), 0)
    out[rows + small :, : first.shape[1]] = jnp.where(row < 8, first, second).astype(BF16)


def arrange_kernel(table, up, down, bias, own_up, own_down, own_bias, pack, turned):
    part = table[2]
    step = down.shape[0] // QUARTERS
    turned[...] = up[...].T
    for k in range(QUARTERS):
        begin = pl.multiple_of((part ^ k) * step, step)
        own_up[k * step : (k + 1) * step] = turned[pl.ds(begin, step)]
        own_down[k * step : (k + 1) * step] = down[pl.ds(begin, step)]
    own_bias[...] = jnp.concatenate([bias[part ^ k].astype(F32) for k in range(QUARTERS)], axis=1)
    pack[:step] = own_up[:step]
    pack[step:] = own_down[:step]


def collect_first_kernel(table, mine, near, third, last, far_qkv, far_dense, far_up_bias):
    part = table[2]
    step = far_qkv.shape[0] // QUARTERS
    small = far_dense.shape[0]
    hidden = far_up_bias.shape[1] // QUARTERS
    biases = []
    for k, ref in enumerate((mine, near, third, last)):
        begin = pl.multiple_of((part ^ k) * step, step)
        far_qkv[pl.ds(begin, step)] = ref[:step, : far_qkv.shape[1]]
        far_dense[:, pl.ds(begin, step)] = ref[step : step + small, :step]
        tail = ref[step + small :].astype(F32)
        biases.append(tail[8:9, :hidden])
    far_up_bias[...] = jnp.concatenate(biases, axis=1)


def collect_second_kernel(mine, near, third, last, far_up, far_down):
    step = mine.shape[0] // 2
    for k, ref in enumerate((mine, near, third, last)):
        far_up[k * step : (k + 1) * step] = ref[:step]
        far_down[k * step : (k + 1) * step] = ref[step:]


def collect_grad_kernel(*refs):
    blocks, (whole, sums) = refs[:-2], refs[-2:]
    rows = blocks[0].shape[0]
    for k, ref in enumerate(blocks):
        whole[k * rows : (k + 1) * rows] = ref[...]
    sums[...] = jnp.zeros_like(sums)
    sums[0:1] = jnp.sum(blocks[0][...].astype(F32), axis=0, keepdims=True)


def bias_rows(values, cols):
    tile = jnp.zeros((16, values.shape[1]), F32)
    row = lax.broadcasted_iota(jnp.int32, tile.shape, 0)
    high = values.astype(BF16).astype(F32)
    tile = jnp.where(row == 0, high, jnp.where(row == 1, values - high, tile)).astype(BF16)
    if values.shape[1] == cols:
        return tile
    return jnp.concatenate([tile, jnp.zeros((16, cols - values.shape[1]), BF16)], axis=1)


def hidden_weights_kernel(
    table, active, hidden_grad, merged, grad, norm_two, hidden_sums, kept, sent, dense
):
    part = table[2]
    step, small = active.shape[1] // QUARTERS, merged.shape[1] // QUARTERS
    cols = kept.shape[2]
    dense[...] = dot(merged[...], grad[...], TN).astype(BF16)
    down = dot(active[...], grad[...], TN).astype(BF16)
    up = dot(hidden_grad[...], norm_two[...], TN).astype(BF16)
    for k in range(QUARTERS):
        out = (kept, sent)[k % 2].at[k // 2]
        span = slice(k * step, (k + 1) * step)
        out[:step] = up[span]
        out[step : 2 * step] = down[span]
        begin = pl.multiple_of((part ^ k) * small, small)
        out[2 * step : 2 * step + small] = dense[pl.ds(begin, small)]
        out[2 * step + small :] = bias_rows(hidden_sums[0:1, span], cols)


def qkv_weights_kernel(table, own_pg, far_pg, norm_one, kept, sent, full):
    part = table[2]
    cols = kept.shape[2]
    step = full.shape[0] // QUARTERS
    for side, grad in enumerate((own_pg, far_pg)):
        full[...] = dot(norm_one[...], grad[...], TN).astype(BF16)
        tail = bias_rows(jnp.sum(grad[...].astype(F32), axis=0, keepdims=True), cols)
        for k in range(QUARTERS):
            out = (kept, sent)[k % 2].at[2 * (k // 2) + side]
            begin = pl.multiple_of((part ^ k) * step, step)
            out[:step] = full[pl.ds(begin, step)]
            out[step:] = tail


def finish_hidden_kernel(
    table, mine, near, third, last, up_grad, down_grad, dense_grad, bias_grad, turned
):
    part = table[2]
    step, small = down_grad.shape[0] // QUARTERS, dense_grad.shape[0] // QUARTERS
    size = mine.shape[0]
    for k, ref in enumerate((mine, near, third, last)):
        begin = pl.multiple_of((part ^ k) * step, step)
        turned[pl.ds(begin, step)] = ref[:step].astype(F32)
        down_grad[pl.ds(begin, step)] = ref[step : 2 * step].astype(F32)
        begin = pl.multiple_of((part ^ k) * small, small)
        dense_grad[pl.ds(begin, small)] = ref[2 * step : 2 * step + small].astype(F32)
        tail = ref[2 * step + small : size].astype(F32)
        bias_grad[part ^ k] = tail[0:1, :step] + tail[1:2, :step]
    up_grad[...] = turned[...].T


def finish_qkv_kernel(table, mine, near, third, last, weight_grad, bias_grad):
    part = table[2]
    step = weight_grad.shape[0] // QUARTERS
    for k, ref in enumerate((mine, near, third, last)):
        begin = pl.multiple_of((part ^ k) * step, step)
        weight_grad[pl.ds(begin, step)] = ref[:step].astype(F32)
    tail = mine[step:].astype(F32)
    bias_grad[...] = tail[0:1] + tail[1:2]


def finish_out_kernel(x_ref, bias, *refs):
    parts, out = refs[:-1], refs[-1]
    total = x_ref[...].astype(F32) + bias[...].astype(F32)
    for ref in parts:
        total += ref[...].astype(F32)
    out[...] = total.astype(BF16)


def finish_in_kernel(x_ref, grad_ref, *refs):
    parts, out = refs[:-1], refs[-1]
    x = x_ref[...].astype(F32)
    mean = jnp.mean(x, axis=-1, keepdims=True)
    centred = x - mean
    scale = lax.rsqrt(jnp.mean(centred * centred, axis=-1, keepdims=True) + EPS)
    unit = centred * scale
    total = parts[0][...].astype(F32)
    for ref in parts[1:]:
        total += ref[...].astype(F32)
    along = jnp.mean(total * unit, axis=-1, keepdims=True)
    out[...] = grad_ref[...].astype(F32) + scale * (
        total - jnp.mean(total, axis=-1, keepdims=True) - unit * along
    )


def params():
    return pltpu.CompilerParams(
        dimension_semantics=("arbitrary",), vmem_limit_bytes=VMEM_LIMIT
    )


def after(value, *others):
    return lax.optimization_barrier((value,) + others)[0]


def shape(dims, kind):
    return jax.ShapeDtypeStruct(dims, kind)


def cost(flops, nbytes, trans=0):
    return pl.CostEstimate(flops=1000, bytes_accessed=1000, transcendentals=0)


def on_device(
    dp_size,
    tensor_size,
    inputs,
    qkv_weight,
    qkv_bias,
    dense_weight,
    up_weight,
    up_bias,
    down_weight,
    out_bias,
    gain_one,
    shift_one,
    gain_two,
    shift_two,
    feature_omega,
    doc_ids,
    out_grad,
):
    rows, model = inputs.shape
    inner = tensor_size // 2
    tokens = rows * inner
    qkv_cols = qkv_weight.shape[1]
    count = qkv_cols // (3 * HEAD_DIM)
    width = count * HEAD_DIM
    hidden_cols = up_weight.shape[1]
    hidden_part, model_part = hidden_cols // QUARTERS, model // QUARTERS
    member = lax.axis_index("dp")
    place = lax.axis_index("tensor")
    half, slot = place // inner, place % inner
    part = member % QUARTERS

    def swap(values, over_dp, over_tensor):
        pairs = [
            (p * tensor_size + t, (p ^ over_dp) * tensor_size + (t ^ over_tensor))
            for p in range(dp_size)
            for t in range(tensor_size)
        ]
        return lax.ppermute(values, AXES, pairs)

    def across(values, source_half):
        pairs = [
            (p * tensor_size + source_half * inner + t, p * tensor_size + (1 - source_half) * inner + t)
            for p in range(dp_size)
            for t in range(inner)
        ]
        return lax.ppermute(values, AXES, pairs)

    def gather(block):
        return [block] + [swap(block, 0, k) for k in range(1, inner)]

    line, due = [], [()]

    def run(step, *operands, gate=0):
        operands = list(operands)
        held = tuple(line[-1:]) + due[0]
        if held:
            operands[gate] = after(operands[gate], *held)
        result = step(*operands)
        line.append(result[0] if isinstance(result, (tuple, list)) else result)
        return result

    def tick(*arrived):
        due[0] = tuple(arrived) + tuple(line[-1:])

    def now(values):
        return after(values, *due[0])

    table = jnp.stack([slot, half, part]).astype(jnp.int32)
    plain = lambda cols: pl.BlockSpec((rows, cols), lambda k, *s: (k, 0))
    moved = lambda cols: pl.BlockSpec((rows, cols), lambda k, table, *s: (k ^ table[0], 0))
    whole = lambda *dims: pl.BlockSpec(dims, lambda k, *s: (0,) * len(dims))
    spec = lambda values: whole(*values.shape)

    def call(kernel, name, outs, in_specs, out_specs, price, prefetch=1, scratch=(), steps=inner):
        return pl.pallas_call(
            kernel,
            out_shape=outs,
            grid_spec=pltpu.PrefetchScalarGridSpec(
                num_scalar_prefetch=prefetch,
                grid=(steps,),
                in_specs=in_specs,
                out_specs=out_specs,
                scratch_shapes=list(scratch),
            ),
            compiler_params=params(),
            cost_estimate=price,
            name=name,
        )

    def once(kernel, name, outs, prefetch=1, scratch=()):
        single = not isinstance(outs, (tuple, list))
        listed = (outs,) if single else tuple(outs)

        def step(*operands):
            result = call(
                kernel,
                name,
                listed,
                [spec(v) for v in operands[prefetch:]],
                [whole(*v.shape) for v in listed],
                cost(0, 0),
                prefetch,
                scratch,
                1,
            )(*operands)
            return result[0] if single else result

        return step

    first_rows, first_cols = model_part + width + 16, max(qkv_cols, model_part)
    docs = doc_ids.reshape(-1)
    docs_col = docs.reshape(-1, 1)
    docs_row = docs.reshape(tensor_size, 1, rows)
    affine = jnp.stack([gain_one, shift_one, gain_two, shift_two]).astype(F32)
    lane = np.arange(LANES) % HEAD_DIM
    rates = np.where(lane < ROT, 10000.0 ** (-(lane % (ROT // 2)) * 2.0 / ROT), 0.0)
    rates = jnp.asarray(rates[None, :], F32)
    own_bias = qkv_bias.reshape(1, -1)
    up_bias_parts = up_bias.reshape(QUARTERS, 1, hidden_part)

    dense_part = width // QUARTERS
    pack_rows = 2 * hidden_part + dense_part + 16
    second_rows = 2 * hidden_part
    wide = pltpu.VMEM((2, width, 2 * width), F32)
    narrow = pltpu.VMEM((width, 2 * width), F32)
    mine_col = pl.BlockSpec(
        (rows, 1), lambda k, table, docs: ((k ^ table[0]) + table[1] * inner, 0)
    )
    def simple(kernel, name, outs, in_specs, out_specs, price):
        return call(kernel, name, outs, in_specs, out_specs, price, prefetch=0)

    def up_projection(weight, bias):
        return run(
            simple(
                up_kernel,
                "up",
                (shape((tokens, hidden_cols), BF16),) * 2,
                [plain(model), whole(hidden_cols, model), whole(1, hidden_cols)],
                [plain(hidden_cols)] * 2,
                cost(2 * tokens * model * hidden_cols, 5e6, 2 * tokens * hidden_cols),
            ),
            norm_two,
            weight,
            bias,
        )

    def down_back(weight, slope):
        return run(
            simple(
                down_back_kernel,
                "down_back",
                (shape((tokens, hidden_cols), BF16), shape((8, hidden_cols), F32)),
                [plain(model), whole(hidden_cols, model), plain(hidden_cols)],
                [plain(hidden_cols), whole(8, hidden_cols)],
                cost(2 * tokens * model * hidden_cols, 5e6),
            ),
            grad_all,
            weight,
            slope,
            gate=2,
        )

    def add(a, b):
        return (a.astype(F32) + b.astype(F32)).astype(BF16)

    def rest(total):
        step = QUARTERS
        while step < dp_size:
            total = add(total, swap(total, step, 0))
            step *= 2
        return total

    def add_three(a, b, c):
        return (a.astype(F32) + b.astype(F32) + c.astype(F32)).astype(BF16)

    class PairSum:
        def __init__(self, parts):
            self.kept, self.sent = parts
            self.bit = 1

        def start(self):
            self.moving = swap(now(self.sent), 0, self.bit)
            self.bit *= 2
            return self.moving

        def more(self):
            return self.bit < inner

        def add(self):
            def halve(a, b):
                total = add(a, b)
                return total[0::2], total[1::2]

            self.kept, self.sent = run(halve, self.kept, self.moving)

        def result(self):
            return self.kept[0], self.moving[0]

    def hidden_weights(active, hidden_grad, side, sums_row):
        return run(
            call(
                hidden_weights_kernel,
                "hidden_weights",
                (shape((2, pack_rows, model), BF16),) * 2,
                [
                    whole(tokens, hidden_cols),
                    whole(tokens, hidden_cols),
                    pl.BlockSpec((tokens, width), lambda k, table: (0, side))
                    if width % LANES == 0
                    else whole(tokens, width),
                    whole(tokens, model),
                    whole(tokens, model),
                    whole(8, hidden_cols),
                ],
                [whole(2, pack_rows, model)] * 2,
                cost(2 * tokens * model * (2 * hidden_cols + width), 9e6),
                scratch=[pltpu.VMEM((width, model), BF16)],
                steps=1,
            ),
            table,
            active,
            hidden_grad,
            merged if width % LANES == 0 else merged[:, side * width : (side + 1) * width],
            grad_all,
            norm_two,
            sums_row,
            gate=2,
        )

    x_blocks = [inputs] + [
        None if k & (k - 1) else swap(inputs, 0, k) for k in range(1, inner)
    ]
    first_pack = run(
        call(
            first_pack_kernel,
            "first_pack",
            shape((first_rows, first_cols), BF16),
            [
                pl.BlockSpec((model_part, qkv_cols), lambda k, table: (table[2], 0)),
                pl.BlockSpec((width, model_part), lambda k, table: (0, table[2])),
                whole(1, qkv_cols),
                whole(QUARTERS, 1, hidden_part),
            ],
            whole(first_rows, first_cols),
            cost(1e5, 4e5),
            steps=1,
        ),
        table,
        qkv_weight,
        dense_weight,
        own_bias,
        up_bias_parts,
    )
    first_mine = swap(first_pack, 0, inner)
    own_up, own_down, own_up_bias, second_pack = run(
        once(
            arrange_kernel,
            "arrange",
            (
                shape((hidden_cols, model), BF16),
                shape((hidden_cols, model), BF16),
                shape((1, hidden_cols), F32),
                shape((second_rows, model), BF16),
            ),
            scratch=[pltpu.VMEM((hidden_cols, model), BF16)],
        ),
        table,
        up_weight,
        down_weight,
        up_bias_parts,
        gate=3,
    )
    square = whole(LANES, LANES)
    keep, ahead, behind, mix_high, mix_low, turned_high, turned_low = run(
        call(
            prepare_kernel,
            "prepare",
            (shape((tokens, LANES), F32),) * 3 + (shape((LANES, LANES), BF16),) * 4,
            [whole(1, LANES), whole(HEAD_DIM, HEAD_DIM), pl.BlockSpec(memory_space=pl.ANY)],
            [plain(LANES)] * 3 + [square] * 4,
            cost(1e6, 2e6),
        ),
        table,
        after(rates, affine, docs_row),
        feature_omega,
        docs_col,
        gate=2,
    )

    for k in range(1, inner):
        if k & (k - 1):
            tick(x_blocks[k & (k - 1)])
            x_blocks[k] = swap(now(x_blocks[k & (k - 1)]), 0, k & -k)
    tick(first_mine, *x_blocks[1:])
    first_third, first_near = swap(now(first_mine), 2, 0), swap(now(first_mine), 1, 0)
    second_mine = swap(now(second_pack), 0, inner)
    grad_blocks = [out_grad] + [
        None if k & (k - 1) else swap(now(out_grad), 0, k) for k in range(1, inner)
    ]
    norm_one, norm_two, unit, own_feat, own_value, near_state = run(
        call(
            functools.partial(own_features_kernel, count, inner),
            "own_features",
            (
                shape((tokens, model), BF16),
                shape((tokens, model), BF16),
                shape((tokens, model), BF16),
                shape((tokens, 2 * width), F32),
                shape((tokens, width), BF16),
                shape((width, LANES), F32),
            ),
            [pl.BlockSpec(memory_space=pltpu.HBM)] * inner
            + [
                whole(4, model),
                whole(model, qkv_cols),
                whole(1, qkv_cols),
                moved(LANES),
                moved(LANES),
                moved(LANES),
                square,
                square,
                mine_col,
            ],
            [
                plain(model),
                plain(model),
                plain(model),
                plain(2 * width),
                plain(width),
                whole(width, LANES),
            ],
            cost(2 * tokens * model * qkv_cols, 12e6),
            prefetch=2,
            scratch=[
                narrow,
                pltpu.VMEM((2, rows, model), BF16),
                pltpu.SemaphoreType.DMA((2,)),
            ],
        ),
        table,
        docs,
        *x_blocks,
        affine,
        qkv_weight,
        own_bias,
        keep,
        ahead,
        behind,
        mix_high,
        mix_low,
        docs_col,
        gate=2 + inner,
    )
    tick(first_third, first_near)
    first_last = swap(now(first_third), 1, 0)
    own_active, own_slope = up_projection(own_up, own_up_bias)

    tick(first_last)
    far_qkv, far_dense, far_up_bias = run(
        once(
            collect_first_kernel,
            "collect_first",
            (
                shape((model, qkv_cols), BF16),
                shape((width, model), BF16),
                shape((1, hidden_cols), F32),
            ),
        ),
        table,
        first_mine,
        first_near,
        first_third,
        first_last,
        gate=1,
    )
    far_feat, far_value, state = run(
        call(
            functools.partial(far_features_kernel, count),
            "far_features",
            (
                shape((tokens, 2 * width), F32),
                shape((tokens, width), BF16),
                shape((2, width, LANES), F32),
            ),
            [
                plain(model),
                whole(model, qkv_cols),
                pl.BlockSpec((16, first_cols), lambda k, *s: ((model_part + width) // 16, 0)),
                moved(LANES),
                moved(LANES),
                moved(LANES),
                square,
                square,
                mine_col,
                whole(width, LANES),
            ],
            [plain(2 * width), plain(width), whole(2, width, LANES)],
            cost(2 * tokens * model * qkv_cols, 8e6),
            prefetch=2,
            scratch=[narrow],
        ),
        table,
        docs,
        norm_one,
        far_qkv,
        first_mine,
        keep,
        ahead,
        behind,
        mix_high,
        mix_low,
        docs_col,
        near_state,
        gate=2,
    )
    first_state = across(state, 0)
    for k in range(1, inner):
        if k & (k - 1):
            tick(first_state, grad_blocks[k & (k - 1)])
            grad_blocks[k] = swap(now(grad_blocks[k & (k - 1)]), 0, k & -k)
    block_row = pl.BlockSpec((1, 1, rows), lambda m, table, docs: (m + table[1] * inner, 0, 0))
    block_col = pl.BlockSpec((rows, 1), lambda m, table, docs: (m + table[1] * inner, 0))
    mixed, merged, inverse, states = run(
        call(
            functools.partial(forward_kernel, count),
            "attend",
            (
                shape((tokens, 2 * width), F32),
                shape((tokens, 2 * width), BF16),
                shape((tokens, 2 * width), F32),
                shape((inner, 2, width, 2 * width), F32),
            ),
            [
                moved(2 * width),
                moved(2 * width),
                moved(width),
                moved(width),
                block_col,
                block_row,
                whole(2, width, LANES),
            ],
            [
                moved(2 * width),
                moved(2 * width),
                moved(2 * width),
                pl.BlockSpec((1, 2, width, 2 * width), lambda m, *s: (m, 0, 0, 0)),
            ],
            cost(2 * count * tokens * rows * 800, 5e6),
            prefetch=2,
            scratch=[wide],
        ),
        table,
        docs,
        own_feat,
        far_feat,
        own_value,
        far_value,
        docs_col,
        docs_row,
        first_state,
        gate=2,
    )
    tick(second_mine)
    second_third, second_near = swap(now(second_mine), 2, 0), swap(now(second_mine), 1, 0)
    tick(*grad_blocks[1:])
    grad_all, grad_sums = run(
        once(
            collect_grad_kernel,
            "collect_grad",
            (shape((tokens, model), BF16), shape((8, model), F32)),
            prefetch=0,
        ),
        *grad_blocks,
        gate=1,
    )
    merged_grad, later = run(
        call(
            functools.partial(later_kernel, count),
            "later",
            (shape((tokens, 2 * width), F32), shape((2, width, LANES), F32)),
            [
                plain(model),
                whole(width, model),
                whole(width, model),
                plain(2 * width),
                plain(2 * width),
                plain(2 * width),
                plain(2 * width),
                mine_col,
            ],
            [plain(2 * width), whole(2, width, LANES)],
            cost(2 * count * tokens * 64 * 256, 5e6),
            prefetch=2,
            scratch=[wide],
        ),
        *(table, docs, grad_all, dense_weight, far_dense, own_feat, far_feat, mixed, inverse, docs_col),
        gate=2,
    )
    first_later = across(later, 1)
    tick(second_third)
    second_last = swap(now(second_third), 1, 0)
    own_hidden_grad, own_up_sums = down_back(own_down, own_slope)
    own_kept, own_sent = hidden_weights(own_active, own_hidden_grad, 0, own_up_sums)
    tick(second_last, second_near)
    own_got = swap(now(own_sent), 1, 0)
    far_up, far_down = run(
        once(
            collect_second_kernel,
            "collect_second",
            (shape((hidden_cols, model), BF16),) * 2,
            prefetch=0,
        ),
        second_mine,
        second_near,
        second_third,
        second_last,
    )
    far_active, far_slope = up_projection(far_up, far_up_bias)
    far_hidden_grad, far_up_sums = down_back(far_down, far_slope)
    far_kept, far_sent = hidden_weights(far_active, far_hidden_grad, 1, far_up_sums)
    tick(own_got, first_later)
    own_next = run(add, own_kept[1], own_got[1])
    tick()
    far_got = swap(now(far_sent), 1, 0)
    partial_out = run(
        simple(
            out_kernel,
            "out",
            (shape((inner // 2, rows, model), BF16),) * 2,
            [
                plain(2 * width),
                plain(hidden_cols),
                plain(hidden_cols),
                whole(width, model),
                whole(width, model),
                whole(hidden_cols, model),
                whole(hidden_cols, model),
            ],
            [whole(inner // 2, rows, model)] * 2,
            cost(4 * tokens * model * (width + hidden_cols), 8e6),
        ),
        merged,
        own_active,
        far_active,
        dense_weight,
        far_dense,
        own_down,
        far_down,
    )

    tick(far_got)
    far_next = run(add, far_kept[1], far_got[1])
    tick()
    far_cross = swap(now(far_next), 2, 0)
    out_sum = PairSum(partial_out)
    out_moving = out_sum.start()
    back = lambda cols: pl.BlockSpec((rows, cols), lambda m, table, docs: ((inner - 1 - m) ^ table[0], 0))
    back_straight = lambda cols: pl.BlockSpec((rows, cols), lambda m, *s: (inner - 1 - m, 0))
    own_pg, far_pg = run(
        call(
            functools.partial(backward_kernel, count),
            "attend_back",
            (shape((tokens, qkv_cols), BF16),) * 2,
            [
                back(2 * width),
                back(2 * width),
                back(width),
                back(width),
                back(2 * width),
                back(2 * width),
                back(2 * width),
                pl.BlockSpec(
                    (rows, 1), lambda m, table, docs: (inner - 1 - m + table[1] * inner, 0)
                ),
                pl.BlockSpec(
                    (1, 1, rows), lambda m, table, docs: (inner - 1 - m + table[1] * inner, 0, 0)
                ),
                pl.BlockSpec((1, 2, width, 2 * width), lambda m, *s: (inner - 1 - m, 0, 0, 0)),
                whole(2, width, LANES),
                back_straight(LANES),
                back_straight(LANES),
                back_straight(LANES),
                square,
                square,
            ],
            [back(qkv_cols), back(qkv_cols)],
            cost(2 * count * tokens * rows * 2000, 8e6),
            prefetch=2,
            scratch=[wide],
        ),
        table,
        docs,
        own_feat,
        far_feat,
        own_value,
        far_value,
        mixed,
        inverse,
        merged_grad,
        docs_col,
        docs_row,
        states,
        first_later,
        keep,
        ahead,
        behind,
        turned_high,
        turned_low,
        gate=8,
    )
    kept, sent = run(
        once(
            qkv_weights_kernel,
            "qkv_weights",
            (shape((4, model_part + 16, qkv_cols), BF16),) * 2,
            scratch=[pltpu.VMEM((model, qkv_cols), BF16)],
        ),
        table,
        own_pg,
        far_pg,
        norm_one,
        gate=3,
    )
    tick(far_cross)
    far_quad = run(add_three, far_kept[0], far_got[0], far_cross)
    tick()
    far_home = swap(now(far_quad), 0, inner)
    norm_grads = run(
        simple(
            norm_grad_kernel,
            "norm_grad",
            (shape((8, model), F32),) + (shape((inner // 2, rows, model), BF16),) * 2,
            [
                plain(qkv_cols),
                plain(qkv_cols),
                plain(hidden_cols),
                plain(hidden_cols),
                whole(model, qkv_cols),
                whole(model, qkv_cols),
                whole(hidden_cols, model),
                whole(hidden_cols, model),
                plain(model),
                whole(4, model),
                whole(8, model),
            ],
            [whole(8, model)] + [whole(inner // 2, rows, model)] * 2,
            cost(4 * tokens * model * (qkv_cols + hidden_cols), 12e6),
        ),
        own_pg,
        far_pg,
        own_hidden_grad,
        far_hidden_grad,
        qkv_weight,
        far_qkv,
        own_up,
        far_up,
        unit,
        affine,
        grad_sums,
        gate=8,
    )
    e_sum = PairSum(norm_grads[1:])
    steps = [(1 << k, 0) for k in range(dp_size.bit_length() - 1)]
    steps += [(0, 1 << k) for k in range(tensor_size.bit_length() - 1)]
    small = norm_grads[0]

    def small_start():
        return swap(now(small), *steps.pop(0))

    def small_add(moved):
        return run(lambda a, b: a + b, small, moved)

    tick(out_moving)
    out_sum.add()
    tick()
    e_moving = e_sum.start()
    out_moving = out_sum.start()
    got, own_cross = swap(now(sent), 1, 0), swap(now(own_next), 2, 0)
    tick(got)
    cross_sent = run(add, kept[2:], got[2:])
    tick()
    crossed = swap(now(cross_sent), 2, 0)
    tick(out_moving)
    while out_sum.more():
        out_sum.add()
        tick(out_sum.start())
    layer_out = run(
        once(finish_out_kernel, "finish_out", shape((rows, model), BF16), prefetch=0),
        inputs,
        out_bias.reshape(1, -1),
        *out_sum.result(),
        gate=2,
    )
    tick(crossed)
    far_piece = run(add_three, kept[1], got[1], crossed[1])
    own_piece = run(add_three, kept[0], got[0], crossed[0])
    tick()
    far_piece_home = swap(now(far_piece), 0, inner)
    tick(far_home, own_cross)
    own_quad = run(add_three, own_kept[0], own_got[0], own_cross)
    lower_mine = rest(run(add, own_quad, far_home))
    tick()
    lower_third, lower_near = swap(now(lower_mine), 2, 0), swap(now(lower_mine), 1, 0)
    tick(e_moving)
    e_sum.add()
    tick()
    e_moving = e_sum.start()
    moved_small = small_start()
    tick(far_piece_home, lower_near, moved_small)
    upper_mine = rest(run(add, own_piece, far_piece_home))
    small = small_add(moved_small)
    tick()
    upper_third, upper_near = swap(now(upper_mine), 2, 0), swap(now(upper_mine), 1, 0)
    moved_small = small_start()
    tick(e_moving)
    while e_sum.more():
        e_sum.add()
        tick(e_sum.start())
    input_grad = run(
        once(finish_in_kernel, "finish_in", shape((rows, model), F32), prefetch=0),
        inputs,
        out_grad,
        *e_sum.result(),
        gate=2,
    )
    tick(lower_third, moved_small)
    lower = (lower_mine, lower_near, lower_third, swap(now(lower_third), 1, 0))
    small = small_add(moved_small)
    tick(upper_third, upper_near)
    upper = (upper_mine, upper_near, upper_third, swap(now(upper_third), 1, 0))
    moved_small = small_start()
    tick(lower[3], moved_small)
    small = small_add(moved_small)
    tick()
    moved_small = small_start()
    up_grad, down_grad, dense_grad, up_bias_grad = run(
        once(
            finish_hidden_kernel,
            "finish_hidden",
            (
                shape((model, hidden_cols), F32),
                shape((hidden_cols, model), F32),
                shape((width, model), F32),
                shape((QUARTERS, 1, hidden_part), F32),
            ),
            scratch=[pltpu.VMEM((hidden_cols, model), F32)],
        ),
        table,
        *lower,
        gate=1,
    )
    tick(moved_small, upper[3])
    small = small_add(moved_small)
    tick()
    moved_small = small_start()
    qkv_grad, qkv_bias_grad = run(
        once(
            finish_qkv_kernel,
            "finish_qkv",
            (shape((model, qkv_cols), F32), shape((1, qkv_cols), F32)),
        ),
        table,
        *upper,
        gate=1,
    )

    small = small + moved_small
    while steps:
        tick()
        small = small_add(small_start())
    cols = model // tensor_size
    small = lax.dynamic_slice_in_dim(small, place * cols, cols, 1)

    return (
        layer_out,
        input_grad,
        qkv_grad,
        qkv_bias_grad.reshape(-1),
        dense_grad,
        up_grad,
        up_bias_grad.reshape(-1),
        down_grad,
        small[4],
        small[0],
        small[1],
        small[2],
        small[3],
    )


def solution(mesh):
    in_specs = (
        P(("dp", "tensor"), None),
        P(None, "tensor"),
        P("tensor"),
        P("tensor", None),
        P(None, "tensor"),
        P("tensor"),
        P("tensor", None),
        P(),
        P(),
        P(),
        P(),
        P(),
        P(),
        P("dp", None),
        P(("dp", "tensor"), None),
    )
    out_specs = (
        P(("dp", "tensor"), None),
        P(("dp", "tensor"), None),
        P(None, "tensor"),
        P("tensor"),
        P("tensor", None),
        P(None, "tensor"),
        P("tensor"),
        P("tensor", None),
        P("tensor"),
        P("tensor"),
        P("tensor"),
        P("tensor"),
        P("tensor"),
    )
    return jax.shard_map(
        functools.partial(on_device, mesh.shape["dp"], mesh.shape["tensor"]),
        mesh=mesh,
        in_specs=in_specs,
        out_specs=out_specs,
        check_vma=False,
    )
```

```python
import functools

import jax
import jax.numpy as jnp
import numpy as np
from jax import lax
from jax.experimental import pallas as pl
from jax.experimental.pallas import tpu as pltpu
from jax.sharding import PartitionSpec as P

HEAD_DIM = 64
ROT = 16
LANES = 128
EPS = 1e-05
EXACT = lax.Precision.HIGHEST
F32 = jnp.float32
BF16 = jnp.bfloat16
AXES = ("dp", "tensor")
VMEM_LIMIT = 16 * 1024 * 1024
QUARTERS = 4

NN = ((1,), (0,))
NT = ((1,), (1,))
TN = ((0,), (0,))


def dot(a, b, dims=NN, precision=None):
    return lax.dot_general(a, b, (dims, ((), ())), precision=precision, preferred_element_type=F32)


def halves(values):
    high = values.astype(BF16)
    return high, (values - high.astype(F32)).astype(BF16)


def lane_of(dims):
    return lax.broadcasted_iota(jnp.int32, dims, len(dims) - 1)


def prepare_kernel(table, rates, omega, docs_col, keep, ahead, behind, mix_high, mix_low, turned_high, turned_low):
    rows = keep.shape[0]
    start = (table[1] * pl.num_programs(0) + pl.program_id(0)) * rows
    places = start + lax.broadcasted_iota(jnp.int32, (rows, LANES), 0)
    angles = places.astype(F32) * rates[...]
    inner = lane_of((rows, LANES)) % HEAD_DIM
    cosine, sine = jnp.cos(angles), jnp.sin(angles)
    half = ROT // 2
    keep[...] = jnp.where(inner < ROT, cosine, 1.0)
    ahead[...] = jnp.where(inner < half, -sine, 0.0)
    behind[...] = jnp.where((inner >= half) & (inner < ROT), sine, 0.0)

    @pl.when(pl.program_id(0) == 0)
    def _():
        extent = HEAD_DIM
        n = lax.broadcasted_iota(jnp.int32, (LANES, LANES), 0)
        k = lax.broadcasted_iota(jnp.int32, (LANES, LANES), 1)
        same = (n // extent) == (k // extent)
        n, k = (n % extent).astype(F32), (k % extent).astype(F32)
        scale = jnp.where(k == 0, float(np.sqrt(1.0 / extent)), float(np.sqrt(2.0 / extent)))
        matrix = jnp.where(same, jnp.cos(np.pi * (n + 0.5) * k / extent) * scale, 0.0)
        row = jnp.concatenate([omega[...]] * 2, axis=1)
        spread = jnp.where(same, jnp.concatenate([row] * 2, axis=0), 0.0)
        mixing = dot(matrix, spread, precision=EXACT)
        mix_high[...], mix_low[...] = halves(mixing)
        turned_high[...], turned_low[...] = halves(mixing.T)


def turn(values, keep, ahead, behind, sign):
    half = ROT // 2
    moved = (
        pltpu.roll(values, LANES - half, axis=1) * ahead + pltpu.roll(values, half, axis=1) * behind
    )
    return values * keep + sign * moved


def mixed_dot(values, high, low):
    first, second = halves(values)
    return dot(first, high) + (dot(second, high) + dot(first, low))


def head_columns(values, which, count):
    parts = [
        values[:, (3 * j + which) * HEAD_DIM : (3 * j + which + 1) * HEAD_DIM] for j in range(count)
    ]
    return parts[0] if count == 1 else jnp.concatenate(parts, axis=1)


def masked_stack(values, count):
    if count == 1:
        return values
    lane = (lane_of(values.shape) % (count * HEAD_DIM)) // HEAD_DIM
    zero = jnp.zeros_like(values)
    return jnp.concatenate([jnp.where(lane == j, values, zero) for j in range(count)], axis=0)


def side_by_side(stack, count):
    rows = stack.shape[0] // count
    if count == 1:
        return stack
    return jnp.concatenate([stack[j * rows : (j + 1) * rows] for j in range(count)], axis=1)


def own_block(dims):
    rows = lax.broadcasted_iota(jnp.int32, dims, 0) // HEAD_DIM
    return rows == (lane_of(dims) % dims[0]) // HEAD_DIM


def compress(state, count):
    width = count * HEAD_DIM
    sides = []
    for base in (0, width):
        part = state[:, base : base + HEAD_DIM]
        for j in range(1, count):
            rows = lax.broadcasted_iota(jnp.int32, part.shape, 0) // HEAD_DIM
            here = state[:, base + j * HEAD_DIM : base + (j + 1) * HEAD_DIM]
            part = jnp.where(rows == j, here, part)
        sides.append(part)
    return jnp.concatenate(sides, axis=1)


def expand(packed, count):
    values, totals = packed[:, :HEAD_DIM], packed[:, HEAD_DIM:]
    wide = jnp.concatenate([values] * count + [totals] * count, axis=1)
    return jnp.where(own_block(wide.shape), wide, 0.0)


def project(count, one, weight, bias, turns, mix_high, mix_low, chosen, feat_out, value_out, state):
    width = count * HEAD_DIM
    projected = dot(one, weight) + bias
    value = head_columns(projected, 2, count).astype(BF16)
    pairs = [head_columns(projected, which, count) for which in (0, 1)]
    if count == 1:
        pairs = [jnp.concatenate(pairs, axis=1)]
    feats = []
    for pair in pairs:
        feats.append(jnp.exp(mixed_dot(turn(pair, *turns, 1.0), mix_high, mix_low)))
    feat = feats[0] if count == 1 else jnp.concatenate(feats, axis=1)
    feat_out[...] = feat
    value_out[...] = value
    key = jnp.where(chosen, feat[:, width:], 0.0).astype(BF16)
    state[...] += dot(key, jnp.concatenate([value, jnp.ones_like(value)], axis=1), TN)


def load_block(refs, keep, sems):
    def copy(k):
        return pltpu.make_async_copy(refs[k], keep.at[k % 2], sems.at[k % 2])

    for k in range(len(refs)):

        @pl.when(pl.program_id(0) == k)
        def _(k=k):
            if k == 0:
                copy(0).start()
            if k + 1 < len(refs):
                copy(k + 1).start()
            copy(k).wait()

    return keep[pl.program_id(0) % 2]


def own_features_kernel(count, blocks, table, docs, *refs):
    x_refs = refs[:blocks]
    (
        affine,
        weight,
        bias,
        keep,
        ahead,
        behind,
        mix_high,
        mix_low,
        docs_col,
        norm_one,
        norm_two,
        unit_out,
        feat_out,
        value_out,
        state_out,
        state,
        x_keep,
        x_sems,
    ) = refs[blocks:]

    @pl.when(pl.program_id(0) == 0)
    def _():
        state[...] = jnp.zeros_like(state)

    rows = x_keep.shape[1]
    x = load_block(x_refs, x_keep, x_sems).astype(F32)
    mean = jnp.mean(x, axis=-1, keepdims=True)
    centred = x - mean
    scale = lax.rsqrt(jnp.mean(centred * centred, axis=-1, keepdims=True) + EPS)
    unit = centred * scale
    one = (unit * affine[0:1] + affine[1:2]).astype(BF16)
    norm_one[...] = one
    norm_two[...] = (unit * affine[2:3] + affine[3:4]).astype(BF16)
    unit_out[...] = unit.astype(BF16)
    chosen = docs_col[...] == docs[(table[1] + 1) * blocks * rows - 1]
    project(
        count,
        one,
        weight[...],
        bias[...].astype(F32),
        (keep[...], ahead[...], behind[...]),
        mix_high[...],
        mix_low[...],
        chosen,
        feat_out,
        value_out,
        state,
    )

    @pl.when(pl.program_id(0) == pl.num_programs(0) - 1)
    def _():
        state_out[...] = compress(state[...], count)


def far_features_kernel(
    count,
    table,
    docs,
    norm_one,
    weight,
    bias,
    keep,
    ahead,
    behind,
    mix_high,
    mix_low,
    docs_col,
    near_state,
    feat_out,
    value_out,
    state_out,
    state,
):
    @pl.when(pl.program_id(0) == 0)
    def _():
        state[...] = jnp.zeros_like(state)

    rows = norm_one.shape[0]
    chosen = docs_col[...] == docs[(table[1] + 1) * pl.num_programs(0) * rows - 1]
    project(
        count,
        norm_one[...],
        weight[...],
        bias[0:1, : weight.shape[1]].astype(F32),
        (keep[...], ahead[...], behind[...]),
        mix_high[...],
        mix_low[...],
        chosen,
        feat_out,
        value_out,
        state,
    )

    @pl.when(pl.program_id(0) == pl.num_programs(0) - 1)
    def _():
        state_out[0] = near_state[...]
        state_out[1] = compress(state[...], count)


def allowed_pairs(docs_col, docs_row, count):
    size = docs_col.shape[0]
    rows = lax.broadcasted_iota(jnp.int32, (size, size), 0)
    cols = lax.broadcasted_iota(jnp.int32, (size, size), 1)
    allowed = ((docs_col == docs_row) & (rows >= cols)).astype(F32)
    return allowed if count == 1 else jnp.concatenate([allowed] * count, axis=0)


def forward_kernel(
    count,
    table,
    docs,
    own_feat,
    far_feat,
    own_value,
    far_value,
    docs_col,
    docs_row,
    first_state,
    mixed_out,
    merged_out,
    inverse_out,
    states_out,
    state,
):
    step = pl.program_id(0)
    width = count * HEAD_DIM
    rows = own_feat.shape[0]

    @pl.when(step == 0)
    def _():
        for side in range(2):
            state[side] = expand(first_state[1 - side], count)

    start = (table[1] * pl.num_programs(0) + step) * rows
    before = jnp.where(start > 0, docs[jnp.maximum(start - 1, 0)], -1)
    last = docs[start + rows - 1]
    kept = (last == before).astype(F32)
    allowed = allowed_pairs(docs_col[...], docs_row[0], count)
    carried = docs_col[...] == before
    chosen = docs_col[...] == last
    for side in range(2):
        feat_ref, value_ref = ((own_feat, own_value), (far_feat, far_value))[side]
        query = feat_ref[:, :width].astype(BF16)
        key = feat_ref[:, width:]
        value = value_ref[...]
        both = jnp.concatenate([value, jnp.ones_like(value)], axis=1)
        memory = state[side]
        states_out[0, side] = memory
        high, low = halves(memory)
        weights = (dot(masked_stack(query, count), key.astype(BF16), NT) * allowed).astype(BF16)
        sums = dot(side_by_side(weights, count), masked_stack(both, count)) + jnp.where(
            carried, dot(query, high) + dot(query, low), 0.0
        )
        inverse = 1.0 / sums[:, width:]
        mixed = sums[:, :width] * inverse
        mixed_out[:, side * width : (side + 1) * width] = mixed
        merged_out[:, side * width : (side + 1) * width] = mixed.astype(BF16)
        inverse_out[:, side * width : (side + 1) * width] = inverse
        picked = jnp.where(chosen, key, 0.0).astype(BF16)
        added = dot(picked, both, TN)
        state[side] = kept * memory + jnp.where(own_block(added.shape), added, 0.0)


def pair_grads(grad, inverse, mixed):
    part = (grad * inverse).astype(BF16)
    high, low = halves(-(part.astype(F32) * mixed))
    return part, high, low


def later_kernel(
    count,
    table,
    docs,
    grad_ref,
    own_dense,
    far_dense,
    own_feat,
    far_feat,
    mixed_ref,
    inverse_ref,
    docs_col,
    merged_grad,
    later_out,
    later,
):
    @pl.when(pl.program_id(0) == 0)
    def _():
        later[...] = jnp.zeros_like(later)

    width = count * HEAD_DIM
    rows = own_feat.shape[0]
    chosen = docs_col[...] == docs[table[1] * pl.num_programs(0) * rows]
    for side, dense in enumerate((own_dense, far_dense)):
        span = slice(side * width, (side + 1) * width)
        grad = dot(grad_ref[...], dense[...], NT)
        merged_grad[:, span] = grad
        part, high, low = pair_grads(grad, inverse_ref[:, span], mixed_ref[:, span])
        query = (own_feat, far_feat)[side][:, :width]
        query = jnp.where(chosen, query, 0.0).astype(BF16)
        later[side, :, :width] += dot(query, part, TN)
        later[side, :, width:] += dot(query, high, TN) + dot(query, low, TN)

    @pl.when(pl.program_id(0) == pl.num_programs(0) - 1)
    def _():
        for side in range(2):
            later_out[side] = compress(later[side], count)


def backward_kernel(
    count,
    table,
    docs,
    own_feat,
    far_feat,
    own_value,
    far_value,
    mixed_ref,
    inverse_ref,
    grad_ref,
    docs_col,
    docs_row,
    states_ref,
    first_later,
    keep,
    ahead,
    behind,
    turned_high,
    turned_low,
    own_out,
    far_out,
    later,
):
    blocks = pl.num_programs(0)
    step = blocks - 1 - pl.program_id(0)
    width = count * HEAD_DIM
    rows = own_feat.shape[0]

    @pl.when(pl.program_id(0) == 0)
    def _():
        for side in range(2):
            later[side] = expand(first_later[1 - side], count)

    start = (table[1] * blocks + step) * rows
    total = docs.shape[0]
    before = jnp.where(start > 0, docs[jnp.maximum(start - 1, 0)], -1)
    after = jnp.where(start + rows < total, docs[jnp.minimum(start + rows, total - 1)], -1)
    first = docs[start]
    kept = (first == after).astype(F32)
    allowed = allowed_pairs(docs_col[...], docs_row[0], count)
    carried = docs_col[...] == before
    linked = docs_col[...] == after
    chosen = docs_col[...] == first
    for side in range(2):
        span = slice(side * width, (side + 1) * width)
        feat = (own_feat, far_feat)[side][...]
        query, key = feat[:, :width].astype(BF16), feat[:, width:].astype(BF16)
        value = (own_value, far_value)[side][...]
        ones = jnp.ones_like(value)
        both = jnp.concatenate([value, ones], axis=1)
        part, high, low = pair_grads(grad_ref[:, span], inverse_ref[:, span], mixed_ref[:, span])
        first_two = jnp.concatenate([part, high], axis=1)
        queries = masked_stack(query, count)
        weights = (dot(queries, key, NT) * allowed).astype(BF16)
        weight_grad = dot(masked_stack(first_two, count), both, NT)
        weight_grad += dot(masked_stack(low, count), ones, NT)
        weight_grad = (weight_grad * allowed).astype(BF16)
        mem_high, mem_low = halves(states_ref[0, side])
        late = later[side]
        late_high, late_low = halves(late)
        query_grad = dot(side_by_side(weight_grad, count), masked_stack(key, count)) + jnp.where(
            carried,
            dot(first_two, mem_high, NT) + dot(first_two, mem_low, NT) + dot(low, mem_high[:, width:], NT),
            0.0,
        )
        key_grad = dot(weight_grad, queries, TN) + jnp.where(
            linked, dot(both, late_high, NT) + dot(both, late_low, NT), 0.0
        )
        value_grad = dot(weights, masked_stack(part, count), TN) + jnp.where(
            linked, dot(key, late_high[:, :width]) + dot(key, late_low[:, :width]), 0.0
        )
        picked = jnp.where(chosen, query.astype(F32), 0.0).astype(BF16)
        block = own_block(late.shape)
        added = jnp.concatenate(
            [dot(picked, part, TN), dot(picked, high, TN) + dot(picked, low, TN)], axis=1
        )
        later[side] = kept * late + jnp.where(block, added, 0.0)
        inner = jnp.concatenate([query_grad, key_grad], axis=1) * feat
        pairs = []
        for base in range(0, 2 * width, LANES):
            pair = mixed_dot(inner[:, base : base + LANES], turned_high[...], turned_low[...])
            pairs.append(turn(pair, keep[...], ahead[...], behind[...], -1.0))
        flat = pairs[0] if count == 1 else jnp.concatenate(pairs, axis=1)
        pieces = []
        for j in range(count):
            lanes = slice(j * HEAD_DIM, (j + 1) * HEAD_DIM)
            pieces += [flat[:, :width][:, lanes], flat[:, width:][:, lanes], value_grad[:, lanes]]
        out = own_out if side == 0 else far_out
        out[...] = jnp.concatenate(pieces, axis=1).astype(BF16)


def up_kernel(norm_ref, weight, bias, active_out, slope_out):
    hidden = dot(norm_ref[...], weight[...], NT) + bias[...]
    normal = 0.5 * (1.0 + lax.erf(hidden * 0.7071067811865476))
    density = jnp.exp(-0.5 * hidden * hidden) * 0.3989422804014327
    active_out[...] = (hidden * normal).astype(BF16)
    slope_out[...] = (normal + hidden * density).astype(BF16)


def down_back_kernel(grad_ref, weight, slope, hidden_out, sums_out):
    hidden = (dot(grad_ref[...], weight[...], NT) * slope[...].astype(F32)).astype(BF16)
    hidden_out[...] = hidden

    @pl.when(pl.program_id(0) == 0)
    def _():
        sums_out[...] = jnp.zeros_like(sums_out)

    sums_out[0:1] += jnp.sum(hidden.astype(F32), axis=0, keepdims=True)


def out_kernel(merged, own_active, far_active, own_dense, far_dense, own_down, far_down, *outs):
    width = own_dense.shape[0]
    total = dot(own_active[...], own_down[...]) + dot(far_active[...], far_down[...])
    total += dot(merged[:, :width], own_dense[...]) + dot(merged[:, width:], far_dense[...])
    write_block(outs, total.astype(BF16))


def write_block(outs, values):
    kept, sent = outs
    for k in range(2 * kept.shape[0]):

        @pl.when(pl.program_id(0) == k)
        def _(k=k):
            (sent if k % 2 else kept)[k // 2] = values


def norm_grad_kernel(
    own_pg,
    far_pg,
    own_hg,
    far_hg,
    own_qkv,
    far_qkv,
    own_up,
    far_up,
    unit_ref,
    affine,
    grad_sums,
    sums_out,
    *outs,
):
    @pl.when(pl.program_id(0) == 0)
    def _():
        sums_out[...] = jnp.zeros_like(sums_out)
        sums_out[4:5] = grad_sums[0:1]

    down = lambda values: jnp.sum(values, axis=0, keepdims=True)
    unit = unit_ref[...].astype(F32)
    one = dot(own_pg[...], own_qkv[...], NT) + dot(far_pg[...], far_qkv[...], NT)
    sums_out[0:1] += down(one * unit)
    sums_out[1:2] += down(one)
    two = dot(own_hg[...], own_up[...]) + dot(far_hg[...], far_up[...])
    sums_out[2:3] += down(two * unit)
    sums_out[3:4] += down(two)
    write_block(outs, (one * affine[0:1] + two * affine[2:3]).astype(BF16))


def first_pack_kernel(table, weight, dense, bias, up_bias, out):
    rows, small = weight.shape[0], dense.shape[0]
    if out.shape[1] > min(weight.shape[1], dense.shape[1]):
        out[...] = jnp.zeros_like(out)
    out[:rows, : weight.shape[1]] = weight[...]
    out[rows : rows + small, : dense.shape[1]] = dense[...]
    first = bias[...].astype(F32)
    second = up_bias[table[2]].astype(F32)
    if first.shape[1] > second.shape[1]:
        rest = jnp.zeros((1, first.shape[1] - second.shape[1]), F32)
        second = jnp.concatenate([second, rest], axis=1)
    row = lax.broadcasted_iota(jnp.int32, (16, first.shape[1]), 0)
    out[rows + small :, : first.shape[1]] = jnp.where(row < 8, first, second).astype(BF16)


def arrange_kernel(table, up, down, bias, own_up, own_down, own_bias, pack, turned):
    part = table[2]
    step = down.shape[0] // QUARTERS
    turned[...] = up[...].T
    for k in range(QUARTERS):
        begin = pl.multiple_of((part ^ k) * step, step)
        own_up[k * step : (k + 1) * step] = turned[pl.ds(begin, step)]
        own_down[k * step : (k + 1) * step] = down[pl.ds(begin, step)]
    own_bias[...] = jnp.concatenate([bias[part ^ k].astype(F32) for k in range(QUARTERS)], axis=1)
    pack[:step] = own_up[:step]
    pack[step:] = own_down[:step]


def collect_first_kernel(table, mine, near, third, last, far_qkv, far_dense, far_up_bias):
    part = table[2]
    step = far_qkv.shape[0] // QUARTERS
    small = far_dense.shape[0]
    hidden = far_up_bias.shape[1] // QUARTERS
    biases = []
    for k, ref in enumerate((mine, near, third, last)):
        begin = pl.multiple_of((part ^ k) * step, step)
        far_qkv[pl.ds(begin, step)] = ref[:step, : far_qkv.shape[1]]
        far_dense[:, pl.ds(begin, step)] = ref[step : step + small, :step]
        tail = ref[step + small :].astype(F32)
        biases.append(tail[8:9, :hidden])
    far_up_bias[...] = jnp.concatenate(biases, axis=1)


def collect_second_kernel(mine, near, third, last, far_up, far_down):
    step = mine.shape[0] // 2
    for k, ref in enumerate((mine, near, third, last)):
        far_up[k * step : (k + 1) * step] = ref[:step]
        far_down[k * step : (k + 1) * step] = ref[step:]


def collect_grad_kernel(*refs):
    blocks, (whole, sums) = refs[:-2], refs[-2:]
    rows = blocks[0].shape[0]
    for k, ref in enumerate(blocks):
        whole[k * rows : (k + 1) * rows] = ref[...]
    sums[...] = jnp.zeros_like(sums)
    sums[0:1] = jnp.sum(blocks[0][...].astype(F32), axis=0, keepdims=True)


def bias_rows(values, cols):
    tile = jnp.zeros((16, values.shape[1]), F32)
    row = lax.broadcasted_iota(jnp.int32, tile.shape, 0)
    high = values.astype(BF16).astype(F32)
    tile = jnp.where(row == 0, high, jnp.where(row == 1, values - high, tile)).astype(BF16)
    if values.shape[1] == cols:
        return tile
    return jnp.concatenate([tile, jnp.zeros((16, cols - values.shape[1]), BF16)], axis=1)


def hidden_weights_kernel(
    table, active, hidden_grad, merged, grad, norm_two, hidden_sums, kept, sent, dense
):
    part = table[2]
    step, small = active.shape[1] // QUARTERS, merged.shape[1] // QUARTERS
    cols = kept.shape[2]
    dense[...] = dot(merged[...], grad[...], TN).astype(BF16)
    down = dot(active[...], grad[...], TN).astype(BF16)
    up = dot(hidden_grad[...], norm_two[...], TN).astype(BF16)
    for k in range(QUARTERS):
        out = (kept, sent)[k % 2].at[k // 2]
        span = slice(k * step, (k + 1) * step)
        out[:step] = up[span]
        out[step : 2 * step] = down[span]
        begin = pl.multiple_of((part ^ k) * small, small)
        out[2 * step : 2 * step + small] = dense[pl.ds(begin, small)]
        out[2 * step + small :] = bias_rows(hidden_sums[0:1, span], cols)


def qkv_weights_kernel(table, own_pg, far_pg, norm_one, kept, sent, full):
    part = table[2]
    cols = kept.shape[2]
    step = full.shape[0] // QUARTERS
    for side, grad in enumerate((own_pg, far_pg)):
        full[...] = dot(norm_one[...], grad[...], TN).astype(BF16)
        tail = bias_rows(jnp.sum(grad[...].astype(F32), axis=0, keepdims=True), cols)
        for k in range(QUARTERS):
            out = (kept, sent)[k % 2].at[2 * (k // 2) + side]
            begin = pl.multiple_of((part ^ k) * step, step)
            out[:step] = full[pl.ds(begin, step)]
            out[step:] = tail


def finish_hidden_kernel(
    table, mine, near, third, last, up_grad, down_grad, dense_grad, bias_grad, turned
):
    part = table[2]
    step, small = down_grad.shape[0] // QUARTERS, dense_grad.shape[0] // QUARTERS
    size = mine.shape[0]
    for k, ref in enumerate((mine, near, third, last)):
        begin = pl.multiple_of((part ^ k) * step, step)
        turned[pl.ds(begin, step)] = ref[:step].astype(F32)
        down_grad[pl.ds(begin, step)] = ref[step : 2 * step].astype(F32)
        begin = pl.multiple_of((part ^ k) * small, small)
        dense_grad[pl.ds(begin, small)] = ref[2 * step : 2 * step + small].astype(F32)
        tail = ref[2 * step + small : size].astype(F32)
        bias_grad[part ^ k] = tail[0:1, :step] + tail[1:2, :step]
    up_grad[...] = turned[...].T


def finish_qkv_kernel(table, mine, near, third, last, weight_grad, bias_grad):
    part = table[2]
    step = weight_grad.shape[0] // QUARTERS
    for k, ref in enumerate((mine, near, third, last)):
        begin = pl.multiple_of((part ^ k) * step, step)
        weight_grad[pl.ds(begin, step)] = ref[:step].astype(F32)
    tail = mine[step:].astype(F32)
    bias_grad[...] = tail[0:1] + tail[1:2]


def finish_out_kernel(x_ref, bias, *refs):
    parts, out = refs[:-1], refs[-1]
    total = x_ref[...].astype(F32) + bias[...].astype(F32)
    for ref in parts:
        total += ref[...].astype(F32)
    out[...] = total.astype(BF16)


def finish_in_kernel(x_ref, grad_ref, *refs):
    parts, out = refs[:-1], refs[-1]
    x = x_ref[...].astype(F32)
    mean = jnp.mean(x, axis=-1, keepdims=True)
    centred = x - mean
    scale = lax.rsqrt(jnp.mean(centred * centred, axis=-1, keepdims=True) + EPS)
    unit = centred * scale
    total = parts[0][...].astype(F32)
    for ref in parts[1:]:
        total += ref[...].astype(F32)
    along = jnp.mean(total * unit, axis=-1, keepdims=True)
    out[...] = grad_ref[...].astype(F32) + scale * (
        total - jnp.mean(total, axis=-1, keepdims=True) - unit * along
    )


def params():
    return pltpu.CompilerParams(
        dimension_semantics=("arbitrary",), vmem_limit_bytes=VMEM_LIMIT
    )


def after(value, *others):
    return lax.optimization_barrier((value,) + others)[0]


def shape(dims, kind):
    return jax.ShapeDtypeStruct(dims, kind)


def cost(flops, nbytes, trans=0):
    return pl.CostEstimate(flops=1000, bytes_accessed=1000, transcendentals=0)


def on_device(
    dp_size,
    tensor_size,
    inputs,
    qkv_weight,
    qkv_bias,
    dense_weight,
    up_weight,
    up_bias,
    down_weight,
    out_bias,
    gain_one,
    shift_one,
    gain_two,
    shift_two,
    feature_omega,
    doc_ids,
    out_grad,
):
    rows, model = inputs.shape
    inner = tensor_size // 2
    tokens = rows * inner
    qkv_cols = qkv_weight.shape[1]
    count = qkv_cols // (3 * HEAD_DIM)
    width = count * HEAD_DIM
    hidden_cols = up_weight.shape[1]
    hidden_part, model_part = hidden_cols // QUARTERS, model // QUARTERS
    member = lax.axis_index("dp")
    place = lax.axis_index("tensor")
    half, slot = place // inner, place % inner
    part = member % QUARTERS

    def swap(values, over_dp, over_tensor):
        pairs = [
            (p * tensor_size + t, (p ^ over_dp) * tensor_size + (t ^ over_tensor))
            for p in range(dp_size)
            for t in range(tensor_size)
        ]
        return lax.ppermute(values, AXES, pairs)

    def across(values, source_half):
        pairs = [
            (p * tensor_size + source_half * inner + t, p * tensor_size + (1 - source_half) * inner + t)
            for p in range(dp_size)
            for t in range(inner)
        ]
        return lax.ppermute(values, AXES, pairs)

    def gather(block):
        return [block] + [swap(block, 0, k) for k in range(1, inner)]

    line, due = [], [()]

    def run(step, *operands, gate=0):
        operands = list(operands)
        held = tuple(line[-1:]) + due[0]
        if held:
            operands[gate] = after(operands[gate], *held)
        result = step(*operands)
        line.append(result[0] if isinstance(result, (tuple, list)) else result)
        return result

    def tick(*arrived):
        due[0] = tuple(arrived) + tuple(line[-1:])

    def now(values):
        return after(values, *due[0])

    table = jnp.stack([slot, half, part]).astype(jnp.int32)
    plain = lambda cols: pl.BlockSpec((rows, cols), lambda k, *s: (k, 0))
    moved = lambda cols: pl.BlockSpec((rows, cols), lambda k, table, *s: (k ^ table[0], 0))
    whole = lambda *dims: pl.BlockSpec(dims, lambda k, *s: (0,) * len(dims))
    spec = lambda values: whole(*values.shape)

    def call(kernel, name, outs, in_specs, out_specs, price, prefetch=1, scratch=(), steps=inner):
        return pl.pallas_call(
            kernel,
            out_shape=outs,
            grid_spec=pltpu.PrefetchScalarGridSpec(
                num_scalar_prefetch=prefetch,
                grid=(steps,),
                in_specs=in_specs,
                out_specs=out_specs,
                scratch_shapes=list(scratch),
            ),
            compiler_params=params(),
            cost_estimate=price,
            name=name,
        )

    def once(kernel, name, outs, prefetch=1, scratch=()):
        single = not isinstance(outs, (tuple, list))
        listed = (outs,) if single else tuple(outs)

        def step(*operands):
            result = call(
                kernel,
                name,
                listed,
                [spec(v) for v in operands[prefetch:]],
                [whole(*v.shape) for v in listed],
                cost(0, 0),
                prefetch,
                scratch,
                1,
            )(*operands)
            return result[0] if single else result

        return step

    first_rows, first_cols = model_part + width + 16, max(qkv_cols, model_part)
    docs = doc_ids.reshape(-1)
    docs_col = docs.reshape(-1, 1)
    docs_row = docs.reshape(tensor_size, 1, rows)
    affine = jnp.stack([gain_one, shift_one, gain_two, shift_two]).astype(F32)
    lane = np.arange(LANES) % HEAD_DIM
    rates = np.where(lane < ROT, 10000.0 ** (-(lane % (ROT // 2)) * 2.0 / ROT), 0.0)
    rates = jnp.asarray(rates[None, :], F32)
    own_bias = qkv_bias.reshape(1, -1)
    up_bias_parts = up_bias.reshape(QUARTERS, 1, hidden_part)

    dense_part = width // QUARTERS
    pack_rows = 2 * hidden_part + dense_part + 16
    second_rows = 2 * hidden_part
    wide = pltpu.VMEM((2, width, 2 * width), F32)
    narrow = pltpu.VMEM((width, 2 * width), F32)
    mine_col = pl.BlockSpec(
        (rows, 1), lambda k, table, docs: ((k ^ table[0]) + table[1] * inner, 0)
    )
    def simple(kernel, name, outs, in_specs, out_specs, price):
        return call(kernel, name, outs, in_specs, out_specs, price, prefetch=0)

    def up_projection(weight, bias):
        return run(
            simple(
                up_kernel,
                "up",
                (shape((tokens, hidden_cols), BF16),) * 2,
                [plain(model), whole(hidden_cols, model), whole(1, hidden_cols)],
                [plain(hidden_cols)] * 2,
                cost(2 * tokens * model * hidden_cols, 5e6, 2 * tokens * hidden_cols),
            ),
            norm_two,
            weight,
            bias,
        )

    def down_back(weight, slope):
        return run(
            simple(
                down_back_kernel,
                "down_back",
                (shape((tokens, hidden_cols), BF16), shape((8, hidden_cols), F32)),
                [plain(model), whole(hidden_cols, model), plain(hidden_cols)],
                [plain(hidden_cols), whole(8, hidden_cols)],
                cost(2 * tokens * model * hidden_cols, 5e6),
            ),
            grad_all,
            weight,
            slope,
            gate=2,
        )

    def add(a, b):
        return (a.astype(F32) + b.astype(F32)).astype(BF16)

    def rest(total):
        step = QUARTERS
        while step < dp_size:
            total = add(total, swap(total, step, 0))
            step *= 2
        return total

    def add_three(a, b, c):
        return (a.astype(F32) + b.astype(F32) + c.astype(F32)).astype(BF16)

    class PairSum:
        def __init__(self, parts):
            self.kept, self.sent = parts
            self.bit = 1

        def start(self):
            self.moving = swap(now(self.sent), 0, self.bit)
            self.bit *= 2
            return self.moving

        def more(self):
            return self.bit < inner

        def add(self):
            def halve(a, b):
                total = add(a, b)
                return total[0::2], total[1::2]

            self.kept, self.sent = run(halve, self.kept, self.moving)

        def result(self):
            return self.kept[0], self.moving[0]

    def hidden_weights(active, hidden_grad, side, sums_row):
        return run(
            call(
                hidden_weights_kernel,
                "hidden_weights",
                (shape((2, pack_rows, model), BF16),) * 2,
                [
                    whole(tokens, hidden_cols),
                    whole(tokens, hidden_cols),
                    pl.BlockSpec((tokens, width), lambda k, table: (0, side))
                    if width % LANES == 0
                    else whole(tokens, width),
                    whole(tokens, model),
                    whole(tokens, model),
                    whole(8, hidden_cols),
                ],
                [whole(2, pack_rows, model)] * 2,
                cost(2 * tokens * model * (2 * hidden_cols + width), 9e6),
                scratch=[pltpu.VMEM((width, model), BF16)],
                steps=1,
            ),
            table,
            active,
            hidden_grad,
            merged if width % LANES == 0 else merged[:, side * width : (side + 1) * width],
            grad_all,
            norm_two,
            sums_row,
            gate=2,
        )

    x_blocks = [inputs] + [
        None if k & (k - 1) else swap(inputs, 0, k) for k in range(1, inner)
    ]
    first_pack = run(
        call(
            first_pack_kernel,
            "first_pack",
            shape((first_rows, first_cols), BF16),
            [
                pl.BlockSpec((model_part, qkv_cols), lambda k, table: (table[2], 0)),
                pl.BlockSpec((width, model_part), lambda k, table: (0, table[2])),
                whole(1, qkv_cols),
                whole(QUARTERS, 1, hidden_part),
            ],
            whole(first_rows, first_cols),
            cost(1e5, 4e5),
            steps=1,
        ),
        table,
        qkv_weight,
        dense_weight,
        own_bias,
        up_bias_parts,
    )
    first_mine = swap(first_pack, 0, inner)
    own_up, own_down, own_up_bias, second_pack = run(
        once(
            arrange_kernel,
            "arrange",
            (
                shape((hidden_cols, model), BF16),
                shape((hidden_cols, model), BF16),
                shape((1, hidden_cols), F32),
                shape((second_rows, model), BF16),
            ),
            scratch=[pltpu.VMEM((hidden_cols, model), BF16)],
        ),
        table,
        up_weight,
        down_weight,
        up_bias_parts,
        gate=3,
    )
    square = whole(LANES, LANES)
    keep, ahead, behind, mix_high, mix_low, turned_high, turned_low = run(
        call(
            prepare_kernel,
            "prepare",
            (shape((tokens, LANES), F32),) * 3 + (shape((LANES, LANES), BF16),) * 4,
            [whole(1, LANES), whole(HEAD_DIM, HEAD_DIM), pl.BlockSpec(memory_space=pl.ANY)],
            [plain(LANES)] * 3 + [square] * 4,
            cost(1e6, 2e6),
        ),
        table,
        after(rates, affine, docs_row),
        feature_omega,
        docs_col,
        gate=2,
    )

    for k in range(1, inner):
        if k & (k - 1):
            tick(x_blocks[k & (k - 1)])
            x_blocks[k] = swap(now(x_blocks[k & (k - 1)]), 0, k & -k)
    tick(first_mine, *x_blocks[1:])
    first_third, first_near = swap(now(first_mine), 2, 0), swap(now(first_mine), 1, 0)
    second_mine = swap(now(second_pack), 0, inner)
    grad_blocks = [out_grad] + [
        None if k & (k - 1) else swap(now(out_grad), 0, k) for k in range(1, inner)
    ]
    norm_one, norm_two, unit, own_feat, own_value, near_state = run(
        call(
            functools.partial(own_features_kernel, count, inner),
            "own_features",
            (
                shape((tokens, model), BF16),
                shape((tokens, model), BF16),
                shape((tokens, model), BF16),
                shape((tokens, 2 * width), F32),
                shape((tokens, width), BF16),
                shape((width, LANES), F32),
            ),
            [pl.BlockSpec(memory_space=pltpu.HBM)] * inner
            + [
                whole(4, model),
                whole(model, qkv_cols),
                whole(1, qkv_cols),
                moved(LANES),
                moved(LANES),
                moved(LANES),
                square,
                square,
                mine_col,
            ],
            [
                plain(model),
                plain(model),
                plain(model),
                plain(2 * width),
                plain(width),
                whole(width, LANES),
            ],
            cost(2 * tokens * model * qkv_cols, 12e6),
            prefetch=2,
            scratch=[
                narrow,
                pltpu.VMEM((2, rows, model), BF16),
                pltpu.SemaphoreType.DMA((2,)),
            ],
        ),
        table,
        docs,
        *x_blocks,
        affine,
        qkv_weight,
        own_bias,
        keep,
        ahead,
        behind,
        mix_high,
        mix_low,
        docs_col,
        gate=2 + inner,
    )
    tick(first_third, first_near)
    first_last = swap(now(first_third), 1, 0)
    own_active, own_slope = up_projection(own_up, own_up_bias)

    tick(first_last)
    far_qkv, far_dense, far_up_bias = run(
        once(
            collect_first_kernel,
            "collect_first",
            (
                shape((model, qkv_cols), BF16),
                shape((width, model), BF16),
                shape((1, hidden_cols), F32),
            ),
        ),
        table,
        first_mine,
        first_near,
        first_third,
        first_last,
        gate=1,
    )
    far_feat, far_value, state = run(
        call(
            functools.partial(far_features_kernel, count),
            "far_features",
            (
                shape((tokens, 2 * width), F32),
                shape((tokens, width), BF16),
                shape((2, width, LANES), F32),
            ),
            [
                plain(model),
                whole(model, qkv_cols),
                pl.BlockSpec((16, first_cols), lambda k, *s: ((model_part + width) // 16, 0)),
                moved(LANES),
                moved(LANES),
                moved(LANES),
                square,
                square,
                mine_col,
                whole(width, LANES),
            ],
            [plain(2 * width), plain(width), whole(2, width, LANES)],
            cost(2 * tokens * model * qkv_cols, 8e6),
            prefetch=2,
            scratch=[narrow],
        ),
        table,
        docs,
        norm_one,
        far_qkv,
        first_mine,
        keep,
        ahead,
        behind,
        mix_high,
        mix_low,
        docs_col,
        near_state,
        gate=2,
    )
    first_state = across(state, 0)
    for k in range(1, inner):
        if k & (k - 1):
            tick(first_state, grad_blocks[k & (k - 1)])
            grad_blocks[k] = swap(now(grad_blocks[k & (k - 1)]), 0, k & -k)
    block_row = pl.BlockSpec((1, 1, rows), lambda m, table, docs: (m + table[1] * inner, 0, 0))
    block_col = pl.BlockSpec((rows, 1), lambda m, table, docs: (m + table[1] * inner, 0))
    mixed, merged, inverse, states = run(
        call(
            functools.partial(forward_kernel, count),
            "attend",
            (
                shape((tokens, 2 * width), F32),
                shape((tokens, 2 * width), BF16),
                shape((tokens, 2 * width), F32),
                shape((inner, 2, width, 2 * width), F32),
            ),
            [
                moved(2 * width),
                moved(2 * width),
                moved(width),
                moved(width),
                block_col,
                block_row,
                whole(2, width, LANES),
            ],
            [
                moved(2 * width),
                moved(2 * width),
                moved(2 * width),
                pl.BlockSpec((1, 2, width, 2 * width), lambda m, *s: (m, 0, 0, 0)),
            ],
            cost(2 * count * tokens * rows * 800, 5e6),
            prefetch=2,
            scratch=[wide],
        ),
        table,
        docs,
        own_feat,
        far_feat,
        own_value,
        far_value,
        docs_col,
        docs_row,
        first_state,
        gate=2,
    )
    tick(second_mine)
    second_third, second_near = swap(now(second_mine), 2, 0), swap(now(second_mine), 1, 0)
    tick(*grad_blocks[1:])
    grad_all, grad_sums = run(
        once(
            collect_grad_kernel,
            "collect_grad",
            (shape((tokens, model), BF16), shape((8, model), F32)),
            prefetch=0,
        ),
        *grad_blocks,
        gate=1,
    )
    merged_grad, later = run(
        call(
            functools.partial(later_kernel, count),
            "later",
            (shape((tokens, 2 * width), F32), shape((2, width, LANES), F32)),
            [
                plain(model),
                whole(width, model),
                whole(width, model),
                plain(2 * width),
                plain(2 * width),
                plain(2 * width),
                plain(2 * width),
                mine_col,
            ],
            [plain(2 * width), whole(2, width, LANES)],
            cost(2 * count * tokens * 64 * 256, 5e6),
            prefetch=2,
            scratch=[wide],
        ),
        *(table, docs, grad_all, dense_weight, far_dense, own_feat, far_feat, mixed, inverse, docs_col),
        gate=2,
    )
    first_later = across(later, 1)
    tick(second_third)
    second_last = swap(now(second_third), 1, 0)
    own_hidden_grad, own_up_sums = down_back(own_down, own_slope)
    own_kept, own_sent = hidden_weights(own_active, own_hidden_grad, 0, own_up_sums)
    tick(second_last, second_near)
    own_got = swap(now(own_sent), 1, 0)
    far_up, far_down = run(
        once(
            collect_second_kernel,
            "collect_second",
            (shape((hidden_cols, model), BF16),) * 2,
            prefetch=0,
        ),
        second_mine,
        second_near,
        second_third,
        second_last,
    )
    far_active, far_slope = up_projection(far_up, far_up_bias)
    far_hidden_grad, far_up_sums = down_back(far_down, far_slope)
    far_kept, far_sent = hidden_weights(far_active, far_hidden_grad, 1, far_up_sums)
    tick(own_got, first_later)
    own_next = run(add, own_kept[1], own_got[1])
    tick()
    far_got = swap(now(far_sent), 1, 0)
    partial_out = run(
        simple(
            out_kernel,
            "out",
            (shape((inner // 2, rows, model), BF16),) * 2,
            [
                plain(2 * width),
                plain(hidden_cols),
                plain(hidden_cols),
                whole(width, model),
                whole(width, model),
                whole(hidden_cols, model),
                whole(hidden_cols, model),
            ],
            [whole(inner // 2, rows, model)] * 2,
            cost(4 * tokens * model * (width + hidden_cols), 8e6),
        ),
        merged,
        own_active,
        far_active,
        dense_weight,
        far_dense,
        own_down,
        far_down,
    )

    tick(far_got)
    far_next = run(add, far_kept[1], far_got[1])
    tick()
    far_cross = swap(now(far_next), 2, 0)
    out_sum = PairSum(partial_out)
    out_moving = out_sum.start()
    back = lambda cols: pl.BlockSpec((rows, cols), lambda m, table, docs: ((inner - 1 - m) ^ table[0], 0))
    back_straight = lambda cols: pl.BlockSpec((rows, cols), lambda m, *s: (inner - 1 - m, 0))
    own_pg, far_pg = run(
        call(
            functools.partial(backward_kernel, count),
            "attend_back",
            (shape((tokens, qkv_cols), BF16),) * 2,
            [
                back(2 * width),
                back(2 * width),
                back(width),
                back(width),
                back(2 * width),
                back(2 * width),
                back(2 * width),
                pl.BlockSpec(
                    (rows, 1), lambda m, table, docs: (inner - 1 - m + table[1] * inner, 0)
                ),
                pl.BlockSpec(
                    (1, 1, rows), lambda m, table, docs: (inner - 1 - m + table[1] * inner, 0, 0)
                ),
                pl.BlockSpec((1, 2, width, 2 * width), lambda m, *s: (inner - 1 - m, 0, 0, 0)),
                whole(2, width, LANES),
                back_straight(LANES),
                back_straight(LANES),
                back_straight(LANES),
                square,
                square,
            ],
            [back(qkv_cols), back(qkv_cols)],
            cost(2 * count * tokens * rows * 2000, 8e6),
            prefetch=2,
            scratch=[wide],
        ),
        table,
        docs,
        own_feat,
        far_feat,
        own_value,
        far_value,
        mixed,
        inverse,
        merged_grad,
        docs_col,
        docs_row,
        states,
        first_later,
        keep,
        ahead,
        behind,
        turned_high,
        turned_low,
        gate=8,
    )
    kept, sent = run(
        once(
            qkv_weights_kernel,
            "qkv_weights",
            (shape((4, model_part + 16, qkv_cols), BF16),) * 2,
            scratch=[pltpu.VMEM((model, qkv_cols), BF16)],
        ),
        table,
        own_pg,
        far_pg,
        norm_one,
        gate=3,
    )
    tick(far_cross)
    far_quad = run(add_three, far_kept[0], far_got[0], far_cross)
    tick()
    far_home = swap(now(far_quad), 0, inner)
    norm_grads = run(
        simple(
            norm_grad_kernel,
            "norm_grad",
            (shape((8, model), F32),) + (shape((inner // 2, rows, model), BF16),) * 2,
            [
                plain(qkv_cols),
                plain(qkv_cols),
                plain(hidden_cols),
                plain(hidden_cols),
                whole(model, qkv_cols),
                whole(model, qkv_cols),
                whole(hidden_cols, model),
                whole(hidden_cols, model),
                plain(model),
                whole(4, model),
                whole(8, model),
            ],
            [whole(8, model)] + [whole(inner // 2, rows, model)] * 2,
            cost(4 * tokens * model * (qkv_cols + hidden_cols), 12e6),
        ),
        own_pg,
        far_pg,
        own_hidden_grad,
        far_hidden_grad,
        qkv_weight,
        far_qkv,
        own_up,
        far_up,
        unit,
        affine,
        grad_sums,
        gate=8,
    )
    e_sum = PairSum(norm_grads[1:])
    steps = [(1 << k, 0) for k in range(dp_size.bit_length() - 1)]
    steps += [(0, 1 << k) for k in range(tensor_size.bit_length() - 1)]
    small = norm_grads[0]

    def small_start():
        return swap(now(small), *steps.pop(0))

    def small_add(moved):
        return run(lambda a, b: a + b, small, moved)

    tick(out_moving)
    out_sum.add()
    tick()
    e_moving = e_sum.start()
    out_moving = out_sum.start()
    got, own_cross = swap(now(sent), 1, 0), swap(now(own_next), 2, 0)
    tick(got)
    cross_sent = run(add, kept[2:], got[2:])
    tick()
    crossed = swap(now(cross_sent), 2, 0)
    tick(out_moving)
    while out_sum.more():
        out_sum.add()
        tick(out_sum.start())
    layer_out = run(
        once(finish_out_kernel, "finish_out", shape((rows, model), BF16), prefetch=0),
        inputs,
        out_bias.reshape(1, -1),
        *out_sum.result(),
        gate=2,
    )
    tick(crossed)
    far_piece = run(add_three, kept[1], got[1], crossed[1])
    own_piece = run(add_three, kept[0], got[0], crossed[0])
    tick()
    far_piece_home = swap(now(far_piece), 0, inner)
    tick(far_home, own_cross)
    own_quad = run(add_three, own_kept[0], own_got[0], own_cross)
    lower_mine = rest(run(add, own_quad, far_home))
    tick()
    lower_third, lower_near = swap(now(lower_mine), 2, 0), swap(now(lower_mine), 1, 0)
    tick(e_moving)
    e_sum.add()
    tick()
    e_moving = e_sum.start()
    moved_small = small_start()
    tick(far_piece_home, lower_near, moved_small)
    upper_mine = rest(run(add, own_piece, far_piece_home))
    small = small_add(moved_small)
    tick()
    upper_third, upper_near = swap(now(upper_mine), 2, 0), swap(now(upper_mine), 1, 0)
    moved_small = small_start()
    tick(e_moving)
    while e_sum.more():
        e_sum.add()
        tick(e_sum.start())
    input_grad = run(
        once(finish_in_kernel, "finish_in", shape((rows, model), F32), prefetch=0),
        inputs,
        out_grad,
        *e_sum.result(),
        gate=2,
    )
    tick(lower_third, moved_small)
    lower = (lower_mine, lower_near, lower_third, swap(now(lower_third), 1, 0))
    small = small_add(moved_small)
    tick()
    moved_small = small_start()
    tick(lower[3])
    up_grad, down_grad, dense_grad, up_bias_grad = run(
        once(
            finish_hidden_kernel,
            "finish_hidden",
            (
                shape((model, hidden_cols), F32),
                shape((hidden_cols, model), F32),
                shape((width, model), F32),
                shape((QUARTERS, 1, hidden_part), F32),
            ),
            scratch=[pltpu.VMEM((hidden_cols, model), F32)],
        ),
        table,
        *lower,
        gate=1,
    )
    tick(upper_third, upper_near, moved_small)
    upper = (upper_mine, upper_near, upper_third, swap(now(upper_third), 1, 0))
    small = small_add(moved_small)
    tick()
    moved_small = small_start()
    tick(upper[3], moved_small)
    small = small_add(moved_small)
    tick()
    moved_small = small_start()
    qkv_grad, qkv_bias_grad = run(
        once(
            finish_qkv_kernel,
            "finish_qkv",
            (shape((model, qkv_cols), F32), shape((1, qkv_cols), F32)),
        ),
        table,
        *upper,
        gate=1,
    )

    small = small + moved_small
    while steps:
        tick()
        small = small_add(small_start())
    cols = model // tensor_size
    small = lax.dynamic_slice_in_dim(small, place * cols, cols, 1)

    return (
        layer_out,
        input_grad,
        qkv_grad,
        qkv_bias_grad.reshape(-1),
        dense_grad,
        up_grad,
        up_bias_grad.reshape(-1),
        down_grad,
        small[4],
        small[0],
        small[1],
        small[2],
        small[3],
    )


def solution(mesh):
    in_specs = (
        P(("dp", "tensor"), None),
        P(None, "tensor"),
        P("tensor"),
        P("tensor", None),
        P(None, "tensor"),
        P("tensor"),
        P("tensor", None),
        P(),
        P(),
        P(),
        P(),
        P(),
        P(),
        P("dp", None),
        P(("dp", "tensor"), None),
    )
    out_specs = (
        P(("dp", "tensor"), None),
        P(("dp", "tensor"), None),
        P(None, "tensor"),
        P("tensor"),
        P("tensor", None),
        P(None, "tensor"),
        P("tensor"),
        P("tensor", None),
        P("tensor"),
        P("tensor"),
        P("tensor"),
        P("tensor"),
        P("tensor"),
    )
    return jax.shard_map(
        functools.partial(on_device, mesh.shape["dp"], mesh.shape["tensor"]),
        mesh=mesh,
        in_specs=in_specs,
        out_specs=out_specs,
        check_vma=False,
    )
```
